256 devices in a mesh: lon: 16 (over z, core), lat: 16 (over x, y).
Axes of the slice: x: 4, y: 4, z: 8, core: 2. Of those that a mesh axis runs over, the one named last changes fastest.
Arguments:
- zonal_current: float32 [10, 1024, 2048], P(None, 'lat', 'lon'), may hold values from -6 to 6
- meridional_current: float32 [10, 1024, 2048], P(None, 'lat', 'lon'), may hold values from -6 to 6
- thermal_anomaly: float32 [10, 1024, 2048], P(None, 'lat', 'lon'), may hold values from -6 to 6
- saltiness_anomaly: float32 [10, 1024, 2048], P(None, 'lat', 'lon'), may hold values from -6 to 6
- water_indicator: int32 [10, 1024, 2048], P(None, 'lat', 'lon'), may hold values 0 or 1
- bottom_layer_index: int32 [1024, 2048], P('lat', 'lon'), may hold values from 1 to 10
- water_elevation: float32 [1024, 2048], P('lat', 'lon'), may hold values from -6 to 6
- zonal_barotropic_flow: float32 [1024, 2048], P('lat', 'lon'), may hold values from -6 to 6
- meridional_barotropic_flow: float32 [1024, 2048], P('lat', 'lon'), may hold values from -6 to 6
- planetary_spin_factor: float32 [1024, 2048], P('lat', 'lon'), may hold values from -1.5 to 1.5
Outputs:
- u_next: float32 [10, 1024, 2048], P(None, 'lat', 'lon')
- v_next: float32 [10, 1024, 2048], P(None, 'lat', 'lon')
- temperature_next: float32 [10, 1024, 2048], P(None, 'lat', 'lon')
- salinity_next: float32 [10, 1024, 2048], P(None, 'lat', 'lon')
- surface_next: float32 [1024, 2048], P('lat', 'lon')
- u_bar_next: float32 [1024, 2048], P('lat', 'lon')
- v_bar_next: float32 [1024, 2048], P('lat', 'lon')
The draws below stay inside these ranges and needn't reach their ends.
All inputs are finite; a program needn't handle non-finite values. No bound on the sum of `water_indicator` on one device may be relied on, other than what follows from the above.
Results may differ from the reference program's by a relative error of at most 0.00002.
Values sent between devices are 32-bit elements; how exact they have to be, the bound alone decides.
No kernel may reach another device: no remote copies, remote signals or barrier semaphores. Data moves between devices by JAX's collectives and lax.ppermute only.
A program may use at most 64 MiB of HBM per device.

```python
import jax
import jax.numpy as jnp

VERTICAL_TIERS = 10
SUBSTEPS = 4
MERIDIAN_POINTS = 1024
PARALLEL_POINTS = 2048


def place_ends(values, stream_key, least, largest):
    index_at = [jax.random.randint(jax.random.fold_in(stream_key, axis), (), 0, length) for axis, length in enumerate(values.shape)]
    main_axis = values.shape.index(max(values.shape))
    next_to = index_at[:main_axis] + [(index_at[main_axis] + 1) % values.shape[main_axis]] + index_at[main_axis + 1:]
    return values.at[tuple(index_at)].set(least).at[tuple(next_to)].set(largest)


def steps_of(rng, extent, pieces, smallest, high):
    factor_of = 1.0
    for position, parts in pieces:
        heights = jax.random.uniform(jax.random.fold_in(jax.random.fold_in(rng, 6), position), (parts,), jnp.float32, smallest / len(pieces), high / len(pieces))
        factor_of = factor_of * jnp.repeat(jnp.exp(heights), extent[position] // parts).reshape((-1,) + (1,) * (len(extent) - 1 - position))
    return factor_of


def gaussian(own_key, extent, scale, most, split=(), held_as=jnp.bfloat16):
    drawn = jax.random.normal(own_key, extent, jnp.float32) * scale
    if len(split) > 0:
        drawn = steps_of(own_key, extent, split, -0.22, 0.18) * drawn
    return jnp.clip(drawn, min=-most, max=most).astype(held_as)


def setup_inputs(seed: int = 0) -> dict:
    seeds = jax.random.split(jax.random.key(seed), 11)
    zonal_current = gaussian(seeds[0], (VERTICAL_TIERS, MERIDIAN_POINTS, PARALLEL_POINTS), 1.0, 6.0, ((1, 16), (2, 16)), jnp.float32)
    meridional_current = gaussian(seeds[1], (VERTICAL_TIERS, MERIDIAN_POINTS, PARALLEL_POINTS), 1.0, 6.0, ((1, 16), (2, 16)), jnp.float32)
    thermal_anomaly = gaussian(seeds[2], (VERTICAL_TIERS, MERIDIAN_POINTS, PARALLEL_POINTS), 1.0, 6.0, ((1, 16), (2, 16)), jnp.float32)
    saltiness_anomaly = gaussian(seeds[3], (VERTICAL_TIERS, MERIDIAN_POINTS, PARALLEL_POINTS), 1.0, 6.0, ((1, 16), (2, 16)), jnp.float32)
    water_indicator = place_ends((jax.random.randint(seeds[4], (VERTICAL_TIERS, MERIDIAN_POINTS, PARALLEL_POINTS), 0, 8) < 7).astype(jnp.int32), jax.random.fold_in(seeds[4], 1), 0, 1)
    bottom_layer_index = place_ends(jax.random.randint(seeds[5], (MERIDIAN_POINTS, PARALLEL_POINTS), 1, VERTICAL_TIERS + 1), jax.random.fold_in(seeds[5], 1), 1, VERTICAL_TIERS).astype(jnp.int32)
    water_elevation = gaussian(seeds[6], (MERIDIAN_POINTS, PARALLEL_POINTS), 1.0, 6.0, ((0, 16), (1, 16)), jnp.float32)
    zonal_barotropic_flow = gaussian(seeds[7], (MERIDIAN_POINTS, PARALLEL_POINTS), 1.0, 6.0, ((0, 16), (1, 16)), jnp.float32)
    meridional_barotropic_flow = gaussian(seeds[8], (MERIDIAN_POINTS, PARALLEL_POINTS), 1.0, 6.0, ((0, 16), (1, 16)), jnp.float32)
    planetary_spin_factor = jnp.clip(jax.random.uniform(seeds[9], (MERIDIAN_POINTS, PARALLEL_POINTS), jnp.float32, -1.5, 1.5) * steps_of(seeds[9], (MERIDIAN_POINTS, PARALLEL_POINTS), ((0, 16), (1, 16)), -0.4, 0.0), -1.5, 1.5)
    return dict(zonal_current=zonal_current, meridional_current=meridional_current, thermal_anomaly=thermal_anomaly, saltiness_anomaly=saltiness_anomaly, water_indicator=water_indicator, bottom_layer_index=bottom_layer_index, water_elevation=water_elevation, zonal_barotropic_flow=zonal_barotropic_flow, meridional_barotropic_flow=meridional_barotropic_flow, planetary_spin_factor=planetary_spin_factor)


advect_scale = 0.25
viscous_scale = 0.02
pressure_scale = 0.5
rotation_scale = 0.3
thermal_scale = 0.2
haline_scale = 0.8
surface_depth = 0.25
gravity_scale = 0.3
divergence_scale = 0.3


def east_west(field):
    return 0.5 * (field[..., 1:-1, 2:] - field[..., 1:-1, :-2])


def north_south(field):
    return 0.5 * (field[..., 2:, 1:-1] - field[..., :-2, 1:-1])


def laplace(field):
    return (field[..., 1:-1, 2:] + field[..., 1:-1, :-2] + field[..., 2:, 1:-1]
            + field[..., :-2, 1:-1] - 4.0 * field[..., 1:-1, 1:-1])


def march_marine_state(zonal_current, meridional_current, thermal_anomaly, saltiness_anomaly, water_indicator, bottom_layer_index,
               water_elevation, zonal_barotropic_flow, meridional_barotropic_flow, planetary_spin_factor, extend):
    levels = zonal_current.shape[0]
    level_index = jnp.arange(levels, dtype=jnp.int32)[:, None, None]
    water_point_total = water_indicator.astype(jnp.float32) * (level_index < bottom_layer_index[None]).astype(jnp.float32)
    state_arrays = jnp.stack([zonal_current, meridional_current, thermal_anomaly, saltiness_anomaly]) * water_point_total[None]
    extended = extend(state_arrays, 2, (-1.0, -1.0, 1.0, 1.0))
    inner_cycle = extended[:, :, 1:-1, 1:-1]
    smooth = laplace(laplace(extended))
    advect = east_west(inner_cycle[0][None] * inner_cycle[2:4]) + north_south(inner_cycle[1][None] * inner_cycle[2:4])
    thickness = ((jnp.arange(levels, dtype=jnp.float32) + 1.0) * (2.0 / (levels * (levels + 1))))[:, None, None]
    density = haline_scale * inner_cycle[3] - thermal_scale * inner_cycle[2]
    weight = density * thickness
    pressure = jnp.cumsum(weight, axis=0) - 0.5 * weight
    u_old = state_arrays[0]
    v_old = state_arrays[1]
    u_star = (u_old + rotation_scale * planetary_spin_factor * v_old - pressure_scale * east_west(pressure)
              - viscous_scale * smooth[0]) * water_point_total
    v_star = (v_old - rotation_scale * planetary_spin_factor * u_old - pressure_scale * north_south(pressure)
              - viscous_scale * smooth[1]) * water_point_total
    tracers = (state_arrays[2:4] - advect_scale * advect - viscous_scale * smooth[2:4]) * water_point_total[None]
    layer_weight = thickness * water_point_total
    column = surface_depth + jnp.sum(layer_weight, axis=0)

    def depth_mean(field):
        return jnp.sum(layer_weight * field, axis=0) / column

    mean_u = depth_mean(u_star)
    mean_v = depth_mean(v_star)
    force_u = (mean_u - depth_mean(u_old)) / SUBSTEPS
    force_v = (mean_v - depth_mean(v_old)) / SUBSTEPS
    wet_column = jnp.max(water_point_total, axis=0)
    surface = water_elevation
    u_bar = zonal_barotropic_flow
    v_bar = meridional_barotropic_flow
    for substep in range(SUBSTEPS):
        surface_ext = extend(surface[None, None], 1, (1.0,))[0, 0]
        u_new = (u_bar - gravity_scale * east_west(surface_ext) + rotation_scale * planetary_spin_factor * v_bar + force_u) * wet_column
        v_new = (v_bar - gravity_scale * north_south(surface_ext) - rotation_scale * planetary_spin_factor * u_bar + force_v) * wet_column
        u_bar = u_new
        v_bar = v_new
        transport = extend(jnp.stack([column * u_bar, column * v_bar])[:, None], 1, (-1.0, -1.0))[:, 0]
        surface = (surface - divergence_scale * (east_west(transport[0]) + north_south(transport[1]))) * wet_column
    u_next = (u_star - mean_u + u_bar) * water_point_total
    v_next = (v_star - mean_v + v_bar) * water_point_total
    return (u_next, v_next, tracers[0], tracers[1], surface, u_bar, v_bar)


def extend_global(fields_in, rim_width, parity):
    sign_table = jnp.array(parity, dtype=jnp.float32).reshape(-1, 1, 1, 1)
    lower_rows = jnp.zeros(fields_in.shape[:2] + (rim_width, fields_in.shape[3]), jnp.float32)
    upper_rows = jnp.flip(fields_in[:, :, fields_in.shape[2] - rim_width:, :], axis=(2, 3)) * sign_table
    extended = jnp.concatenate([lower_rows, fields_in, upper_rows], axis=2)
    return jnp.concatenate([extended[..., -rim_width:], extended, extended[..., :rim_width]], axis=3)


def reference(zonal_current, meridional_current, thermal_anomaly, saltiness_anomaly, water_indicator, bottom_layer_index,
              water_elevation, zonal_barotropic_flow, meridional_barotropic_flow, planetary_spin_factor):
    return march_marine_state(zonal_current, meridional_current, thermal_anomaly, saltiness_anomaly, water_indicator, bottom_layer_index,
                      water_elevation, zonal_barotropic_flow, meridional_barotropic_flow, planetary_spin_factor, extend_global)
```

```python
import functools

import jax
import jax.numpy as jnp
from jax import lax
from jax.experimental import pallas as pl
from jax.experimental.pallas import tpu as pltpu
from jax.sharding import PartitionSpec as P

SUBSTEPS = 4
LEVELS = 10
ROWS = 64
COLS = 128
RIM = 9
PLANES = 54
PER_SLAB = 14
SLABS = 4
TAIL = PLANES * 8
ROW_SLAB = TAIL + 24
SLAB_ROWS = 88
TOP = 16
HIGH = 96

advect_scale = 0.25
viscous_scale = 0.02
pressure_scale = 0.5
rotation_scale = 0.3
thermal_scale = 0.2
haline_scale = 0.8
surface_depth = 0.25
gravity_scale = 0.3
divergence_scale = 0.3

F32 = jnp.float32
SIGNS = [-1.0] * 20 + [1.0] * 30 + [1.0, -1.0, -1.0, 1.0]
THICK = [(k + 1.0) * (2.0 / (LEVELS * (LEVELS + 1))) for k in range(LEVELS)]


def whole(shape):
    return pl.BlockSpec(shape, lambda i: (0,) * len(shape))


def call(kernel, name, out, scratch, flops, *args, in_specs=None):
    return pl.pallas_call(
        kernel,
        grid=(1,),
        out_shape=[jax.ShapeDtypeStruct(s, F32) for s in out],
        in_specs=in_specs or [whole(a.shape) for a in args],
        out_specs=[whole(s) for s in out],
        scratch_shapes=scratch,
        name=name,
        cost_estimate=pl.CostEstimate(flops=flops, bytes_accessed=2_000_000, transcendentals=0),
        compiler_params=pltpu.CompilerParams(vmem_limit_bytes=48 * 1024 * 1024),
    )(*args)


def lane_iota(rows=8):
    return lax.broadcasted_iota(jnp.int32, (rows, COLS), 1)


def sub_iota():
    return lax.broadcasted_iota(jnp.int32, (8, COLS), 0)


def flip_lanes(x):
    return jnp.take_along_axis(x, COLS - 1 - lax.broadcasted_iota(jnp.int32, x.shape, 1), axis=1, mode="promise_in_bounds")


def flip_rows(x):
    return jnp.take_along_axis(x, 7 - lax.broadcasted_iota(jnp.int32, x.shape, 0), axis=0, mode="promise_in_bounds")


def lat_place():
    index = lax.axis_index("lat")
    return index % 2 == 0, index == lax.axis_size("lat") - 1


def pack_rows(u0, u1, v0, v1, t0, t1, s0, s1, w0, w1, bottom, eta, ub, vb, cor, a_ref, b_ref, low9, high9):
    even, top = lat_place()
    low9[...] = jnp.zeros((24, COLS), F32)
    high9[...] = jnp.zeros((24, COLS), F32)
    b0 = bottom[0:16, :]
    b1 = bottom[ROWS - 16 : ROWS, :]

    def put(p, down, up):
        fold = SIGNS[p] * flip_rows(flip_lanes(up))
        a_ref[8 * p : 8 * p + 8, :] = jnp.where(even, up, down)
        b_ref[8 * p : 8 * p + 8, :] = jnp.where(even, down, jnp.where(top, fold, up))

    for k in range(LEVELS):
        wl = jnp.where(k < b0, w0[k].astype(F32), 0.0)
        wh = jnp.where(k < b1, w1[k].astype(F32), 0.0)
        for f, (lo, hi) in enumerate(((u0, u1), (v0, v1), (t0, t1), (s0, s1))):
            p = 10 * f + k
            low = lo[k] * wl
            high = hi[k] * wh
            put(p, low[0:8], high[8:16])
            if f < 2:
                low9[p : p + 1, :] = low[8:9]
                high9[p : p + 1, :] = high[7:8]
        put(40 + k, wl[0:8], wh[8:16])
    for j, ref in enumerate((eta, ub, vb, cor)):
        put(50 + j, ref[0:8, :], ref[ROWS - 8 : ROWS, :])
    for r in range(0, 24, 8):
        down = low9[r : r + 8, :]
        up = high9[r : r + 8, :]
        fold = -flip_lanes(up)
        a_ref[TAIL + r : TAIL + r + 8, :] = jnp.where(even, up, down)
        b_ref[TAIL + r : TAIL + r + 8, :] = jnp.where(even, down, jnp.where(top, fold, up))


def put_columns(val, p, lane, east, west):
    q, j = divmod(p, PER_SLAB)
    here = (lane >= RIM * j) & (lane < RIM * j + RIM)
    east[q] = jnp.where(here, pltpu.roll(val, RIM * j, 1), east[q])
    west[q] = jnp.where(here, pltpu.roll(val, (RIM * j + RIM) % COLS, 1), west[q])


def pack_centre(u, v, t, s, w, bottom, eta, ub, vb, cor, x_ref, east_ref, west_ref):
    lane = lane_iota()

    def tile(i, carry):
        rows = pl.ds(pl.multiple_of(8 * i, 8), 8)
        deep = bottom[rows, :]
        zero = jnp.zeros((8, COLS), F32)
        east = [zero] * SLABS
        west = [zero] * SLABS
        for k in range(LEVELS):
            wet = jnp.where(k < deep, w[k, rows, :].astype(F32), 0.0)
            for f, ref in enumerate((u, v, t, s)):
                val = ref[k, rows, :] * wet
                x_ref[10 * f + k, rows, :] = val
                put_columns(val, 10 * f + k, lane, east, west)
            x_ref[40 + k, rows, :] = wet
            put_columns(wet, 40 + k, lane, east, west)
        for j, ref in enumerate((eta, ub, vb, cor)):
            val = ref[rows, :]
            x_ref[50 + j, rows, :] = val
            put_columns(val, 50 + j, lane, east, west)
        for q in range(SLABS):
            east_ref[q, rows, :] = east[q]
            west_ref[q, rows, :] = west[q]
        return carry

    lax.fori_loop(0, ROWS // 8, tile, 0)


def pack_rims(a_ref, b_ref, ec, wc, e_ref, w_ref):
    even, _ = lat_place()
    lane = lane_iota()
    sub = sub_iota()
    zero = jnp.zeros((8, COLS), F32)
    for q in range(SLABS):
        e_ref[q, 16 : 16 + ROWS, :] = ec[q]
        w_ref[q, 16 : 16 + ROWS, :] = wc[q]

    def both(r, n):
        a = a_ref[r : r + n, :]
        b = b_ref[r : r + n, :]
        return jnp.where(even, b, a), jnp.where(even, a, b)

    packs = [([zero] * SLABS, [zero] * SLABS) for _ in range(3)]
    for p in range(PLANES):
        south, north = both(8 * p, 8)
        put_columns(south, p, lane, *packs[1])
        put_columns(north, p, lane, *packs[2])
        if p < 20:
            south, north = both(TAIL + p, 1)
            put_columns(jnp.where(sub == 0, south, north), p, lane, *packs[0])
    for at, (east, west) in zip((0, 8, 16 + ROWS), packs):
        for q in range(SLABS):
            e_ref[q, at : at + 8, :] = east[q]
            w_ref[q, at : at + 8, :] = west[q]


class Wide:
    def __init__(self, own, rim):
        self.own, self.rim = own, rim

    def with_other(self, other, op):
        if isinstance(other, Wide):
            return Wide(op(self.own, other.own), op(self.rim, other.rim))
        return Wide(op(self.own, other), op(self.rim, other))

    def __add__(self, other):
        return self.with_other(other, lambda a, b: a + b)

    def __sub__(self, other):
        return self.with_other(other, lambda a, b: a - b)

    def __mul__(self, other):
        return self.with_other(other, lambda a, b: a * b)

    __rmul__ = __mul__

    def __truediv__(self, other):
        return self.with_other(other, lambda a, b: a / b)


def east_of(x):
    last = lane_iota() == COLS - 1
    own = pltpu.roll(x.own, COLS - 1, 1)
    rim = pltpu.roll(x.rim, COLS - 1, 1)
    return Wide(jnp.where(last, rim, own), jnp.where(last, own, rim))


def west_of(x):
    first = lane_iota() == 0
    own = pltpu.roll(x.own, 1, 1)
    rim = pltpu.roll(x.rim, 1, 1)
    return Wide(jnp.where(first, rim, own), jnp.where(first, own, rim))


def sides(x):
    return east_of(x) + west_of(x)


def slope(x):
    return east_of(x) - west_of(x)


def step(x_ref, a_ref, b_ref, es, ws, u_out, v_out, t_out, s_out, eta_out, ub_out, vb_out,
         own, rim, us, vs, fu, fv, mu, mv, col, tu, tv):
    even, _ = lat_place()
    lane = lane_iota()

    def place(p, carry):
        own[p, TOP : TOP + ROWS, :] = x_ref[p]
        row = pl.multiple_of(8 * p, 8)
        a = a_ref[pl.ds(row, 8), :]
        b = b_ref[pl.ds(row, 8), :]
        own[p, 8:16, :] = jnp.where(even, b, a)
        own[p, TOP + ROWS : TOP + ROWS + 8, :] = jnp.where(even, a, b)
        return carry

    lax.fori_loop(0, PLANES, place, 0)
    for p in range(20):
        a = a_ref[TAIL + p : TAIL + p + 1, :]
        b = b_ref[TAIL + p : TAIL + p + 1, :]
        own[p, 7:8, :] = jnp.where(even, b, a)
        own[p, TOP + ROWS + 8 : TOP + ROWS + 9, :] = jnp.where(even, a, b)

    def unpack(j, carry):
        shift = RIM * j
        for q in range(SLABS):
            for r in range(0, SLAB_ROWS, 8):
                east = pltpu.roll(es[q, r : r + 8, :], lax.rem(COLS - shift, COLS), 1)
                west = pltpu.roll(ws[q, r : r + 8, :], lax.rem(2 * COLS - RIM - shift, COLS), 1)
                val = jnp.where(lane < RIM, east, jnp.where(lane >= COLS - RIM, west, 0.0))
                if r == 0:
                    rim[PER_SLAB * q + j, 7:8, :] = val[0:1]
                    rim[PER_SLAB * q + j, TOP + ROWS + 8 : TOP + ROWS + 9, :] = val[1:2]
                else:
                    rim[PER_SLAB * q + j, r : r + 8, :] = val
        return carry

    lax.fori_loop(0, PER_SLAB, unpack, 0)

    def wide(ref, at):
        return Wide(ref[0, at, :], ref[1, at, :])

    def keep(ref, at, x):
        ref[0, at, :] = x.own
        ref[1, at, :] = x.rim

    def momentum(i, carry):
        r0 = 8 * i + 8

        def at(p, d):
            rows = pl.ds(r0 + d, 8)
            return Wide(own[p, rows, :], rim[p, rows, :])

        spin = rotation_scale * at(53, 0)
        none = jnp.zeros((8, COLS), F32)
        zero = Wide(none, none)
        acc = acc_ns = sum_u = sum_v = diff_u = diff_v = depth = zero
        for k in range(LEVELS):
            wet = at(40 + k, 0)
            u = at(k, 0)
            v = at(10 + k, 0)
            smooth = []
            for p, c in ((k, u), (10 + k, v)):
                ns = at(p, 1) + at(p, -1)
                smooth.append(sides(sides(c) + 2.0 * ns - 8.0 * c) + (at(p, 2) + at(p, -2) - 8.0 * ns + 18.0 * c))
            half = (0.5 * THICK[k]) * (haline_scale * at(30 + k, 0) - thermal_scale * at(20 + k, 0))
            half_ns = (0.5 * THICK[k]) * (
                haline_scale * (at(30 + k, 1) - at(30 + k, -1)) - thermal_scale * (at(20 + k, 1) - at(20 + k, -1))
            )
            pressure = acc + half
            pressure_ns = acc_ns + half_ns
            acc = pressure + half
            acc_ns = pressure_ns + half_ns
            u_star = wet * (u + spin * v - (0.5 * pressure_scale) * slope(pressure) - viscous_scale * smooth[0])
            v_star = wet * (v - spin * u - (0.5 * pressure_scale) * pressure_ns - viscous_scale * smooth[1])
            us[k, pl.ds(pl.multiple_of(8 * i, 8), 8), :] = u_star.own
            vs[k, pl.ds(pl.multiple_of(8 * i, 8), 8), :] = v_star.own
            sum_u = sum_u + THICK[k] * u_star
            sum_v = sum_v + THICK[k] * v_star
            diff_u = diff_u + THICK[k] * (u_star - u)
            diff_v = diff_v + THICK[k] * (v_star - v)
            depth = depth + THICK[k] * wet
        column = depth + surface_depth
        here = pl.ds(pl.multiple_of(r0, 8), 8)
        keep(fu, here, diff_u / column * (1.0 / SUBSTEPS))
        keep(fv, here, diff_v / column * (1.0 / SUBSTEPS))
        mu[here, :] = sum_u.own / column.own
        mv[here, :] = sum_v.own / column.own
        keep(col, here, column)
        own[53, here, :] = spin.own
        rim[53, here, :] = spin.rim
        return carry

    lax.fori_loop(0, 10, momentum, 0)

    def flat(p, r):
        return Wide(own[p, r : r + 8, :], rim[p, r : r + 8, :])

    def wet_of(column):
        return Wide(jnp.where(column.own > surface_depth, 1.0, 0.0), jnp.where(column.rim > surface_depth, 1.0, 0.0))

    def substep(n, carry):
        for r in range(8, 88, 8):
            here = slice(r, r + 8)
            column = wide(col, here)
            wet = wet_of(column)
            u = flat(51, r)
            v = flat(52, r)
            spin = flat(53, r)
            un = wet * (u - (0.5 * gravity_scale) * slope(flat(50, r)) + spin * v + wide(fu, here))
            vn = wet * (v - (0.5 * gravity_scale) * (flat(50, r + 1) - flat(50, r - 1)) - spin * u + wide(fv, here))
            for p, x in ((51, un), (52, vn)):
                own[p, here, :] = x.own
                rim[p, here, :] = x.rim
            keep(tu, here, column * un)
            keep(tv, here, column * vn)
        for r in range(8, 88, 8):
            here = slice(r, r + 8)
            wet = wet_of(wide(col, here))
            flow = slope(wide(tu, here)) + (wide(tv, slice(r + 1, r + 9)) - wide(tv, slice(r - 1, r + 7)))
            eta = wet * (flat(50, r) - (0.5 * divergence_scale) * flow)
            own[50, here, :] = eta.own
            rim[50, here, :] = eta.rim
        return carry

    lax.fori_loop(0, SUBSTEPS, substep, 0)
    eta_out[...] = own[50, TOP : TOP + ROWS, :]
    ub_out[...] = own[51, TOP : TOP + ROWS, :]
    vb_out[...] = own[52, TOP : TOP + ROWS, :]

    def finish(i, carry):
        r0 = 8 * i + TOP
        here = pl.ds(pl.multiple_of(r0, 8), 8)
        rows = pl.ds(pl.multiple_of(8 * i, 8), 8)
        star = pl.ds(pl.multiple_of(8 * i + 8, 8), 8)

        def at(p, d):
            return Wide(own[p, pl.ds(r0 + d, 8), :], rim[p, pl.ds(r0 + d, 8), :])

        gain_u = own[51, here, :] - mu[here, :]
        gain_v = own[52, here, :] - mv[here, :]
        for k in range(LEVELS):
            wet = own[40 + k, here, :]
            u_out[k, rows, :] = us[k, star, :] + wet * gain_u
            v_out[k, rows, :] = vs[k, star, :] + wet * gain_v
            u = at(k, 0)
            vn = own[10 + k, pl.ds(r0 + 1, 8), :]
            vsouth = own[10 + k, pl.ds(r0 - 1, 8), :]
            for p, out in ((20 + k, t_out), (30 + k, s_out)):
                c = at(p, 0)
                n = at(p, 1)
                s = at(p, -1)
                far = own[p, pl.ds(r0 + 2, 8), :] + own[p, pl.ds(r0 - 2, 8), :]
                ns = n + s
                inner = sides(c) + 2.0 * ns - 8.0 * c
                smooth = sides(inner).own + (far - 8.0 * ns.own + 18.0 * c.own)
                advect = slope(u * c).own + (vn * n.own - vsouth * s.own)
                out[k, rows, :] = wet * (c.own - (0.5 * advect_scale) * advect - viscous_scale * smooth)
        return carry

    lax.fori_loop(0, ROWS // 8, finish, 0)


def colour(parity, lats, lons):
    pairs = []
    for lat in range(lats):
        for lon in range(lons):
            if (lat + parity) % 2 == 0:
                to = (lon, lat + 1) if lat + 1 < lats else (lons - 1 - lon, lat)
            elif lat > 0:
                to = (lon, lat - 1)
            else:
                continue
            pairs.append((lon * lats + lat, to[0] * lats + to[1]))
    return pairs


def local(u, v, t, s, w, bottom, eta, ub, vb, cor):
    lats = lax.axis_size("lat")
    lons = lax.axis_size("lon")
    ends = []
    for _ in range(5):
        ends.append(pl.BlockSpec((LEVELS, 16, COLS), lambda i: (0, 0, 0)))
        ends.append(pl.BlockSpec((LEVELS, 16, COLS), lambda i: (0, ROWS // 16 - 1, 0)))
    flat = whole((ROWS, COLS))
    a, b = call(
        pack_rows, "pack_rows", [(ROW_SLAB, COLS)] * 2, [pltpu.VMEM((24, COLS), F32)] * 2, 1_000_000,
        u, u, v, v, t, t, s, s, w, w, bottom, eta, ub, vb, cor, in_specs=ends + [flat] * 5,
    )
    a = lax.ppermute(a, ("lon", "lat"), colour(0, lats, lons))
    b = lax.ppermute(b, ("lon", "lat"), colour(1, lats, lons))
    x, ec, wc = call(
        pack_centre, "pack_centre", [(PLANES, ROWS, COLS)] + [(SLABS, ROWS, COLS)] * 2, [], 10_000_000,
        u, v, t, s, w, bottom, eta, ub, vb, cor,
    )
    e, west = call(pack_rims, "pack_rims", [(SLABS, SLAB_ROWS, COLS)] * 2, [], 1_000_000, a, b, ec, wc)
    e = lax.ppermute(e, "lon", [((i + 1) % lons, i) for i in range(lons)])
    west = lax.ppermute(west, "lon", [(i, (i + 1) % lons) for i in range(lons)])
    cube = (LEVELS, ROWS, COLS)
    plane = (ROWS, COLS)
    wide = pltpu.VMEM((2, HIGH, COLS), F32)
    thin = pltpu.VMEM((HIGH, COLS), F32)
    star = pltpu.VMEM((LEVELS, 80, COLS), F32)
    planes = pltpu.VMEM((SLABS * PER_SLAB, HIGH, COLS), F32)
    return tuple(
        call(
            step, "step", [cube] * 4 + [plane] * 3,
            [planes, planes, star, star, wide, wide, thin, thin, wide, wide, wide],
            50_000_000, x, a, b, e, west,
        )
    )


def solution(mesh):
    deep = P(None, "lat", "lon")
    flat = P("lat", "lon")
    return jax.shard_map(
        local,
        mesh=mesh,
        in_specs=(deep,) * 5 + (flat,) * 5,
        out_specs=(deep,) * 4 + (flat,) * 3,
        check_vma=False,
    )
```

```python
import functools

import jax
import jax.numpy as jnp
from jax import lax
from jax.experimental import pallas as pl
from jax.experimental.pallas import tpu as pltpu
from jax.sharding import PartitionSpec as P

SUBSTEPS = 4
LEVELS = 10
ROWS = 64
COLS = 128
U, V, D, WET, T, S, FLAT = 0, 10, 20, 30, 40, 50, 60
PLANES = 64
BLOCKS = 44
NINTH = 8 * BLOCKS
PAIRS = NINTH + 24
ROW_SLAB = PAIRS + 4 * LEVELS
STRIDE = 11
SLABS = 4
SLAB_ROWS = 88
TOP = 16
HIGH = 96
BAND = 40

advect_scale = 0.25
viscous_scale = 0.02
pressure_scale = 0.5
rotation_scale = 0.3
thermal_scale = 0.2
haline_scale = 0.8
surface_depth = 0.25
gravity_scale = 0.3
divergence_scale = 0.3

F32 = jnp.float32
SIGNS = [-1.0] * 20 + [1.0] * 20 + [1.0, -1.0, -1.0, 1.0]
THICK = [(k + 1.0) * (2.0 / (LEVELS * (LEVELS + 1))) for k in range(LEVELS)]
HBM = pl.BlockSpec(memory_space=pltpu.HBM)
VMEM = pl.BlockSpec(memory_space=pltpu.VMEM)
CUBE = (LEVELS, ROWS, COLS)
PLANE = (ROWS, COLS)


def call(kernel, name, out, scratch, flops, *args, ins=None, outs=None):
    return pl.pallas_call(
        kernel,
        out_shape=[jax.ShapeDtypeStruct(s, F32) for s in out],
        in_specs=ins or [VMEM] * len(args),
        out_specs=outs or [VMEM] * len(out),
        scratch_shapes=scratch,
        name=name,
        cost_estimate=pl.CostEstimate(flops=flops, bytes_accessed=2_000_000, transcendentals=0),
        compiler_params=pltpu.CompilerParams(vmem_limit_bytes=LIMIT),
    )(*args)


LIMIT = 40 * 1024 * 1024


def lanes(rows=8):
    return lax.broadcasted_iota(jnp.int32, (rows, COLS), 1)


def flip_lanes(x):
    return jnp.take_along_axis(x, COLS - 1 - lax.broadcasted_iota(jnp.int32, x.shape, 1), axis=1, mode="promise_in_bounds")


def flip_rows(x):
    return jnp.take_along_axis(x, 7 - lax.broadcasted_iota(jnp.int32, x.shape, 0), axis=0, mode="promise_in_bounds")


def turn(x, shift):
    return pltpu.roll(x, shift % COLS, 1)


def lat_place():
    index = lax.axis_index("lat")
    return index % 2 == 0, index == lax.axis_size("lat") - 1


def fetch(pairs, sem):
    copies = [pltpu.make_async_copy(src, dst, sem.at[n]) for n, (src, dst) in enumerate(pairs)]
    for copy in copies:
        copy.start()
    return copies


def pack_rows(u, v, t, s, w, bottom, eta, ub, vb, cor, a_ref, b_ref,
              u2, v2, t2, s2, w2, flat, deep, low9, high9, low2, high2, fold2, sem):
    even, top = lat_place()
    moves = []
    for src, dst in ((u, u2), (v, v2), (t, t2), (s, s2), (w, w2)):
        moves.append((src.at[:, 0:16, :], dst.at[0]))
        moves.append((src.at[:, ROWS - 16 : ROWS, :], dst.at[1]))
    for n, src in enumerate((eta, ub, vb, cor)):
        moves.append((src, flat.at[n]))
    moves.append((bottom, deep))
    for copy in fetch(moves, sem):
        copy.wait()
    low9[...] = jnp.zeros((24, COLS), F32)
    high9[...] = jnp.zeros((24, COLS), F32)
    d0 = deep[0:16, :]
    d1 = deep[ROWS - 16 : ROWS, :]

    def send(r, down, up, fold):
        a_ref[r : r + 8, :] = jnp.where(even, up, down)
        b_ref[r : r + 8, :] = jnp.where(even, down, jnp.where(top, fold, up))

    def put(p, down, up):
        send(8 * p, down, up, SIGNS[p] * flip_rows(flip_lanes(up)))

    for k in range(LEVELS):
        wl = jnp.where(k < d0, w2[0, k].astype(F32), 0.0)
        wh = jnp.where(k < d1, w2[1, k].astype(F32), 0.0)
        for f, ref in ((U, u2), (V, v2)):
            low = ref[0, k] * wl
            high = ref[1, k] * wh
            put(f + k, low[0:8], high[8:16])
            low9[f + k : f + k + 1, :] = low[8:9]
            high9[f + k : f + k + 1, :] = high[7:8]
        tl = t2[0, k] * wl
        th = t2[1, k] * wh
        sl = s2[0, k] * wl
        sh = s2[1, k] * wh
        put(D + k, (haline_scale * sl - thermal_scale * tl)[0:8], (haline_scale * sh - thermal_scale * th)[8:16])
        put(WET + k, wl[0:8], wh[8:16])
        for n, (low, high) in enumerate(((tl, th), (sl, sh))):
            r = 4 * k + 2 * n
            low2[r : r + 2, :] = low[0:2]
            high2[r : r + 2, :] = high[14:16]
            fold2[r : r + 1, :] = high[15:16]
            fold2[r + 1 : r + 2, :] = high[14:15]
    for n in range(4):
        put(40 + n, flat[n, 0:8, :], flat[n, ROWS - 8 : ROWS, :])
    for r in range(0, 24, 8):
        up = high9[r : r + 8, :]
        send(NINTH + r, low9[r : r + 8, :], up, -flip_lanes(up))
    for r in range(0, 40, 8):
        send(PAIRS + r, low2[r : r + 8, :], high2[r : r + 8, :], flip_lanes(fold2[r : r + 8, :]))


class Columns:
    def __init__(self, lane):
        self.lane = lane
        zero = jnp.zeros((8, COLS), F32)
        self.east = [zero] * SLABS
        self.west = [zero] * SLABS

    def put_east(self, q, moved, at, count):
        lane = self.lane
        self.east[q] = jnp.where((lane >= at) & (lane < at + count), moved, self.east[q])

    def put_west(self, q, moved, end, count):
        lane = self.lane
        low = (end - count) % COLS
        here = (lane >= low) & (lane < end) if low < end else (lane >= low) | (lane < end)
        self.west[q] = jnp.where(here, moved, self.west[q])

    def put(self, q, val, shift, count):
        moved = turn(val, shift)
        self.put_east(q, moved, shift, count)
        self.put_west(q, moved, shift, count)

    def level(self, q, k, val):
        self.put(q, val, STRIDE * k + 2, 9)

    def tracers(self, k, t, s):
        for q, val in enumerate((t, s)):
            self.put_east(q, turn(val, STRIDE * k), STRIDE * k, 2)
            self.put_west(q, turn(val, STRIDE * k + 4), STRIDE * k + 4, 2)

    def flat(self, n, val):
        if n % 2 == 0:
            self.put(n // 2, val, 112, 9)
        else:
            self.put(n // 2, val, 121, 7)


def shifted(x, d):
    lane = lanes()
    keep = lane < COLS - d if d > 0 else lane >= -d
    return jnp.where(keep, turn(x, -d), 0.0)


def smoothed(at, p, c, shift):
    north, south = at(p, 1), at(p, -1)
    q = (north + south) - 4.0 * c
    both = shift(c, 2) + shift(c, -2) + (at(p, 2) + at(p, -2))
    return both + 2.0 * ((shift(q, 1) + shift(q, -1)) - 4.0 * q) - 12.0 * c, north, south


def own_tile(at, spin, put_u, put_v, put_t, put_s):
    zero = jnp.zeros((8, COLS), F32)
    acc = acc_ns = sum_u = sum_v = old_u = old_v = depth = zero
    for k in range(LEVELS):
        wet = at(WET + k, 0)
        u = at(U + k, 0)
        v = at(V + k, 0)
        smooth_u, _, _ = smoothed(at, U + k, u, shifted)
        smooth_v, v_north, v_south = smoothed(at, V + k, v, shifted)
        half = (0.5 * THICK[k]) * at(D + k, 0)
        half_ns = (0.5 * THICK[k]) * (at(D + k, 1) - at(D + k, -1))
        pressure = acc + half
        pressure_ns = acc_ns + half_ns
        acc = pressure + half
        acc_ns = pressure_ns + half_ns
        slope = shifted(pressure, 1) - shifted(pressure, -1)
        u_star = wet * (u + spin * v - (0.5 * pressure_scale) * slope - viscous_scale * smooth_u)
        v_star = wet * (v - spin * u - (0.5 * pressure_scale) * pressure_ns - viscous_scale * smooth_v)
        sum_u = sum_u + THICK[k] * u_star
        sum_v = sum_v + THICK[k] * v_star
        old_u = old_u + THICK[k] * u
        old_v = old_v + THICK[k] * v
        depth = depth + THICK[k] * wet
        if put_u is None:
            continue
        put_u(k, u_star)
        put_v(k, v_star)
        for p, put in ((T + k, put_t), (S + k, put_s)):
            c = at(p, 0)
            smooth, north, south = smoothed(at, p, c, shifted)
            flux = u * c
            advect = (shifted(flux, 1) - shifted(flux, -1)) + (v_north * north - v_south * south)
            put(k, wet * (c - (0.5 * advect_scale) * advect - viscous_scale * smooth))
    return sum_u, sum_v, sum_u - old_u, sum_v - old_v, depth


def centre(u, v, t, s, w, bottom, eta, ub, vb, cor, x_ref, ec, wc, us, vs, tn, sn, sums,
           u2, v2, t2, s2, w2, deep, sem):
    moves = list(zip((u, v, t, s, w, bottom), (u2, v2, t2, s2, w2, deep)))
    for n, src in enumerate((eta, ub, vb, cor)):
        moves.append((src, x_ref.at[FLAT + n]))
    for copy in fetch(moves, sem):
        copy.wait()
    lane = lanes()

    def pack(i, carry):
        rows = pl.ds(pl.multiple_of(8 * i, 8), 8)
        bed = deep[rows, :]
        columns = Columns(lane)
        for k in range(LEVELS):
            wet = jnp.where(k < bed, w2[k, rows, :].astype(F32), 0.0)
            uk = u2[k, rows, :] * wet
            vk = v2[k, rows, :] * wet
            tk = t2[k, rows, :] * wet
            sk = s2[k, rows, :] * wet
            dk = haline_scale * sk - thermal_scale * tk
            for p, val in ((U, uk), (V, vk), (D, dk), (WET, wet), (T, tk), (S, sk)):
                x_ref[p + k, rows, :] = val
            for q, val in enumerate((uk, vk, dk, wet)):
                columns.level(q, k, val)
            columns.tracers(k, tk, sk)
        for n in range(4):
            columns.flat(n, x_ref[FLAT + n, rows, :])
        for q in range(SLABS):
            ec[q, rows, :] = columns.east[q]
            wc[q, rows, :] = columns.west[q]
        return carry

    lax.fori_loop(0, ROWS // 8, pack, 0)

    def inner(i, carry):
        r0 = 8 * i
        rows = pl.ds(pl.multiple_of(r0, 8), 8)

        def store(ref):
            def put(k, val):
                ref[k, rows, :] = val
            return put

        got = own_tile(
            lambda p, d: x_ref[p, pl.ds(r0 + d, 8), :], rotation_scale * x_ref[FLAT + 3, rows, :],
            store(us), store(vs), store(tn), store(sn),
        )
        for n in range(5):
            sums[n, rows, :] = got[n]
        return carry

    lax.fori_loop(1, ROWS // 8 - 1, inner, 0)


def pack_rims(a_ref, b_ref, ec, wc, e_ref, w_ref):
    even, _ = lat_place()
    lane = lanes()
    sub = lax.broadcasted_iota(jnp.int32, (8, COLS), 0)
    for q in range(SLABS):
        e_ref[q, TOP : TOP + ROWS, :] = ec[q]
        w_ref[q, TOP : TOP + ROWS, :] = wc[q]

    def both(r, n):
        a = a_ref[r : r + n, :]
        b = b_ref[r : r + n, :]
        return jnp.where(even, b, a), jnp.where(even, a, b)

    ninth, south, north = Columns(lane), Columns(lane), Columns(lane)
    for k in range(LEVELS):
        for q in range(4):
            lo, hi = both(8 * (10 * q + k), 8)
            south.level(q, k, lo)
            north.level(q, k, hi)
            if q < 2:
                lo, hi = both(NINTH + 10 * q + k, 1)
                ninth.level(q, k, jnp.where(sub == 0, lo, hi))
        pairs = [both(PAIRS + 4 * k + n, 1) for n in range(4)]
        t_lo, s_lo = (jnp.where(sub == 6, pairs[n][0], pairs[n + 1][0]) for n in (0, 2))
        t_hi, s_hi = (jnp.where(sub == 0, pairs[n][1], pairs[n + 1][1]) for n in (0, 2))
        south.tracers(k, t_lo, s_lo)
        north.tracers(k, t_hi, s_hi)
    for n in range(4):
        lo, hi = both(8 * (40 + n), 8)
        south.flat(n, lo)
        north.flat(n, hi)
    for at, columns in ((0, ninth), (8, south), (TOP + ROWS, north)):
        for q in range(SLABS):
            e_ref[q, at : at + 8, :] = columns.east[q]
            w_ref[q, at : at + 8, :] = columns.west[q]


def edges(x_ref, a_ref, b_ref, us, vs, tn, sn, sums, low, high):
    even, _ = lat_place()

    def both(r, n):
        a = a_ref[pl.ds(r, n), :]
        b = b_ref[pl.ds(r, n), :]
        return jnp.where(even, b, a), jnp.where(even, a, b)

    def place(p, carry):
        low[p, 16:32, :] = x_ref[p, 0:16, :]
        high[p, 0:16, :] = x_ref[p, ROWS - 16 : ROWS, :]
        return carry

    lax.fori_loop(0, FLAT, place, 0)

    def rims(p, carry):
        lo, hi = both(pl.multiple_of(8 * p, 8), 8)
        low[p, 8:16, :] = lo
        high[p, 16:24, :] = hi
        return carry

    lax.fori_loop(0, 40, rims, 0)
    for p in range(20):
        lo, hi = both(NINTH + p, 1)
        low[p, 7:8, :] = lo
        high[p, 24:25, :] = hi
    for k in range(LEVELS):
        for n, p in enumerate((T + k, S + k)):
            lo, hi = both(PAIRS + 4 * k + 2 * n, 2)
            low[p, 14:16, :] = lo
            high[p, 16:18, :] = hi
    spin_low, spin_high = both(8 * 43, 8)
    for n, (ref, r0, spin) in enumerate((
        (low, 16, x_ref[FLAT + 3, 0:8, :]),
        (high, 8, x_ref[FLAT + 3, ROWS - 8 : ROWS, :]),
        (low, 8, spin_low),
        (high, 16, spin_high),
    )):
        def store(out):
            def put(k, val):
                out[k, 8 * n : 8 * n + 8, :] = val
            return put

        puts = [store(out) for out in (us, vs, tn, sn)] if n < 2 else [None] * 4
        got = own_tile(lambda p, d: ref[p, r0 + d : r0 + d + 8, :], rotation_scale * spin, *puts)
        for m in range(5):
            sums[m, 8 * n : 8 * n + 8, :] = got[m]


class Wide:
    def __init__(self, own, rim):
        self.own, self.rim = own, rim

    def with_other(self, other, op):
        if isinstance(other, Wide):
            return Wide(op(self.own, other.own), op(self.rim, other.rim))
        return Wide(op(self.own, other), op(self.rim, other))

    def __add__(self, other):
        return self.with_other(other, lambda a, b: a + b)

    def __sub__(self, other):
        return self.with_other(other, lambda a, b: a - b)

    def __mul__(self, other):
        return self.with_other(other, lambda a, b: a * b)

    __rmul__ = __mul__

    def __truediv__(self, other):
        return self.with_other(other, lambda a, b: a / b)


def slope(x):
    lane = lanes()
    east_own, east_rim = turn(x.own, -1), turn(x.rim, -1)
    west_own, west_rim = turn(x.own, 1), turn(x.rim, 1)
    last, first = lane == COLS - 1, lane == 0
    return Wide(
        jnp.where(last, east_rim, east_own) - jnp.where(first, west_rim, west_own),
        jnp.where(last, east_own, east_rim) - jnp.where(first, west_own, west_rim),
    )


def group_sum(x):
    one = x + turn(x, -STRIDE)
    two = one + turn(one, -2 * STRIDE)
    return two + turn(two, -4 * STRIDE) + turn(one, -8 * STRIDE)


def step(x_ref, a_ref, b_ref, e_mine, w_mine, e_got, w_got, us, vs, tn, sn, sums, us2, vs2, tn2, sn2, sums2,
         u_out, v_out, t_out, s_out, eta_out, ub_out, vb_out,
         es, ws, own, rim, fix, total, col, fu, fv, mu, mv, tu, tv, spins, t_new, s_new, u_new, v_new, flats, sem):
    even, _ = lat_place()
    lane = lanes()
    rest = lane % STRIDE
    inside = lane < LEVELS * STRIDE
    for r in range(0, SLAB_ROWS, 8):
        for q in range(SLABS):
            here = slice(r, r + 8)
            east = jnp.where((rest < 2) & inside, w_mine[q, here, :], e_got[q, here, :])
            west = jnp.where(((rest == 2) | (rest == 3)) & inside, e_mine[q, here, :], w_got[q, here, :])
            for ref, val in ((es, east), (ws, west)):
                if r == 0:
                    ref[q, 7:8, :] = val[0:1]
                    ref[q, TOP + ROWS + 8 : TOP + ROWS + 9, :] = val[1:2]
                else:
                    ref[q, here, :] = val
            if q < 2 and r > 0:
                es[SLABS + q, here, :] = turn(e_got[q, here, :], 2)
                ws[SLABS + q, here, :] = turn(w_got[q, here, :], -2)
    for n in range(4):
        a = a_ref[8 * (40 + n) : 8 * (41 + n), :]
        b = b_ref[8 * (40 + n) : 8 * (41 + n), :]
        own[n, 8:16, :] = jnp.where(even, b, a)
        own[n, TOP : TOP + ROWS, :] = x_ref[FLAT + n]
        own[n, TOP + ROWS : TOP + ROWS + 8, :] = jnp.where(even, a, b)
        q, second = divmod(n, 2)
        for r in range(8, 88, 8):
            at = (121, 7) if second else (112, 16)
            rim[n, r : r + 8, :] = turn(jnp.where(lane >= at[0], es[q, r : r + 8, :], ws[q, r : r + 8, :]), at[1])
    for m in range(5):
        total[m, 8:16, :] = sums2[m, 16:24, :]
        total[m, 16:24, :] = sums2[m, 0:8, :]
        total[m, 24:72, :] = sums[m, 8:56, :]
        total[m, 72:80, :] = sums2[m, 8:16, :]
        total[m, 80:88, :] = sums2[m, 24:32, :]

    short = lane
    lane = lanes(BAND)
    rest = lane % STRIDE
    inside = lane < LEVELS * STRIDE
    level_e = jnp.minimum(lane // STRIDE, LEVELS)
    level_w = jnp.minimum(((lane + 7) % COLS) // STRIDE, LEVELS)
    thick_e = jnp.where(level_e < LEVELS, (level_e + 1).astype(F32) * THICK[0], 0.0)
    thick_w = jnp.where(level_w < LEVELS, (level_w + 1).astype(F32) * THICK[0], 0.0)
    edge = (lane < 2) | (lane >= COLS - 2)
    border = (short < 2) | (short >= COLS - 2)

    def slab_tile(i, carry):
        r0 = BAND * i + 8
        here = pl.ds(pl.multiple_of(r0, 8), BAND)
        parts = []
        for ref, level, thick, ahead in ((es, level_e, thick_e, 1), (ws, level_w, thick_w, -1)):
            def at(q, d):
                return ref[q, pl.ds(r0 + d, BAND), :]

            def stacked(x):
                for n in (1, 2, 4, 8):
                    x = x + jnp.where(level >= n, turn(x, n * STRIDE), 0.0)
                return x

            def around(x, d):
                return turn(x, -d)

            if ahead > 0:
                near, pair = (rest == 2) & inside, ((rest == 2) | (rest == 3)) & inside
            else:
                near, pair = (rest == 1) & inside, (rest < 2) & inside
            wet = at(3, 0)
            u = at(0, 0)
            v = at(1, 0)
            weight = thick * at(2, 0)
            weight_ns = thick * (at(2, 1) - at(2, -1))
            pressure = stacked(weight) - 0.5 * weight
            pressure_ns = stacked(weight_ns) - 0.5 * weight_ns
            smooth_u, un, us_ = smoothed(at, 0, u, around)
            smooth_v, vn, vs_ = smoothed(at, 1, v, around)
            change = pressure_scale * 0.5 * (turn(pressure, -1) - turn(pressure, 1)) + viscous_scale * smooth_u
            change_ns = pressure_scale * 0.5 * pressure_ns + viscous_scale * smooth_v
            parts.append((wet * thick, -change, -change_ns, u, v, wet))

            def beyond(c, ns, extra):
                far = viscous_scale * jnp.where(pair, c, 0.0)
                close = jnp.where(near, (2.0 * viscous_scale) * (ns - 4.0 * c) + extra, 0.0)
                return -(turn(far, -2 * ahead) + turn(close, -ahead))

            push = (0.5 * pressure_scale * ahead) * pressure
            fixes = [beyond(u, un + us_, push), beyond(v, vn + vs_, 0.0)]
            carry_u = (0.5 * advect_scale * ahead) * u
            for q in (SLABS, SLABS + 1):
                c = at(q, 0)
                fixes.append(beyond(c, at(q, 1) + at(q, -1), carry_u * c))
            parts.append(fixes)
        (we, due, dve, ue, ve, wet_e), fix_e, (ww, duw, dvw, uw, vw, wet_w), fix_w = parts
        own_wet = jnp.where(rest < 2, wet_e, wet_w)
        own_thick = jnp.where(rest < 2, thick_e, thick_w)
        fixes = [own_wet * (x + y) for x, y in zip(fix_e, fix_w)]
        for n in range(4):
            fix[n, here, :] = fixes[n]

        def to_rim(e, w):
            return turn(jnp.where((lane >= 2) & (lane <= 10), group_sum(e), group_sum(w)), -2)

        def to_own(x):
            return jnp.where(edge, turn(group_sum(own_thick * x), -2), 0.0)

        spin = Wide(rotation_scale * own[3, here, :], rotation_scale * rim[3, here, :])
        column = Wide(surface_depth + total[4, here, :], surface_depth + to_rim(we, ww))
        rim_u = to_rim(we * due, ww * duw) + spin.rim * to_rim(we * ve, ww * vw)
        rim_v = to_rim(we * dve, ww * dvw) - spin.rim * to_rim(we * ue, ww * uw)
        fix_u = to_own(fixes[0])
        fix_v = to_own(fixes[1])
        part = Wide(1.0 / column.own, 1.0 / column.rim)
        for ref, mean, own_sum, own_diff, rim_diff, x in (
            (fu, mu, total[0, here, :], total[2, here, :], rim_u, fix_u),
            (fv, mv, total[1, here, :], total[3, here, :], rim_v, fix_v),
        ):
            ref[0, here, :] = (own_diff + x) * part.own * (1.0 / SUBSTEPS)
            ref[1, here, :] = rim_diff * part.rim * (1.0 / SUBSTEPS)
            mean[here, :] = (own_sum + x) * part.own
        for ref, x in ((col, column), (spins, spin)):
            ref[0, here, :] = x.own
            ref[1, here, :] = x.rim
        return carry

    lax.fori_loop(0, 80 // BAND, slab_tile, 0)

    def mend(n, k, rows_fix):
        return jnp.where(border, turn(fix[n, rows_fix, :], -(STRIDE * k + 2)), 0.0)

    def tile_of(i):
        return pl.ds(pl.multiple_of(8 * i, 8), 8), pl.ds(pl.multiple_of(8 * i + TOP, 8), 8)

    def tracer_tile(rows, fixed, refs, src):
        for n, (ref, out) in enumerate(zip(refs, (t_new, s_new))):
            for k in range(LEVELS):
                out[k, rows, :] = ref[k, src, :] + mend(2 + n, k, fixed)

    def tracer_loop(i, carry):
        rows, fixed = tile_of(i)
        tracer_tile(rows, fixed, (tn, sn), rows)
        return carry

    lax.fori_loop(1, ROWS // 8 - 1, tracer_loop, 0)
    for n, i in enumerate((0, ROWS // 8 - 1)):
        tracer_tile(slice(8 * i, 8 * i + 8), slice(8 * i + TOP, 8 * i + TOP + 8), (tn2, sn2), slice(8 * n, 8 * n + 8))
    first = [pltpu.make_async_copy(src, dst, sem.at[n]) for n, (src, dst) in enumerate(((t_new, t_out), (s_new, s_out)))]
    for copy in first:
        copy.start()

    def wide(ref, at):
        return Wide(ref[0, at, :], ref[1, at, :])

    def keep(ref, at, x):
        ref[0, at, :] = x.own
        ref[1, at, :] = x.rim

    def flat(p, r):
        return Wide(own[p, r : r + 8, :], rim[p, r : r + 8, :])

    def wet_of(column):
        return Wide(jnp.where(column.own > surface_depth, 1.0, 0.0), jnp.where(column.rim > surface_depth, 1.0, 0.0))

    def substep(n, carry):
        for r in range(8, 88, 8):
            here = slice(r, r + 8)
            column = wide(col, here)
            wet = wet_of(column)
            u = flat(1, r)
            v = flat(2, r)
            spin = wide(spins, here)
            un = wet * (u - (0.5 * gravity_scale) * slope(flat(0, r)) + spin * v + wide(fu, here))
            vn = wet * (v - (0.5 * gravity_scale) * (flat(0, r + 1) - flat(0, r - 1)) - spin * u + wide(fv, here))
            for p, x in ((1, un), (2, vn)):
                own[p, here, :] = x.own
                rim[p, here, :] = x.rim
            keep(tu, here, column * un)
            keep(tv, here, column * vn)
        for r in range(8, 88, 8):
            here = slice(r, r + 8)
            wet = wet_of(wide(col, here))
            flow = slope(wide(tu, here)) + (wide(tv, slice(r + 1, r + 9)) - wide(tv, slice(r - 1, r + 7)))
            eta = wet * (flat(0, r) - (0.5 * divergence_scale) * flow)
            own[0, here, :] = eta.own
            rim[0, here, :] = eta.rim
        return carry

    lax.fori_loop(0, SUBSTEPS, substep, 0)
    second = []
    for n, dst in enumerate((eta_out, ub_out, vb_out)):
        flats[n] = own[n, TOP : TOP + ROWS, :]
        second.append(pltpu.make_async_copy(flats.at[n], dst, sem.at[2 + n]))
        second[-1].start()

    def flow_tile(rows, fixed, refs, src):
        gain = (own[1, fixed, :] - mu[fixed, :], own[2, fixed, :] - mv[fixed, :])
        for k in range(LEVELS):
            wet = x_ref[WET + k, rows, :]
            for n, (ref, out) in enumerate(zip(refs, (u_new, v_new))):
                out[k, rows, :] = ref[k, src, :] + mend(n, k, fixed) + wet * gain[n]

    def flow_loop(i, carry):
        rows, fixed = tile_of(i)
        flow_tile(rows, fixed, (us, vs), rows)
        return carry

    lax.fori_loop(1, ROWS // 8 - 1, flow_loop, 0)
    for n, i in enumerate((0, ROWS // 8 - 1)):
        flow_tile(slice(8 * i, 8 * i + 8), slice(8 * i + TOP, 8 * i + TOP + 8), (us2, vs2), slice(8 * n, 8 * n + 8))
    last = [pltpu.make_async_copy(src, dst, sem.at[5 + n]) for n, (src, dst) in enumerate(((u_new, u_out), (v_new, v_out)))]
    for copy in last:
        copy.start()
    for copy in first + second + last:
        copy.wait()


def colour(parity, lats, lons):
    pairs = []
    for lat in range(lats):
        for lon in range(lons):
            if (lat + parity) % 2 == 0:
                to = (lon, lat + 1) if lat + 1 < lats else (lons - 1 - lon, lat)
            elif lat > 0:
                to = (lon, lat - 1)
            else:
                continue
            pairs.append((lon * lats + lat, to[0] * lats + to[1]))
    return pairs


def local(u, v, t, s, w, bottom, eta, ub, vb, cor):
    lats = lax.axis_size("lat")
    lons = lax.axis_size("lon")
    raw = tuple(pltpu.with_memory_space_constraint(z, pltpu.HBM) for z in (u, v, t, s, w, bottom, eta, ub, vb, cor))
    vmem = pltpu.VMEM
    dma = pltpu.SemaphoreType.DMA
    two = (2, LEVELS, 16, COLS)
    a, b = call(
        pack_rows, "pack_rows", [(ROW_SLAB, COLS)] * 2,
        [vmem(two, F32)] * 4 + [vmem(two, jnp.int32), vmem((4, ROWS, COLS), F32), vmem(PLANE, jnp.int32)]
        + [vmem((24, COLS), F32)] * 2 + [vmem((40, COLS), F32)] * 3 + [dma((15,))],
        1_000_000, *raw, ins=[HBM] * 10,
    )
    b = lax.ppermute(b, ("lon", "lat"), colour(1, lats, lons))
    a = lax.ppermute(a, ("lon", "lat"), colour(0, lats, lons))
    x, ec, wc, us, vs, tn, sn, sums = call(
        centre, "centre", [(PLANES, ROWS, COLS)] + [(SLABS, ROWS, COLS)] * 2 + [CUBE] * 4 + [(5, ROWS, COLS)],
        [vmem(CUBE, F32)] * 4 + [vmem(CUBE, jnp.int32), vmem(PLANE, jnp.int32), dma((10,))],
        20_000_000, *raw, ins=[HBM] * 10,
    )
    e_mine, w_mine = call(pack_rims, "pack_rims", [(SLABS, SLAB_ROWS, COLS)] * 2, [], 1_000_000, a, b, ec, wc)
    e_got = lax.ppermute(e_mine, "lon", [((i + 1) % lons, i) for i in range(lons)])
    w_got = lax.ppermute(w_mine, "lon", [(i, (i + 1) % lons) for i in range(lons)])
    window = vmem((FLAT, 32, COLS), F32)
    us2, vs2, tn2, sn2, sums2 = call(
        edges, "edges", [(LEVELS, 16, COLS)] * 4 + [(5, 32, COLS)], [window] * 2, 10_000_000, x, a, b,
    )
    wide = vmem((2, HIGH, COLS), F32)
    thin = vmem((HIGH, COLS), F32)
    slab = vmem((SLABS + 2, HIGH, COLS), F32)
    four = vmem((4, HIGH, COLS), F32)
    return tuple(
        call(
            step, "step", [CUBE] * 4 + [PLANE] * 3,
            [slab] * 2 + [four] * 3 + [vmem((5, HIGH, COLS), F32)] + [wide] * 3 + [thin] * 2 + [wide] * 3
            + [vmem(CUBE, F32)] * 4 + [vmem((3, ROWS, COLS), F32), dma((7,))],
            50_000_000, x, a, b, e_mine, w_mine, e_got, w_got, us, vs, tn, sn, sums, us2, vs2, tn2, sn2, sums2,
            outs=[HBM] * 7,
        )
    )


def solution(mesh):
    deep = P(None, "lat", "lon")
    flat = P("lat", "lon")
    return jax.shard_map(
        local,
        mesh=mesh,
        in_specs=(deep,) * 5 + (flat,) * 5,
        out_specs=(deep,) * 4 + (flat,) * 3,
        check_vma=False,
    )
```

```python
import jax
import jax.numpy as jnp
from jax import lax
from jax.experimental import pallas as pl
from jax.experimental.pallas import tpu as pltpu
from jax.sharding import PartitionSpec as P


SUBSTEPS = 4
LEVELS = 10
ROWS = 64
COLS = 128
U, V, D, WET, T, S, FLAT = 0, 10, 20, 30, 40, 50, 60
PLANES = 64
BLOCKS = 44
NINTH = 8 * BLOCKS
PAIRS = NINTH + 24
ROW_SLAB = PAIRS + 4 * LEVELS
STRIDE = 11
SLABS = 4
SLAB_ROWS = 88
TOP = 16
HIGH = 96
BAND = 80

advect_scale = 0.25
viscous_scale = 0.02
pressure_scale = 0.5
rotation_scale = 0.3
thermal_scale = 0.2
haline_scale = 0.8
surface_depth = 0.25
gravity_scale = 0.3
divergence_scale = 0.3

F32 = jnp.float32
SIGNS = [-1.0] * 20 + [1.0] * 20 + [1.0, -1.0, -1.0, 1.0]
THICK = [(k + 1.0) * (2.0 / (LEVELS * (LEVELS + 1))) for k in range(LEVELS)]
HBM = pl.BlockSpec(memory_space=pltpu.HBM)
VMEM = pl.BlockSpec(memory_space=pltpu.VMEM)
CUBE = (LEVELS, ROWS, COLS)
PLANE = (ROWS, COLS)


def call(kernel, out, scratch, flops, *args, ins=None, outs=None):
    return pl.pallas_call(
        kernel,
        out_shape=[jax.ShapeDtypeStruct(s, F32) for s in out],
        in_specs=ins or [VMEM] * len(args),
        out_specs=outs or [VMEM] * len(out),
        scratch_shapes=scratch,
        cost_estimate=pl.CostEstimate(flops=flops, bytes_accessed=2_000_000, transcendentals=0),
        compiler_params=pltpu.CompilerParams(vmem_limit_bytes=LIMIT),
    )(*args)


LIMIT = 40 * 1024 * 1024


def lanes(rows=8):
    return lax.broadcasted_iota(jnp.int32, (rows, COLS), 1)


def flip_lanes(x):
    return jnp.take_along_axis(x, COLS - 1 - lax.broadcasted_iota(jnp.int32, x.shape, 1), axis=1, mode="promise_in_bounds")


def flip_rows(x):
    return jnp.take_along_axis(x, 7 - lax.broadcasted_iota(jnp.int32, x.shape, 0), axis=0, mode="promise_in_bounds")


def turn(x, shift):
    return pltpu.roll(x, shift % COLS, 1)


def lat_place():
    index = lax.axis_index("lat")
    return index % 2 == 0, index == lax.axis_size("lat") - 1


def fetch(pairs, sem):
    copies = [pltpu.make_async_copy(src, dst, sem.at[n]) for n, (src, dst) in enumerate(pairs)]
    for copy in copies:
        copy.start()
    return copies


def pack_rows(u, v, t, s, w, bottom, eta, ub, vb, cor, a_ref, b_ref,
              u2, v2, t2, s2, w2, flat, deep, low9, high9, low2, high2, fold2, sem):
    even, top = lat_place()
    moves = []
    for src, dst in ((u, u2), (v, v2), (t, t2), (s, s2), (w, w2)):
        moves.append((src.at[:, 0:16, :], dst.at[0]))
        moves.append((src.at[:, ROWS - 16 : ROWS, :], dst.at[1]))
    for n, src in enumerate((eta, ub, vb, cor)):
        moves.append((src, flat.at[n]))
    moves.append((bottom, deep))
    for copy in fetch(moves, sem):
        copy.wait()
    low9[...] = jnp.zeros((24, COLS), F32)
    high9[...] = jnp.zeros((24, COLS), F32)
    d0 = deep[0:16, :]
    d1 = deep[ROWS - 16 : ROWS, :]

    def send(r, down, up, fold):
        a_ref[r : r + 8, :] = jnp.where(even, up, down)
        b_ref[r : r + 8, :] = jnp.where(even, down, jnp.where(top, fold, up))

    def put(p, down, up):
        send(8 * p, down, up, SIGNS[p] * flip_rows(flip_lanes(up)))

    for k in range(LEVELS):
        wl = jnp.where(k < d0, w2[0, k].astype(F32), 0.0)
        wh = jnp.where(k < d1, w2[1, k].astype(F32), 0.0)
        for f, ref in ((U, u2), (V, v2)):
            low = ref[0, k] * wl
            high = ref[1, k] * wh
            put(f + k, low[0:8], high[8:16])
            low9[f + k : f + k + 1, :] = low[8:9]
            high9[f + k : f + k + 1, :] = high[7:8]
        tl = t2[0, k] * wl
        th = t2[1, k] * wh
        sl = s2[0, k] * wl
        sh = s2[1, k] * wh
        put(D + k, (haline_scale * sl - thermal_scale * tl)[0:8], (haline_scale * sh - thermal_scale * th)[8:16])
        put(WET + k, wl[0:8], wh[8:16])
        for n, (low, high) in enumerate(((tl, th), (sl, sh))):
            r = 4 * k + 2 * n
            low2[r : r + 2, :] = low[0:2]
            high2[r : r + 2, :] = high[14:16]
            fold2[r : r + 1, :] = high[15:16]
            fold2[r + 1 : r + 2, :] = high[14:15]
    for n in range(4):
        put(40 + n, flat[n, 0:8, :], flat[n, ROWS - 8 : ROWS, :])
    for r in range(0, 24, 8):
        up = high9[r : r + 8, :]
        send(NINTH + r, low9[r : r + 8, :], up, -flip_lanes(up))
    for r in range(0, 40, 8):
        send(PAIRS + r, low2[r : r + 8, :], high2[r : r + 8, :], flip_lanes(fold2[r : r + 8, :]))


class Columns:
    def __init__(self, lane):
        self.lane = lane
        zero = jnp.zeros((8, COLS), F32)
        self.east = [zero] * SLABS
        self.west = [zero] * SLABS

    def put_east(self, q, moved, at, count):
        lane = self.lane
        self.east[q] = jnp.where((lane >= at) & (lane < at + count), moved, self.east[q])

    def put_west(self, q, moved, end, count):
        lane = self.lane
        low = (end - count) % COLS
        here = (lane >= low) & (lane < end) if low < end else (lane >= low) | (lane < end)
        self.west[q] = jnp.where(here, moved, self.west[q])

    def put(self, q, val, shift, count):
        moved = turn(val, shift)
        self.put_east(q, moved, shift, count)
        self.put_west(q, moved, shift, count)

    def level(self, q, k, val):
        self.put(q, val, STRIDE * k + 2, 9)

    def tracers(self, k, t, s):
        for q, val in enumerate((t, s)):
            self.put_east(q, turn(val, STRIDE * k), STRIDE * k, 2)
            self.put_west(q, turn(val, STRIDE * k + 4), STRIDE * k + 4, 2)

    def flat(self, n, val):
        if n % 2 == 0:
            self.put(n // 2, val, 112, 9)
        else:
            self.put(n // 2, val, 121, 7)


def shifted(x, d):
    lane = lanes()
    keep = lane < COLS - d if d > 0 else lane >= -d
    return jnp.where(keep, turn(x, -d), 0.0)


def smoothed(at, p, c, shift):
    north, south = at(p, 1), at(p, -1)
    q = (north + south) - 4.0 * c
    both = shift(c, 2) + shift(c, -2) + (at(p, 2) + at(p, -2))
    return both + 2.0 * ((shift(q, 1) + shift(q, -1)) - 4.0 * q) - 12.0 * c, north, south


def own_tile(at, spin, put_u, put_v, put_t, put_s):
    zero = jnp.zeros((8, COLS), F32)
    acc = acc_ns = sum_u = sum_v = old_u = old_v = depth = zero
    for k in range(LEVELS):
        wet = at(WET + k, 0)
        u = at(U + k, 0)
        v = at(V + k, 0)
        smooth_u, _, _ = smoothed(at, U + k, u, shifted)
        smooth_v, v_north, v_south = smoothed(at, V + k, v, shifted)
        half = (0.5 * THICK[k]) * at(D + k, 0)
        half_ns = (0.5 * THICK[k]) * (at(D + k, 1) - at(D + k, -1))
        pressure = acc + half
        pressure_ns = acc_ns + half_ns
        acc = pressure + half
        acc_ns = pressure_ns + half_ns
        slope = shifted(pressure, 1) - shifted(pressure, -1)
        u_star = wet * (u + spin * v - (0.5 * pressure_scale) * slope - viscous_scale * smooth_u)
        v_star = wet * (v - spin * u - (0.5 * pressure_scale) * pressure_ns - viscous_scale * smooth_v)
        sum_u = sum_u + THICK[k] * u_star
        sum_v = sum_v + THICK[k] * v_star
        old_u = old_u + THICK[k] * u
        old_v = old_v + THICK[k] * v
        depth = depth + THICK[k] * wet
        if put_u is None:
            continue
        put_u(k, u_star)
        put_v(k, v_star)
        for p, put in ((T + k, put_t), (S + k, put_s)):
            c = at(p, 0)
            smooth, north, south = smoothed(at, p, c, shifted)
            flux = u * c
            advect = (shifted(flux, 1) - shifted(flux, -1)) + (v_north * north - v_south * south)
            put(k, wet * (c - (0.5 * advect_scale) * advect - viscous_scale * smooth))
    return sum_u, sum_v, sum_u - old_u, sum_v - old_v, depth


def level_sums(mats):
    i = lax.broadcasted_iota(jnp.int32, (COLS, COLS), 0)
    j = lax.broadcasted_iota(jnp.int32, (COLS, COLS), 1)
    for side, offset in enumerate((0, 7)):
        def place(x):
            y = (x + offset) & (COLS - 1)
            return jnp.where(y < STRIDE * LEVELS, y % STRIDE, -1), y // STRIDE

        def above(src, dst):
            same = (src[0] == dst[0]) & (src[0] >= 0)
            return jnp.where(same & (src[1] < dst[1]), 1.0, jnp.where(same & (src[1] == dst[1]), 0.5, 0.0))

        src = place(i)
        mats[2 * side] = above(src, place(j))
        mats[2 * side + 1] = above(src, place(j + 1)) - above(src, place(j - 1))
        target = j + 2 if side == 0 else (j + 9) & (COLS - 1)
        low = 2 if side == 0 else 0
        mats[4 + side] = jnp.where((target >= low) & (target < low + 9) & (src[0] == target), 1.0, 0.0)
        if side == 0:
            mats[6] = jnp.where((src[0] == ((j + 2) & (COLS - 1))) & (((j + 2) & (COLS - 1)) < 4), 1.0, 0.0)


def dot(x, mat):
    return jnp.dot(x, mat, precision=lax.Precision.HIGHEST, preferred_element_type=F32)


def centre(u, v, t, s, w, bottom, eta, ub, vb, cor, x_ref, ec, wc, us, vs, tn, sn, sums, mats,
           u2, v2, t2, s2, w2, deep, sem):
    moves = list(zip((u, v, t, s, w, bottom), (u2, v2, t2, s2, w2, deep)))
    for n, src in enumerate((eta, ub, vb, cor)):
        moves.append((src, x_ref.at[FLAT + n]))
    copies = fetch(moves, sem)
    level_sums(mats)
    for copy in copies:
        copy.wait()
    lane = lanes()

    def pack(i, carry):
        rows = pl.ds(pl.multiple_of(8 * i, 8), 8)
        bed = deep[rows, :]
        columns = Columns(lane)
        for k in range(LEVELS):
            wet = jnp.where(k < bed, w2[k, rows, :].astype(F32), 0.0)
            uk = u2[k, rows, :] * wet
            vk = v2[k, rows, :] * wet
            tk = t2[k, rows, :] * wet
            sk = s2[k, rows, :] * wet
            dk = haline_scale * sk - thermal_scale * tk
            for p, val in ((U, uk), (V, vk), (D, dk), (WET, wet), (T, tk), (S, sk)):
                x_ref[p + k, rows, :] = val
            for q, val in enumerate((uk, vk, dk, wet)):
                columns.level(q, k, val)
            columns.tracers(k, tk, sk)
        for n in range(4):
            columns.flat(n, x_ref[FLAT + n, rows, :])
        for q in range(SLABS):
            ec[q, rows, :] = columns.east[q]
            wc[q, rows, :] = columns.west[q]
        return carry

    lax.fori_loop(0, ROWS // 8, pack, 0)

    def inner(i, carry):
        r0 = 8 * i
        rows = pl.ds(pl.multiple_of(r0, 8), 8)

        def store(ref):
            def put(k, val):
                ref[k, rows, :] = val

            return put

        got = own_tile(
            lambda p, d: x_ref[p, pl.ds(r0 + d, 8), :], rotation_scale * x_ref[FLAT + 3, rows, :],
            store(us), store(vs), store(tn), store(sn),
        )
        for n in range(5):
            sums[n, rows, :] = got[n]
        return carry

    lax.fori_loop(1, ROWS // 8 - 1, inner, 0)


def pack_rims(a_ref, b_ref, ec, wc, e_ref, w_ref):
    even, _ = lat_place()
    lane = lanes()
    sub = lax.broadcasted_iota(jnp.int32, (8, COLS), 0)
    for q in range(SLABS):
        e_ref[q, TOP : TOP + ROWS, :] = ec[q]
        w_ref[q, TOP : TOP + ROWS, :] = wc[q]

    def both(r, n):
        a = a_ref[r : r + n, :]
        b = b_ref[r : r + n, :]
        return jnp.where(even, b, a), jnp.where(even, a, b)

    ninth, south, north = Columns(lane), Columns(lane), Columns(lane)
    for k in range(LEVELS):
        for q in range(4):
            lo, hi = both(8 * (10 * q + k), 8)
            south.level(q, k, lo)
            north.level(q, k, hi)
            if q < 2:
                lo, hi = both(NINTH + 10 * q + k, 1)
                ninth.level(q, k, jnp.where(sub == 0, lo, hi))
        pairs = [both(PAIRS + 4 * k + n, 1) for n in range(4)]
        t_lo, s_lo = (jnp.where(sub == 6, pairs[n][0], pairs[n + 1][0]) for n in (0, 2))
        t_hi, s_hi = (jnp.where(sub == 0, pairs[n][1], pairs[n + 1][1]) for n in (0, 2))
        south.tracers(k, t_lo, s_lo)
        north.tracers(k, t_hi, s_hi)
    for n in range(4):
        lo, hi = both(8 * (40 + n), 8)
        south.flat(n, lo)
        north.flat(n, hi)
    for at, columns in ((0, ninth), (8, south), (TOP + ROWS, north)):
        for q in range(SLABS):
            e_ref[q, at : at + 8, :] = columns.east[q]
            w_ref[q, at : at + 8, :] = columns.west[q]


def edges(x_ref, a_ref, b_ref, us, vs, tn, sn, sums, low, high):
    even, _ = lat_place()

    def both(r, n):
        a = a_ref[pl.ds(r, n), :]
        b = b_ref[pl.ds(r, n), :]
        return jnp.where(even, b, a), jnp.where(even, a, b)

    def place(p, carry):
        low[p, 16:32, :] = x_ref[p, 0:16, :]
        high[p, 0:16, :] = x_ref[p, ROWS - 16 : ROWS, :]
        return carry

    lax.fori_loop(0, FLAT, place, 0)

    def rims(p, carry):
        lo, hi = both(pl.multiple_of(8 * p, 8), 8)
        low[p, 8:16, :] = lo
        high[p, 16:24, :] = hi
        return carry

    lax.fori_loop(0, 40, rims, 0)
    for p in range(20):
        lo, hi = both(NINTH + p, 1)
        low[p, 7:8, :] = lo
        high[p, 24:25, :] = hi
    for k in range(LEVELS):
        for n, p in enumerate((T + k, S + k)):
            lo, hi = both(PAIRS + 4 * k + 2 * n, 2)
            low[p, 14:16, :] = lo
            high[p, 16:18, :] = hi
    spin_low, spin_high = both(8 * 43, 8)
    for n, (ref, r0, spin) in enumerate((
        (low, 16, x_ref[FLAT + 3, 0:8, :]),
        (high, 8, x_ref[FLAT + 3, ROWS - 8 : ROWS, :]),
        (low, 8, spin_low),
        (high, 16, spin_high),
    )):
        def store(out):
            def put(k, val):
                out[k, 8 * n : 8 * n + 8, :] = val

            return put

        puts = [store(out) for out in (us, vs, tn, sn)] if n < 2 else [None] * 4
        got = own_tile(lambda p, d: ref[p, r0 + d : r0 + d + 8, :], rotation_scale * spin, *puts)
        for m in range(5):
            sums[m, 8 * n : 8 * n + 8, :] = got[m]


class Wide:
    def __init__(self, own, rim):
        self.own, self.rim = own, rim

    def with_other(self, other, op):
        if isinstance(other, Wide):
            return Wide(op(self.own, other.own), op(self.rim, other.rim))
        return Wide(op(self.own, other), op(self.rim, other))

    def __add__(self, other):
        return self.with_other(other, lambda a, b: a + b)

    def __sub__(self, other):
        return self.with_other(other, lambda a, b: a - b)

    def __mul__(self, other):
        return self.with_other(other, lambda a, b: a * b)

    __rmul__ = __mul__

    def __truediv__(self, other):
        return self.with_other(other, lambda a, b: a / b)


def slope(x):
    lane = lanes()
    east_own, east_rim = turn(x.own, -1), turn(x.rim, -1)
    west_own, west_rim = turn(x.own, 1), turn(x.rim, 1)
    last, first = lane == COLS - 1, lane == 0
    return Wide(
        jnp.where(last, east_rim, east_own) - jnp.where(first, west_rim, west_own),
        jnp.where(last, east_own, east_rim) - jnp.where(first, west_own, west_rim),
    )


def step(x_ref, a_ref, b_ref, e_mine, w_mine, e_got, w_got, us, vs, tn, sn, sums, us2, vs2, tn2, sn2, sums2, mats,
         u_out, v_out, t_out, s_out, eta_out, ub_out, vb_out,
         es, ws, own, rim, fix, total, col, fu, fv, mu, mv, tu, tv, spins, t_new, s_new, u_new, v_new, flats, sem):
    even, _ = lat_place()
    lane = lanes()
    rest = lane % STRIDE
    inside = lane < LEVELS * STRIDE
    for r in range(0, SLAB_ROWS, 8):
        for q in range(SLABS):
            here = slice(r, r + 8)
            east = jnp.where((rest < 2) & inside, w_mine[q, here, :], e_got[q, here, :])
            west = jnp.where(((rest == 2) | (rest == 3)) & inside, e_mine[q, here, :], w_got[q, here, :])
            for ref, val in ((es, east), (ws, west)):
                if r == 0:
                    ref[q, 7:8, :] = val[0:1]
                    ref[q, TOP + ROWS + 8 : TOP + ROWS + 9, :] = val[1:2]
                else:
                    ref[q, here, :] = val
            if q < 2 and r > 0:
                es[SLABS + q, here, :] = turn(e_got[q, here, :], 2)
                ws[SLABS + q, here, :] = turn(w_got[q, here, :], -2)
    for n in range(4):
        a = a_ref[8 * (40 + n) : 8 * (41 + n), :]
        b = b_ref[8 * (40 + n) : 8 * (41 + n), :]
        own[n, 8:16, :] = jnp.where(even, b, a)
        own[n, TOP : TOP + ROWS, :] = x_ref[FLAT + n]
        own[n, TOP + ROWS : TOP + ROWS + 8, :] = jnp.where(even, a, b)
        q, second = divmod(n, 2)
        for r in range(8, 88, 8):
            at = (121, 7) if second else (112, 16)
            rim[n, r : r + 8, :] = turn(jnp.where(lane >= at[0], es[q, r : r + 8, :], ws[q, r : r + 8, :]), at[1])
    for m in range(5):
        total[m, 8:16, :] = sums2[m, 16:24, :]
        total[m, 16:24, :] = sums2[m, 0:8, :]
        total[m, 24:72, :] = sums[m, 8:56, :]
        total[m, 72:80, :] = sums2[m, 8:16, :]
        total[m, 80:88, :] = sums2[m, 24:32, :]

    short = lane
    lane = lanes(BAND)
    rest = lane % STRIDE
    inside = lane < LEVELS * STRIDE
    level_e = jnp.minimum(lane // STRIDE, LEVELS)
    level_w = jnp.minimum(((lane + 7) % COLS) // STRIDE, LEVELS)
    thick_e = jnp.where(level_e < LEVELS, (level_e + 1).astype(F32) * THICK[0], 0.0)
    thick_w = jnp.where(level_w < LEVELS, (level_w + 1).astype(F32) * THICK[0], 0.0)
    edge = (lane < 2) | (lane >= COLS - 2)
    border = (short < 2) | (short >= COLS - 2)

    def slab_tile(i, carry):
        r0 = BAND * i + 8
        here = pl.ds(pl.multiple_of(r0, 8), BAND)
        parts = []
        for ref, side, thick, ahead in ((es, 0, thick_e, 1), (ws, 1, thick_w, -1)):
            def at(q, d):
                return ref[q, pl.ds(r0 + d, BAND), :]

            def around(x, d):
                return turn(x, -d)

            if ahead > 0:
                near, pair = (rest == 2) & inside, ((rest == 2) | (rest == 3)) & inside
            else:
                near, pair = (rest == 1) & inside, (rest < 2) & inside
            wet = at(3, 0)
            u = at(0, 0)
            v = at(1, 0)
            weight = thick * at(2, 0)
            weight_ns = thick * (at(2, 1) - at(2, -1))
            pressure = dot(weight, mats[2 * side])
            pressure_slope = dot(weight, mats[2 * side + 1])
            pressure_ns = dot(weight_ns, mats[2 * side])
            smooth_u, un, us_ = smoothed(at, 0, u, around)
            smooth_v, vn, vs_ = smoothed(at, 1, v, around)
            change = pressure_scale * 0.5 * pressure_slope + viscous_scale * smooth_u
            change_ns = pressure_scale * 0.5 * pressure_ns + viscous_scale * smooth_v
            parts.append((wet * thick, -change, -change_ns, u, v, wet))

            def beyond(c, ns, extra):
                far = viscous_scale * jnp.where(pair, c, 0.0)
                close = jnp.where(near, (2.0 * viscous_scale) * (ns - 4.0 * c) + extra, 0.0)
                return -(turn(far, -2 * ahead) + turn(close, -ahead))

            push = (0.5 * pressure_scale * ahead) * pressure
            fixes = [beyond(u, un + us_, push), beyond(v, vn + vs_, 0.0)]
            carry_u = (0.5 * advect_scale * ahead) * u
            for q in (SLABS, SLABS + 1):
                c = at(q, 0)
                fixes.append(beyond(c, at(q, 1) + at(q, -1), carry_u * c))
            parts.append(fixes)
        (we, due, dve, ue, ve, wet_e), fix_e, (ww, duw, dvw, uw, vw, wet_w), fix_w = parts
        own_wet = jnp.where(rest < 2, wet_e, wet_w)
        own_thick = jnp.where(rest < 2, thick_e, thick_w)
        fixes = [own_wet * (x + y) for x, y in zip(fix_e, fix_w)]
        for n in range(4):
            fix[n, here, :] = fixes[n]

        east = jnp.concatenate([we, we * due, we * dve, we * ue, we * ve], axis=0)
        west = jnp.concatenate([ww, ww * duw, ww * dvw, ww * uw, ww * vw], axis=0)
        rims = dot(east, mats[4]) + dot(west, mats[5])
        rim_depth, rim_du, rim_dv, rim_u, rim_v = (rims[BAND * n : BAND * n + BAND] for n in range(5))
        owns = dot(jnp.concatenate([own_thick * fixes[0], own_thick * fixes[1]], axis=0), mats[6])
        spin = Wide(rotation_scale * own[3, here, :], rotation_scale * rim[3, here, :])
        column = Wide(surface_depth + total[4, here, :], surface_depth + rim_depth)
        diff_u = rim_du + spin.rim * rim_v
        diff_v = rim_dv - spin.rim * rim_u
        fix_u, fix_v = owns[0:BAND], owns[BAND : 2 * BAND]
        part = Wide(1.0 / column.own, 1.0 / column.rim)
        for ref, mean, own_sum, own_diff, rim_diff, x in (
            (fu, mu, total[0, here, :], total[2, here, :], diff_u, fix_u),
            (fv, mv, total[1, here, :], total[3, here, :], diff_v, fix_v),
        ):
            ref[0, here, :] = (own_diff + x) * part.own * (1.0 / SUBSTEPS)
            ref[1, here, :] = rim_diff * part.rim * (1.0 / SUBSTEPS)
            mean[here, :] = (own_sum + x) * part.own
        for ref, x in ((col, column), (spins, spin)):
            ref[0, here, :] = x.own
            ref[1, here, :] = x.rim
        return carry

    lax.fori_loop(0, 80 // BAND, slab_tile, 0)

    def mend(n, k, rows_fix):
        return jnp.where(border, turn(fix[n, rows_fix, :], -(STRIDE * k + 2)), 0.0)

    def tile_of(i):
        return pl.ds(pl.multiple_of(8 * i, 8), 8), pl.ds(pl.multiple_of(8 * i + TOP, 8), 8)

    def tracer_tile(rows, fixed, refs, src):
        for n, (ref, out) in enumerate(zip(refs, (t_new, s_new))):
            for k in range(LEVELS):
                out[k, rows, :] = ref[k, src, :] + mend(2 + n, k, fixed)

    def tracer_loop(i, carry):
        rows, fixed = tile_of(i)
        tracer_tile(rows, fixed, (tn, sn), rows)
        return carry

    lax.fori_loop(1, ROWS // 8 - 1, tracer_loop, 0)
    for n, i in enumerate((0, ROWS // 8 - 1)):
        tracer_tile(slice(8 * i, 8 * i + 8), slice(8 * i + TOP, 8 * i + TOP + 8), (tn2, sn2), slice(8 * n, 8 * n + 8))
    first = [pltpu.make_async_copy(src, dst, sem.at[n]) for n, (src, dst) in enumerate(((t_new, t_out), (s_new, s_out)))]
    for copy in first:
        copy.start()

    def wide(ref, at):
        return Wide(ref[0, at, :], ref[1, at, :])

    def keep(ref, at, x):
        ref[0, at, :] = x.own
        ref[1, at, :] = x.rim

    def flat(p, r):
        return Wide(own[p, r : r + 8, :], rim[p, r : r + 8, :])

    def wet_of(column):
        return Wide(jnp.where(column.own > surface_depth, 1.0, 0.0), jnp.where(column.rim > surface_depth, 1.0, 0.0))

    def substep(n, carry):
        for r in range(8, 88, 8):
            here = slice(r, r + 8)
            column = wide(col, here)
            wet = wet_of(column)
            u = flat(1, r)
            v = flat(2, r)
            spin = wide(spins, here)
            un = wet * (u - (0.5 * gravity_scale) * slope(flat(0, r)) + spin * v + wide(fu, here))
            vn = wet * (v - (0.5 * gravity_scale) * (flat(0, r + 1) - flat(0, r - 1)) - spin * u + wide(fv, here))
            for p, x in ((1, un), (2, vn)):
                own[p, here, :] = x.own
                rim[p, here, :] = x.rim
            keep(tu, here, column * un)
            keep(tv, here, column * vn)
        for r in range(8, 88, 8):
            here = slice(r, r + 8)
            wet = wet_of(wide(col, here))
            flow = slope(wide(tu, here)) + (wide(tv, slice(r + 1, r + 9)) - wide(tv, slice(r - 1, r + 7)))
            eta = wet * (flat(0, r) - (0.5 * divergence_scale) * flow)
            own[0, here, :] = eta.own
            rim[0, here, :] = eta.rim
        return carry

    lax.fori_loop(0, SUBSTEPS, substep, 0)
    second = []
    for n, dst in enumerate((eta_out, ub_out, vb_out)):
        flats[n] = own[n, TOP : TOP + ROWS, :]
        second.append(pltpu.make_async_copy(flats.at[n], dst, sem.at[2 + n]))
        second[-1].start()

    def flow_tile(rows, fixed, refs, src):
        gain = (own[1, fixed, :] - mu[fixed, :], own[2, fixed, :] - mv[fixed, :])
        for k in range(LEVELS):
            wet = x_ref[WET + k, rows, :]
            for n, (ref, out) in enumerate(zip(refs, (u_new, v_new))):
                out[k, rows, :] = ref[k, src, :] + mend(n, k, fixed) + wet * gain[n]

    def flow_loop(i, carry):
        rows, fixed = tile_of(i)
        flow_tile(rows, fixed, (us, vs), rows)
        return carry

    lax.fori_loop(1, ROWS // 8 - 1, flow_loop, 0)
    for n, i in enumerate((0, ROWS // 8 - 1)):
        flow_tile(slice(8 * i, 8 * i + 8), slice(8 * i + TOP, 8 * i + TOP + 8), (us2, vs2), slice(8 * n, 8 * n + 8))
    last = [pltpu.make_async_copy(src, dst, sem.at[5 + n]) for n, (src, dst) in enumerate(((u_new, u_out), (v_new, v_out)))]
    for copy in last:
        copy.start()
    for copy in first + second + last:
        copy.wait()


def colour(parity, lats, lons):
    pairs = []
    for lat in range(lats):
        for lon in range(lons):
            if (lat + parity) % 2 == 0:
                to = (lon, lat + 1) if lat + 1 < lats else (lons - 1 - lon, lat)
            elif lat > 0:
                to = (lon, lat - 1)
            else:
                continue
            pairs.append((lon * lats + lat, to[0] * lats + to[1]))
    return pairs


def local(u, v, t, s, w, bottom, eta, ub, vb, cor):
    lats = lax.axis_size("lat")
    lons = lax.axis_size("lon")
    raw = tuple(pltpu.with_memory_space_constraint(z, pltpu.HBM) for z in (u, v, t, s, w, bottom, eta, ub, vb, cor))
    vmem = pltpu.VMEM
    dma = pltpu.SemaphoreType.DMA
    two = (2, LEVELS, 16, COLS)
    a, b = call(
        pack_rows, [(ROW_SLAB, COLS)] * 2,
        [vmem(two, F32)] * 4 + [vmem(two, jnp.int32), vmem((4, ROWS, COLS), F32), vmem(PLANE, jnp.int32)]
        + [vmem((24, COLS), F32)] * 2 + [vmem((40, COLS), F32)] * 3 + [dma((15,))],
        1_000_000, *raw, ins=[HBM] * 10,
    )
    b = lax.ppermute(b, ("lon", "lat"), colour(1, lats, lons))
    a = lax.ppermute(a, ("lon", "lat"), colour(0, lats, lons))
    x, ec, wc, us, vs, tn, sn, sums, mats = call(
        centre, [(PLANES, ROWS, COLS)] + [(SLABS, ROWS, COLS)] * 2 + [CUBE] * 4 + [(5, ROWS, COLS), (7, COLS, COLS)],
        [vmem(CUBE, F32)] * 4 + [vmem(CUBE, jnp.int32), vmem(PLANE, jnp.int32), dma((10,))],
        20_000_000, *raw, ins=[HBM] * 10,
    )
    e_mine, w_mine = call(pack_rims, [(SLABS, SLAB_ROWS, COLS)] * 2, [], 1_000_000, a, b, ec, wc)
    e_got = lax.ppermute(e_mine, "lon", [((i + 1) % lons, i) for i in range(lons)])
    w_got = lax.ppermute(w_mine, "lon", [(i, (i + 1) % lons) for i in range(lons)])
    window = vmem((FLAT, 32, COLS), F32)
    us2, vs2, tn2, sn2, sums2 = call(
        edges, [(LEVELS, 16, COLS)] * 4 + [(5, 32, COLS)], [window] * 2, 10_000_000, x, a, b,
    )
    wide = vmem((2, HIGH, COLS), F32)
    thin = vmem((HIGH, COLS), F32)
    slab = vmem((SLABS + 2, HIGH, COLS), F32)
    four = vmem((4, HIGH, COLS), F32)
    return tuple(
        call(
            step, [CUBE] * 4 + [PLANE] * 3,
            [slab] * 2 + [four] * 3 + [vmem((5, HIGH, COLS), F32)] + [wide] * 3 + [thin] * 2 + [wide] * 3
            + [vmem(CUBE, F32)] * 4 + [vmem((3, ROWS, COLS), F32), dma((7,))],
            50_000_000, x, a, b, e_mine, w_mine, e_got, w_got, us, vs, tn, sn, sums, us2, vs2, tn2, sn2, sums2, mats,
            outs=[HBM] * 7,
        )
    )


def solution(mesh):
    deep = P(None, "lat", "lon")
    flat = P("lat", "lon")
    return jax.shard_map(
        local,
        mesh=mesh,
        in_specs=(deep,) * 5 + (flat,) * 5,
        out_specs=(deep,) * 4 + (flat,) * 3,
        check_vma=False,
    )
```

```python
import jax
import jax.numpy as jnp
from jax import lax
from jax.experimental import pallas as pl
from jax.experimental.pallas import tpu as pltpu
from jax.sharding import PartitionSpec as P


SUBSTEPS = 4
LEVELS = 10
ROWS = 64
COLS = 128
U, V, D, WET, T, S, FLAT = 0, 10, 20, 30, 40, 50, 60
PLANES = 64
AT_PAIR = 120
AT_FLAT = AT_PAIR + 64
AT_SUM = AT_FLAT + 32
AT_SLAB = AT_SUM + 24
AT_NINE = AT_SLAB + 64
ROW_SLAB = AT_NINE + 8
STRIDE = 11
SLABS = 4
SLAB_ROWS = 88
TOP = 16
HIGH = 96
BAND = 80

advect_scale = 0.25
viscous_scale = 0.02
pressure_scale = 0.5
rotation_scale = 0.3
thermal_scale = 0.2
haline_scale = 0.8
surface_depth = 0.25
gravity_scale = 0.3
divergence_scale = 0.3

F32 = jnp.float32
THICK = [(k + 1.0) * (2.0 / (LEVELS * (LEVELS + 1))) for k in range(LEVELS)]
HBM = pl.BlockSpec(memory_space=pltpu.HBM)
VMEM = pl.BlockSpec(memory_space=pltpu.VMEM)
CUBE = (LEVELS, ROWS, COLS)
PLANE = (ROWS, COLS)


def call(kernel, out, scratch, flops, *args, ins=None, outs=None):
    return pl.pallas_call(
        kernel,
        out_shape=[jax.ShapeDtypeStruct(s, F32) for s in out],
        in_specs=ins or [VMEM] * len(args),
        out_specs=outs or [VMEM] * len(out),
        scratch_shapes=scratch,
        cost_estimate=pl.CostEstimate(flops=flops, bytes_accessed=2_000_000, transcendentals=0),
        compiler_params=pltpu.CompilerParams(vmem_limit_bytes=LIMIT),
    )(*args)


LIMIT = 40 * 1024 * 1024


def lanes(rows=8):
    return lax.broadcasted_iota(jnp.int32, (rows, COLS), 1)


def flip_lanes(x):
    return jnp.take_along_axis(x, COLS - 1 - lax.broadcasted_iota(jnp.int32, x.shape, 1), axis=1, mode="promise_in_bounds")


def flip_rows(x):
    return jnp.take_along_axis(x, 7 - lax.broadcasted_iota(jnp.int32, x.shape, 0), axis=0, mode="promise_in_bounds")


def turn(x, shift):
    return pltpu.roll(x, shift % COLS, 1)


def lat_place():
    index = lax.axis_index("lat")
    return index % 2 == 0, index == lax.axis_size("lat") - 1


def lon_odd():
    return lax.axis_index("lon") % 2 == 1


def fetch(pairs, sem):
    copies = [pltpu.make_async_copy(src, dst, sem.at[n]) for n, (src, dst) in enumerate(pairs)]
    for copy in copies:
        copy.start()
    return copies


class Columns:
    def __init__(self, lane):
        self.lane = lane
        zero = jnp.zeros((8, COLS), F32)
        self.east = [zero] * SLABS
        self.west = [zero] * SLABS

    def put_east(self, q, moved, at, count):
        lane = self.lane
        self.east[q] = jnp.where((lane >= at) & (lane < at + count), moved, self.east[q])

    def put_west(self, q, moved, end, count):
        lane = self.lane
        low = (end - count) % COLS
        here = (lane >= low) & (lane < end) if low < end else (lane >= low) | (lane < end)
        self.west[q] = jnp.where(here, moved, self.west[q])

    def put(self, q, val, shift, count):
        moved = turn(val, shift)
        self.put_east(q, moved, shift, count)
        self.put_west(q, moved, shift, count)

    def level(self, q, k, val):
        self.put(q, val, STRIDE * k + 2, 9)

    def tracers(self, k, t, s):
        for q, val in enumerate((t, s)):
            self.put_east(q, turn(val, STRIDE * k), STRIDE * k, 2)
            self.put_west(q, turn(val, STRIDE * k + 4), STRIDE * k + 4, 2)

    def flat(self, n, val):
        if n % 2 == 0:
            self.put(n // 2, val, 112, 9)
        else:
            self.put(n // 2, val, 121, 7)


def shifted(x, d):
    lane = lanes()
    keep = lane < COLS - d if d > 0 else lane >= -d
    return jnp.where(keep, turn(x, -d), 0.0)


def smoothed(at, p, c, shift):
    north, south = at(p, 1), at(p, -1)
    q = (north + south) - 4.0 * c
    both = shift(c, 2) + shift(c, -2) + (at(p, 2) + at(p, -2))
    return both + 2.0 * ((shift(q, 1) + shift(q, -1)) - 4.0 * q) - 12.0 * c, north, south


def own_tile(at, spin, put_u, put_v, put_t, put_s):
    zero = jnp.zeros((8, COLS), F32)
    acc = acc_ns = sum_u = sum_v = old_u = old_v = depth = zero
    for k in range(LEVELS):
        wet = at(WET + k, 0)
        u = at(U + k, 0)
        v = at(V + k, 0)
        smooth_u, _, _ = smoothed(at, U + k, u, shifted)
        smooth_v, v_north, v_south = smoothed(at, V + k, v, shifted)
        half = (0.5 * THICK[k]) * at(D + k, 0)
        half_ns = (0.5 * THICK[k]) * (at(D + k, 1) - at(D + k, -1))
        pressure = acc + half
        pressure_ns = acc_ns + half_ns
        acc = pressure + half
        acc_ns = pressure_ns + half_ns
        slope = shifted(pressure, 1) - shifted(pressure, -1)
        u_star = wet * (u + spin * v - (0.5 * pressure_scale) * slope - viscous_scale * smooth_u)
        v_star = wet * (v - spin * u - (0.5 * pressure_scale) * pressure_ns - viscous_scale * smooth_v)
        sum_u = sum_u + THICK[k] * u_star
        sum_v = sum_v + THICK[k] * v_star
        old_u = old_u + THICK[k] * u
        old_v = old_v + THICK[k] * v
        depth = depth + THICK[k] * wet
        if put_u is None:
            continue
        put_u(k, u_star)
        put_v(k, v_star)
        for p, put in ((T + k, put_t), (S + k, put_s)):
            c = at(p, 0)
            smooth, north, south = smoothed(at, p, c, shifted)
            flux = u * c
            advect = (shifted(flux, 1) - shifted(flux, -1)) + (v_north * north - v_south * south)
            put(k, wet * (c - (0.5 * advect_scale) * advect - viscous_scale * smooth))
    return sum_u, sum_v, sum_u - old_u, sum_v - old_v, depth


def mirrored_lanes(side):
    lane = lanes()
    offset = 7 * side
    y = (lane + offset) & (COLS - 1)
    level = y // STRIDE
    col = y % STRIDE
    group = y < STRIDE * LEVELS
    second = lane >= (121 if side == 0 else 112)
    source = jnp.where(group, 2 * STRIDE * level + 3 - lane, jnp.where(second, 241 - lane, 223 - lane)) & (COLS - 1)
    tracer = (col < 2) if side == 0 else (col >= STRIDE - 2)
    with_u = jnp.where(group, jnp.where(tracer, 1.0, -1.0), jnp.where(second, -1.0, 1.0))
    with_v = jnp.where(group, jnp.where(tracer, 1.0, -1.0), jnp.where(second, 1.0, -1.0))
    return source, (with_u, with_v, 1.0, 1.0)


def pick(x, source):
    return jnp.take_along_axis(x, source, axis=1, mode="promise_in_bounds")


def pack_rows(u, v, t, s, w, bottom, eta, ub, vb, cor, a_ref, b_ref,
              u2, v2, t2, s2, w2, flat, deep, lo, hi, low4, high4, fold4, low2, high2, fold2, low1, high1, fold1, sem):
    even, top = lat_place()
    lane = lanes()
    sub = lax.broadcasted_iota(jnp.int32, (8, COLS), 0)
    moves = []
    for src, dst in ((u, u2), (v, v2), (t, t2), (s, s2), (w, w2)):
        moves.append((src.at[:, 0:16, :], dst.at[0]))
        moves.append((src.at[:, ROWS - 16 : ROWS, :], dst.at[1]))
    for n, src in enumerate((eta, ub, vb, cor)):
        moves.append((src, flat.at[n]))
    moves.append((bottom, deep))
    copies = fetch(moves, sem)
    sources = [mirrored_lanes(side) for side in (0, 1)]
    for copy in copies:
        copy.wait()
    for ref in (low2, high2, fold2):
        ref[56:64, :] = jnp.zeros((8, COLS), F32)
    for ref in (low1, high1, fold1):
        ref[...] = jnp.zeros((8, COLS), F32)
    d0 = deep[0:16, :]
    d1 = deep[ROWS - 16 : ROWS, :]
    south, north, ninth = Columns(lane), Columns(lane), Columns(lane)

    def send(r, down, up, fold):
        a_ref[r : r + 8, :] = jnp.where(even, up, down)
        b_ref[r : r + 8, :] = jnp.where(even, down, jnp.where(top, fold, up))

    def turned(x):
        return flip_rows(flip_lanes(x))

    for k in range(LEVELS):
        wl = jnp.where(k < d0, w2[0, k].astype(F32), 0.0)
        wh = jnp.where(k < d1, w2[1, k].astype(F32), 0.0)
        low = [ref[0, k] * wl for ref in (u2, v2, t2, s2)]
        high = [ref[1, k] * wh for ref in (u2, v2, t2, s2)]
        low_d = haline_scale * low[3] - thermal_scale * low[2]
        high_d = haline_scale * high[3] - thermal_scale * high[2]
        for p, q, sign, x, y in (
            (U, 0, -1.0, low[0], high[0]), (V, 1, -1.0, low[1], high[1]), (D, 2, 1.0, low_d, high_d), (WET, 3, 1.0, wl, wh),
        ):
            lo[p + k, 8:24, :] = x
            hi[p + k, 0:16, :] = y
            south.level(q, k, x[0:8])
            north.level(q, k, y[8:16])
            if q < 2:
                ninth.level(q, k, jnp.where(sub == 0, x[8:9], y[7:8]))
            if q < 3:
                r = 4 * (p + k)
                low4[r : r + 4, :] = x[0:4]
                high4[r : r + 4, :] = y[12:16]
                fold4[r : r + 4, :] = sign * turned(y[8:16])[0:4]
        south.tracers(k, low[2][0:8], low[3][0:8])
        north.tracers(k, high[2][8:16], high[3][8:16])
        for n, (x, y) in enumerate(((low[2], high[2]), (low[3], high[3]), (wl, wh))):
            r = 20 * n + 2 * k
            low2[r : r + 2, :] = x[0:2]
            high2[r : r + 2, :] = y[14:16]
            fold2[r : r + 2, :] = turned(y[8:16])[0:2]
    for n in range(4):
        down, up = flat[n, 0:8, :], flat[n, ROWS - 8 : ROWS, :]
        south.flat(n, down)
        north.flat(n, up)
        send(AT_FLAT + 8 * n, down, up, (-1.0 if n in (1, 2) else 1.0) * turned(up))
    for r in range(0, AT_PAIR, 8):
        send(r, low4[r : r + 8, :], high4[r : r + 8, :], fold4[r : r + 8, :])
    for r in range(0, 64, 8):
        send(AT_PAIR + r, low2[r : r + 8, :], high2[r : r + 8, :], fold2[r : r + 8, :])
    none = [None] * 4
    down = own_tile(lambda p, d: lo[p, 8 + d : 16 + d, :], rotation_scale * flat[3, 0:8, :], *none)
    up = own_tile(lambda p, d: hi[p, 8 + d : 16 + d, :], rotation_scale * flat[3, ROWS - 8 : ROWS, :], *none)
    for n, sign in enumerate((-1.0, -1.0, 1.0)):
        send(AT_SUM + 8 * n, down[2 + n], up[2 + n], sign * turned(up[2 + n]))
    for side, (downs, ups, others) in enumerate(((south.east, north.east, north.west), (south.west, north.west, north.east))):
        source, signs = sources[side]
        for q in range(SLABS):
            send(AT_SLAB + 32 * side + 8 * q, downs[q], ups[q], signs[q] * flip_rows(pick(others[q], source)))
    for side, (mine, other) in enumerate(((ninth.east, ninth.west), (ninth.west, ninth.east))):
        for q in range(2):
            r = 2 * side + q
            low1[r : r + 1, :] = mine[q][0:1]
            high1[r : r + 1, :] = mine[q][1:2]
            fold1[r : r + 1, :] = -pick(other[q], sources[side][0])[1:2]
    send(AT_NINE, low1[...], high1[...], fold1[...])


def level_sums(mats):
    i = lax.broadcasted_iota(jnp.int32, (COLS, COLS), 0)
    j = lax.broadcasted_iota(jnp.int32, (COLS, COLS), 1)
    for side, offset in enumerate((0, 7)):
        def place(x):
            y = (x + offset) & (COLS - 1)
            return jnp.where(y < STRIDE * LEVELS, y % STRIDE, -1), y // STRIDE

        def above(src, dst):
            same = (src[0] == dst[0]) & (src[0] >= 0)
            return jnp.where(same & (src[1] < dst[1]), 1.0, jnp.where(same & (src[1] == dst[1]), 0.5, 0.0))

        src = place(i)
        mats[2 * side] = above(src, place(j))
        mats[2 * side + 1] = above(src, place(j + 1)) - above(src, place(j - 1))
        target = j + 2 if side == 0 else (j + 9) & (COLS - 1)
        low = 2 if side == 0 else 0
        mats[4 + side] = jnp.where((target >= low) & (target < low + 9) & (src[0] == target), 1.0, 0.0)
        if side == 0:
            mats[6] = jnp.where((src[0] == ((j + 2) & (COLS - 1))) & (((j + 2) & (COLS - 1)) < 4), 1.0, 0.0)


def dot(x, mat):
    return jnp.dot(x, mat, precision=lax.Precision.HIGHEST, preferred_element_type=F32)


def centre(u, v, t, s, w, bottom, eta, ub, vb, cor, x_ref, ec, wc, us, vs, tn, sn, sums, mats,
           u2, v2, t2, s2, w2, deep, sem):
    moves = list(zip((u, v, t, s, w, bottom), (u2, v2, t2, s2, w2, deep)))
    for n, src in enumerate((eta, ub, vb, cor)):
        moves.append((src, x_ref.at[FLAT + n]))
    copies = fetch(moves, sem)
    level_sums(mats)
    for copy in copies:
        copy.wait()
    lane = lanes()

    def pack(i, carry):
        rows = pl.ds(pl.multiple_of(8 * i, 8), 8)
        bed = deep[rows, :]
        columns = Columns(lane)
        for k in range(LEVELS):
            wet = jnp.where(k < bed, w2[k, rows, :].astype(F32), 0.0)
            uk = u2[k, rows, :] * wet
            vk = v2[k, rows, :] * wet
            tk = t2[k, rows, :] * wet
            sk = s2[k, rows, :] * wet
            dk = haline_scale * sk - thermal_scale * tk
            for p, val in ((U, uk), (V, vk), (D, dk), (WET, wet), (T, tk), (S, sk)):
                x_ref[p + k, rows, :] = val
            for q, val in enumerate((uk, vk, dk, wet)):
                columns.level(q, k, val)
            columns.tracers(k, tk, sk)
        for n in range(4):
            columns.flat(n, x_ref[FLAT + n, rows, :])
        for q in range(SLABS):
            ec[q, rows, :] = columns.east[q]
            wc[q, rows, :] = columns.west[q]
        return carry

    lax.fori_loop(0, ROWS // 8, pack, 0)

    def inner(i, carry):
        r0 = 8 * i
        rows = pl.ds(pl.multiple_of(r0, 8), 8)

        def store(ref):
            def put(k, val):
                ref[k, rows, :] = val

            return put

        got = own_tile(
            lambda p, d: x_ref[p, pl.ds(r0 + d, 8), :], rotation_scale * x_ref[FLAT + 3, rows, :],
            store(us), store(vs), store(tn), store(sn),
        )
        for n in range(5):
            sums[n, rows, :] = got[n]
        return carry

    lax.fori_loop(1, ROWS // 8 - 1, inner, 0)


def pack_rims(a_ref, b_ref, ec, wc, far_ref, near_ref):
    even, _ = lat_place()
    odd = lon_odd()
    sub = lax.broadcasted_iota(jnp.int32, (8, COLS), 0)

    def send(q, at, east, west):
        far_ref[q, at, :] = jnp.where(odd, west, east)
        near_ref[q, at, :] = jnp.where(odd, east, west)

    for q in range(SLABS):
        send(q, slice(TOP, TOP + ROWS), ec[q], wc[q])

    def both(r, n):
        a = a_ref[r : r + n, :]
        b = b_ref[r : r + n, :]
        return jnp.where(even, b, a), jnp.where(even, a, b)

    for q in range(SLABS):
        (e_lo, e_hi), (w_lo, w_hi) = (both(AT_SLAB + 32 * side + 8 * q, 8) for side in (0, 1))
        send(q, slice(8, 16), e_lo, w_lo)
        send(q, slice(TOP + ROWS, SLAB_ROWS), e_hi, w_hi)
        if q < 2:
            rows = [both(AT_NINE + 2 * side + q, 1) for side in (0, 1)]
            send(q, slice(0, 8), *(jnp.where(sub == 0, lo, hi) for lo, hi in rows))
        else:
            send(q, slice(0, 8), *[jnp.zeros((8, COLS), F32)] * 2)


def edges(x_ref, a_ref, b_ref, us, vs, tn, sn, sums, low, high):
    even, _ = lat_place()

    def both(r, n):
        a = a_ref[pl.ds(r, n), :]
        b = b_ref[pl.ds(r, n), :]
        return jnp.where(even, b, a), jnp.where(even, a, b)

    sub = lax.broadcasted_iota(jnp.int32, (8, COLS), 0)

    def place(p, carry):
        low[p, 16:32, :] = x_ref[p, 0:16, :]
        high[p, 0:16, :] = x_ref[p, ROWS - 16 : ROWS, :]
        return carry

    lax.fori_loop(0, FLAT, place, 0)

    for p in range(30):
        lo, hi = both(4 * p, 4)
        low[p, 12:16, :] = lo
        high[p, 16:20, :] = hi
    for n, p in enumerate((T, S, WET)):
        for k in range(LEVELS):
            lo, hi = both(AT_PAIR + 20 * n + 2 * k, 2)
            low[p + k, 14:16, :] = lo
            high[p + k, 16:18, :] = hi
    spin_low, spin_high = both(AT_FLAT + 24, 8)
    for n, (ref, r0, spin) in enumerate((
        (low, 16, x_ref[FLAT + 3, 0:8, :]),
        (high, 8, x_ref[FLAT + 3, ROWS - 8 : ROWS, :]),
        (low, 8, spin_low),
        (high, 16, spin_high),
    )):
        def store(out):
            def put(k, val):
                out[k, 8 * n : 8 * n + 8, :] = val

            return put

        puts = [store(out) for out in (us, vs, tn, sn)] if n < 2 else [None] * 4
        got = own_tile(lambda p, d: ref[p, r0 + d : r0 + d + 8, :], rotation_scale * spin, *puts)
        for m in range(5):
            val = got[m]
            if n >= 2 and m >= 2:
                lo, hi = both(AT_SUM + 8 * (m - 2), 8)
                val = jnp.where(sub >= 6, val, lo) if n == 2 else jnp.where(sub < 2, val, hi)
            sums[m, 8 * n : 8 * n + 8, :] = val


class Wide:
    def __init__(self, own, rim):
        self.own, self.rim = own, rim

    def with_other(self, other, op):
        if isinstance(other, Wide):
            return Wide(op(self.own, other.own), op(self.rim, other.rim))
        return Wide(op(self.own, other), op(self.rim, other))

    def __add__(self, other):
        return self.with_other(other, lambda a, b: a + b)

    def __sub__(self, other):
        return self.with_other(other, lambda a, b: a - b)

    def __mul__(self, other):
        return self.with_other(other, lambda a, b: a * b)

    __rmul__ = __mul__

    def __truediv__(self, other):
        return self.with_other(other, lambda a, b: a / b)


def slope(x):
    lane = lanes()
    east_own, east_rim = turn(x.own, -1), turn(x.rim, -1)
    west_own, west_rim = turn(x.own, 1), turn(x.rim, 1)
    last, first = lane == COLS - 1, lane == 0
    return Wide(
        jnp.where(last, east_rim, east_own) - jnp.where(first, west_rim, west_own),
        jnp.where(last, east_own, east_rim) - jnp.where(first, west_own, west_rim),
    )


def step(x_ref, a_ref, b_ref, far_mine, near_mine, far_got, near_got, us, vs, tn, sn, sums, us2, vs2, tn2, sn2, sums2, mats,
         u_out, v_out, t_out, s_out, eta_out, ub_out, vb_out,
         es, ws, own, rim, fix, total, col, fu, fv, mu, mv, tu, tv, spins, t_new, s_new, u_new, v_new, flats, sem):
    even, _ = lat_place()
    lane = lanes()
    rest = lane % STRIDE
    inside = lane < LEVELS * STRIDE
    odd = lon_odd()
    for r in range(0, SLAB_ROWS, 8):
        for q in range(SLABS):
            here = slice(r, r + 8)
            far_in, near_in = far_got[q, here, :], near_got[q, here, :]
            far_out, near_out = far_mine[q, here, :], near_mine[q, here, :]
            e_got, w_got = jnp.where(odd, far_in, near_in), jnp.where(odd, near_in, far_in)
            e_mine, w_mine = jnp.where(odd, near_out, far_out), jnp.where(odd, far_out, near_out)
            east = jnp.where((rest < 2) & inside, w_mine, e_got)
            west = jnp.where(((rest == 2) | (rest == 3)) & inside, e_mine, w_got)
            for ref, val in ((es, east), (ws, west)):
                if r == 0:
                    ref[q, 7:8, :] = val[0:1]
                    ref[q, TOP + ROWS + 8 : TOP + ROWS + 9, :] = val[1:2]
                else:
                    ref[q, here, :] = val
            if q < 2 and r > 0:
                es[SLABS + q, here, :] = turn(e_got, 2)
                ws[SLABS + q, here, :] = turn(w_got, -2)
    for n in range(4):
        a = a_ref[AT_FLAT + 8 * n : AT_FLAT + 8 * n + 8, :]
        b = b_ref[AT_FLAT + 8 * n : AT_FLAT + 8 * n + 8, :]
        own[n, 8:16, :] = jnp.where(even, b, a)
        own[n, TOP : TOP + ROWS, :] = x_ref[FLAT + n]
        own[n, TOP + ROWS : TOP + ROWS + 8, :] = jnp.where(even, a, b)
        q, second = divmod(n, 2)
        for r in range(8, 88, 8):
            at = (121, 7) if second else (112, 16)
            rim[n, r : r + 8, :] = turn(jnp.where(lane >= at[0], es[q, r : r + 8, :], ws[q, r : r + 8, :]), at[1])
    for m in range(5):
        total[m, 8:16, :] = sums2[m, 16:24, :]
        total[m, 16:24, :] = sums2[m, 0:8, :]
        total[m, 24:72, :] = sums[m, 8:56, :]
        total[m, 72:80, :] = sums2[m, 8:16, :]
        total[m, 80:88, :] = sums2[m, 24:32, :]

    short = lane
    lane = lanes(BAND)
    rest = lane % STRIDE
    inside = lane < LEVELS * STRIDE
    level_e = jnp.minimum(lane // STRIDE, LEVELS)
    level_w = jnp.minimum(((lane + 7) % COLS) // STRIDE, LEVELS)
    thick_e = jnp.where(level_e < LEVELS, (level_e + 1).astype(F32) * THICK[0], 0.0)
    thick_w = jnp.where(level_w < LEVELS, (level_w + 1).astype(F32) * THICK[0], 0.0)
    edge = (lane < 2) | (lane >= COLS - 2)
    border = (short < 2) | (short >= COLS - 2)

    def slab_tile(i, carry):
        r0 = BAND * i + 8
        here = pl.ds(pl.multiple_of(r0, 8), BAND)
        parts = []
        for ref, side, thick, ahead in ((es, 0, thick_e, 1), (ws, 1, thick_w, -1)):
            def at(q, d):
                return ref[q, pl.ds(r0 + d, BAND), :]

            def around(x, d):
                return turn(x, -d)

            if ahead > 0:
                near, pair = (rest == 2) & inside, ((rest == 2) | (rest == 3)) & inside
            else:
                near, pair = (rest == 1) & inside, (rest < 2) & inside
            wet = at(3, 0)
            u = at(0, 0)
            v = at(1, 0)
            weight = thick * at(2, 0)
            weight_ns = thick * (at(2, 1) - at(2, -1))
            pressure = dot(weight, mats[2 * side])
            pressure_slope = dot(weight, mats[2 * side + 1])
            pressure_ns = dot(weight_ns, mats[2 * side])
            smooth_u, un, us_ = smoothed(at, 0, u, around)
            smooth_v, vn, vs_ = smoothed(at, 1, v, around)
            change = pressure_scale * 0.5 * pressure_slope + viscous_scale * smooth_u
            change_ns = pressure_scale * 0.5 * pressure_ns + viscous_scale * smooth_v
            parts.append((wet * thick, -change, -change_ns, u, v, wet))

            def beyond(c, ns, extra):
                far = viscous_scale * jnp.where(pair, c, 0.0)
                close = jnp.where(near, (2.0 * viscous_scale) * (ns - 4.0 * c) + extra, 0.0)
                return -(turn(far, -2 * ahead) + turn(close, -ahead))

            push = (0.5 * pressure_scale * ahead) * pressure
            fixes = [beyond(u, un + us_, push), beyond(v, vn + vs_, 0.0)]
            carry_u = (0.5 * advect_scale * ahead) * u
            for q in (SLABS, SLABS + 1):
                c = at(q, 0)
                fixes.append(beyond(c, at(q, 1) + at(q, -1), carry_u * c))
            parts.append(fixes)
        (we, due, dve, ue, ve, wet_e), fix_e, (ww, duw, dvw, uw, vw, wet_w), fix_w = parts
        own_wet = jnp.where(rest < 2, wet_e, wet_w)
        own_thick = jnp.where(rest < 2, thick_e, thick_w)
        fixes = [own_wet * (x + y) for x, y in zip(fix_e, fix_w)]
        for n in range(4):
            fix[n, here, :] = fixes[n]

        east = jnp.concatenate([we, we * due, we * dve, we * ue, we * ve], axis=0)
        west = jnp.concatenate([ww, ww * duw, ww * dvw, ww * uw, ww * vw], axis=0)
        rims = dot(east, mats[4]) + dot(west, mats[5])
        rim_depth, rim_du, rim_dv, rim_u, rim_v = (rims[BAND * n : BAND * n + BAND] for n in range(5))
        owns = dot(jnp.concatenate([own_thick * fixes[0], own_thick * fixes[1]], axis=0), mats[6])
        spin = Wide(rotation_scale * own[3, here, :], rotation_scale * rim[3, here, :])
        column = Wide(surface_depth + total[4, here, :], surface_depth + rim_depth)
        diff_u = rim_du + spin.rim * rim_v
        diff_v = rim_dv - spin.rim * rim_u
        fix_u, fix_v = owns[0:BAND], owns[BAND : 2 * BAND]
        part = Wide(1.0 / column.own, 1.0 / column.rim)
        for ref, mean, own_sum, own_diff, rim_diff, x in (
            (fu, mu, total[0, here, :], total[2, here, :], diff_u, fix_u),
            (fv, mv, total[1, here, :], total[3, here, :], diff_v, fix_v),
        ):
            ref[0, here, :] = (own_diff + x) * part.own * (1.0 / SUBSTEPS)
            ref[1, here, :] = rim_diff * part.rim * (1.0 / SUBSTEPS)
            mean[here, :] = (own_sum + x) * part.own
        for ref, x in ((col, column), (spins, spin)):
            ref[0, here, :] = x.own
            ref[1, here, :] = x.rim
        return carry

    lax.fori_loop(0, 80 // BAND, slab_tile, 0)

    def mend(n, k, rows_fix):
        return jnp.where(border, turn(fix[n, rows_fix, :], -(STRIDE * k + 2)), 0.0)

    def tile_of(i):
        return pl.ds(pl.multiple_of(8 * i, 8), 8), pl.ds(pl.multiple_of(8 * i + TOP, 8), 8)

    def tracer_tile(rows, fixed, refs, src):
        for n, (ref, out) in enumerate(zip(refs, (t_new, s_new))):
            for k in range(LEVELS):
                out[k, rows, :] = ref[k, src, :] + mend(2 + n, k, fixed)

    def tracer_loop(i, carry):
        rows, fixed = tile_of(i)
        tracer_tile(rows, fixed, (tn, sn), rows)
        return carry

    lax.fori_loop(1, ROWS // 8 - 1, tracer_loop, 0)
    for n, i in enumerate((0, ROWS // 8 - 1)):
        tracer_tile(slice(8 * i, 8 * i + 8), slice(8 * i + TOP, 8 * i + TOP + 8), (tn2, sn2), slice(8 * n, 8 * n + 8))
    first = [pltpu.make_async_copy(src, dst, sem.at[n]) for n, (src, dst) in enumerate(((t_new, t_out), (s_new, s_out)))]
    for copy in first:
        copy.start()

    def wide(ref, at):
        return Wide(ref[0, at, :], ref[1, at, :])

    def keep(ref, at, x):
        ref[0, at, :] = x.own
        ref[1, at, :] = x.rim

    def flat(p, r):
        return Wide(own[p, r : r + 8, :], rim[p, r : r + 8, :])

    def wet_of(column):
        return Wide(jnp.where(column.own > surface_depth, 1.0, 0.0), jnp.where(column.rim > surface_depth, 1.0, 0.0))

    def substep(n, carry):
        for r in range(8, 88, 8):
            here = slice(r, r + 8)
            column = wide(col, here)
            wet = wet_of(column)
            u = flat(1, r)
            v = flat(2, r)
            spin = wide(spins, here)
            un = wet * (u - (0.5 * gravity_scale) * slope(flat(0, r)) + spin * v + wide(fu, here))
            vn = wet * (v - (0.5 * gravity_scale) * (flat(0, r + 1) - flat(0, r - 1)) - spin * u + wide(fv, here))
            for p, x in ((1, un), (2, vn)):
                own[p, here, :] = x.own
                rim[p, here, :] = x.rim
            keep(tu, here, column * un)
            keep(tv, here, column * vn)
        for r in range(8, 88, 8):
            here = slice(r, r + 8)
            wet = wet_of(wide(col, here))
            flow = slope(wide(tu, here)) + (wide(tv, slice(r + 1, r + 9)) - wide(tv, slice(r - 1, r + 7)))
            eta = wet * (flat(0, r) - (0.5 * divergence_scale) * flow)
            own[0, here, :] = eta.own
            rim[0, here, :] = eta.rim
        return carry

    lax.fori_loop(0, SUBSTEPS, substep, 0)
    second = []
    for n, dst in enumerate((eta_out, ub_out, vb_out)):
        flats[n] = own[n, TOP : TOP + ROWS, :]
        second.append(pltpu.make_async_copy(flats.at[n], dst, sem.at[2 + n]))
        second[-1].start()

    def flow_tile(rows, fixed, refs, src):
        gain = (own[1, fixed, :] - mu[fixed, :], own[2, fixed, :] - mv[fixed, :])
        for k in range(LEVELS):
            wet = x_ref[WET + k, rows, :]
            for n, (ref, out) in enumerate(zip(refs, (u_new, v_new))):
                out[k, rows, :] = ref[k, src, :] + mend(n, k, fixed) + wet * gain[n]

    def flow_loop(i, carry):
        rows, fixed = tile_of(i)
        flow_tile(rows, fixed, (us, vs), rows)
        return carry

    lax.fori_loop(1, ROWS // 8 - 1, flow_loop, 0)
    for n, i in enumerate((0, ROWS // 8 - 1)):
        flow_tile(slice(8 * i, 8 * i + 8), slice(8 * i + TOP, 8 * i + TOP + 8), (us2, vs2), slice(8 * n, 8 * n + 8))
    last = [pltpu.make_async_copy(src, dst, sem.at[5 + n]) for n, (src, dst) in enumerate(((u_new, u_out), (v_new, v_out)))]
    for copy in last:
        copy.start()
    for copy in first + second + last:
        copy.wait()


def colour(parity, lats, lons):
    pairs = []
    for lat in range(lats):
        for lon in range(lons):
            if (lat + parity) % 2 == 0:
                to = (lon, lat + 1) if lat + 1 < lats else (lons - 1 - lon, lat)
            elif lat > 0:
                to = (lon, lat - 1)
            else:
                continue
            pairs.append((lon * lats + lat, to[0] * lats + to[1]))
    return pairs


def partners(first, lons):
    pairs = []
    for west in range(first, lons + first, 2):
        east = (west + 1) % lons
        pairs += [(west % lons, east), (east, west % lons)]
    return pairs


def local(u, v, t, s, w, bottom, eta, ub, vb, cor):
    lats = lax.axis_size("lat")
    lons = lax.axis_size("lon")
    raw = tuple(pltpu.with_memory_space_constraint(z, pltpu.HBM) for z in (u, v, t, s, w, bottom, eta, ub, vb, cor))
    vmem = pltpu.VMEM
    dma = pltpu.SemaphoreType.DMA
    two = (2, LEVELS, 16, COLS)
    a, b = call(
        pack_rows, [(ROW_SLAB, COLS)] * 2,
        [vmem(two, F32)] * 4 + [vmem(two, jnp.int32), vmem((4, ROWS, COLS), F32), vmem(PLANE, jnp.int32)]
        + [vmem((40, 24, COLS), F32)] * 2 + [vmem((AT_PAIR, COLS), F32)] * 3 + [vmem((64, COLS), F32)] * 3
        + [vmem((8, COLS), F32)] * 3 + [dma((15,))],
        1_000_000, *raw, ins=[HBM] * 10,
    )
    b = lax.ppermute(b, ("lon", "lat"), colour(1, lats, lons))
    a = lax.ppermute(a, ("lon", "lat"), colour(0, lats, lons))
    x, ec, wc, us, vs, tn, sn, sums, mats = call(
        centre, [(PLANES, ROWS, COLS)] + [(SLABS, ROWS, COLS)] * 2 + [CUBE] * 4 + [(5, ROWS, COLS), (7, COLS, COLS)],
        [vmem(CUBE, F32)] * 4 + [vmem(CUBE, jnp.int32), vmem(PLANE, jnp.int32), dma((10,))],
        20_000_000, *raw, ins=[HBM] * 10,
    )
    far, near = call(pack_rims, [(SLABS, SLAB_ROWS, COLS)] * 2, [], 1_000_000, a, b, ec, wc)
    far_got = lax.ppermute(far, "lon", partners(1, lons))
    near_got = lax.ppermute(near, "lon", partners(0, lons))
    window = vmem((FLAT, 32, COLS), F32)
    us2, vs2, tn2, sn2, sums2 = call(
        edges, [(LEVELS, 16, COLS)] * 4 + [(5, 32, COLS)], [window] * 2, 10_000_000, x, a, b,
    )
    wide = vmem((2, HIGH, COLS), F32)
    thin = vmem((HIGH, COLS), F32)
    slab = vmem((SLABS + 2, HIGH, COLS), F32)
    four = vmem((4, HIGH, COLS), F32)
    return tuple(
        call(
            step, [CUBE] * 4 + [PLANE] * 3,
            [slab] * 2 + [four] * 3 + [vmem((5, HIGH, COLS), F32)] + [wide] * 3 + [thin] * 2 + [wide] * 3
            + [vmem(CUBE, F32)] * 4 + [vmem((3, ROWS, COLS), F32), dma((7,))],
            50_000_000, x, a, b, far, near, far_got, near_got, us, vs, tn, sn, sums, us2, vs2, tn2, sn2, sums2, mats,
            outs=[HBM] * 7,
        )
    )


def solution(mesh):
    deep = P(None, "lat", "lon")
    flat = P("lat", "lon")
    return jax.shard_map(
        local,
        mesh=mesh,
        in_specs=(deep,) * 5 + (flat,) * 5,
        out_specs=(deep,) * 4 + (flat,) * 3,
        check_vma=False,
    )
```

```python
import jax
import jax.numpy as jnp
from jax import lax
from jax.experimental import pallas as pl
from jax.experimental.pallas import tpu as pltpu
from jax.sharding import PartitionSpec as P


SUBSTEPS = 4
LEVELS = 10
ROWS = 64
COLS = 128
U, V, D, WET, T, S, FLAT = 0, 10, 20, 30, 40, 50, 60
PLANES = 64
AT_THREE = 80
AT_PAIR = AT_THREE + 30
AT_FLAT = AT_PAIR + 60
AT_SUM = AT_FLAT + 29
AT_SLAB = AT_SUM + 15
AT_NINE = AT_SLAB + 64
ROW_SLAB = AT_NINE + 10
FLAT_ROWS = ((0, 8), (8, 7), (15, 7), (22, 7))
STRIDE = 11
SLABS = 4
TALL = 80
COLUMN_SLAB = SLABS * TALL + 8
TOP = 16
HIGH = 96
BAND = 80

advect_scale = 0.25
viscous_scale = 0.02
pressure_scale = 0.5
rotation_scale = 0.3
thermal_scale = 0.2
haline_scale = 0.8
surface_depth = 0.25
gravity_scale = 0.3
divergence_scale = 0.3

F32 = jnp.float32
THICK = [(k + 1.0) * (2.0 / (LEVELS * (LEVELS + 1))) for k in range(LEVELS)]
HBM = pl.BlockSpec(memory_space=pltpu.HBM)
VMEM = pl.BlockSpec(memory_space=pltpu.VMEM)
CUBE = (LEVELS, ROWS, COLS)
PLANE = (ROWS, COLS)


def call(kernel, out, scratch, flops, *args, ins=None, outs=None):
    return pl.pallas_call(
        kernel,
        out_shape=[jax.ShapeDtypeStruct(s, F32) for s in out],
        in_specs=ins or [VMEM] * len(args),
        out_specs=outs or [VMEM] * len(out),
        scratch_shapes=scratch,
        cost_estimate=pl.CostEstimate(flops=flops, bytes_accessed=2_000_000, transcendentals=0),
        compiler_params=pltpu.CompilerParams(vmem_limit_bytes=LIMIT),
    )(*args)


LIMIT = 40 * 1024 * 1024


def lanes(rows=8):
    return lax.broadcasted_iota(jnp.int32, (rows, COLS), 1)


def flip_lanes(x):
    return jnp.take_along_axis(x, COLS - 1 - lax.broadcasted_iota(jnp.int32, x.shape, 1), axis=1, mode="promise_in_bounds")


def flip_rows(x):
    return jnp.take_along_axis(x, 7 - lax.broadcasted_iota(jnp.int32, x.shape, 0), axis=0, mode="promise_in_bounds")


def turn(x, shift):
    return pltpu.roll(x, shift % COLS, 1)


def lat_place():
    index = lax.axis_index("lat")
    return index % 2 == 0, index == lax.axis_size("lat") - 1


def lon_odd():
    return lax.axis_index("lon") % 2 == 1


def fetch(pairs, sem):
    copies = [pltpu.make_async_copy(src, dst, sem.at[n]) for n, (src, dst) in enumerate(pairs)]
    for copy in copies:
        copy.start()
    return copies


class Columns:
    def __init__(self, lane):
        self.lane = lane
        zero = jnp.zeros((8, COLS), F32)
        self.east = [zero] * SLABS
        self.west = [zero] * SLABS

    def put_east(self, q, moved, at, count):
        lane = self.lane
        self.east[q] = jnp.where((lane >= at) & (lane < at + count), moved, self.east[q])

    def put_west(self, q, moved, end, count):
        lane = self.lane
        low = (end - count) % COLS
        here = (lane >= low) & (lane < end) if low < end else (lane >= low) | (lane < end)
        self.west[q] = jnp.where(here, moved, self.west[q])

    def put(self, q, val, shift, count):
        moved = turn(val, shift)
        self.put_east(q, moved, shift, count)
        self.put_west(q, moved, shift, count)

    def level(self, q, k, val):
        self.put(q, val, STRIDE * k + 2, 9)

    def tracers(self, k, t, s):
        for q, val in enumerate((t, s)):
            self.put_east(q, turn(val, STRIDE * k), STRIDE * k, 2)
            self.put_west(q, turn(val, STRIDE * k + 4), STRIDE * k + 4, 2)

    def flat(self, n, val):
        if n % 2 == 0:
            self.put(n // 2, val, 112, 9)
        else:
            self.put(n // 2, val, 121, 7)


def shifted(x, d):
    lane = lanes()
    keep = lane < COLS - d if d > 0 else lane >= -d
    return jnp.where(keep, turn(x, -d), 0.0)


def smoothed(at, p, c, shift):
    north, south = at(p, 1), at(p, -1)
    q = (north + south) - 4.0 * c
    both = shift(c, 2) + shift(c, -2) + (at(p, 2) + at(p, -2))
    return both + 2.0 * ((shift(q, 1) + shift(q, -1)) - 4.0 * q) - 12.0 * c, north, south


def own_tile(at, spin, put_u, put_v, put_t, put_s):
    zero = jnp.zeros((8, COLS), F32)
    acc = acc_ns = sum_u = sum_v = old_u = old_v = depth = zero
    for k in range(LEVELS):
        wet = at(WET + k, 0)
        u = at(U + k, 0)
        v = at(V + k, 0)
        smooth_u, _, _ = smoothed(at, U + k, u, shifted)
        smooth_v, v_north, v_south = smoothed(at, V + k, v, shifted)
        half = (0.5 * THICK[k]) * at(D + k, 0)
        half_ns = (0.5 * THICK[k]) * (at(D + k, 1) - at(D + k, -1))
        pressure = acc + half
        pressure_ns = acc_ns + half_ns
        acc = pressure + half
        acc_ns = pressure_ns + half_ns
        slope = shifted(pressure, 1) - shifted(pressure, -1)
        u_star = wet * (u + spin * v - (0.5 * pressure_scale) * slope - viscous_scale * smooth_u)
        v_star = wet * (v - spin * u - (0.5 * pressure_scale) * pressure_ns - viscous_scale * smooth_v)
        sum_u = sum_u + THICK[k] * u_star
        sum_v = sum_v + THICK[k] * v_star
        old_u = old_u + THICK[k] * u
        old_v = old_v + THICK[k] * v
        depth = depth + THICK[k] * wet
        if put_u is None:
            continue
        put_u(k, u_star)
        put_v(k, v_star)
        for p, put in ((T + k, put_t), (S + k, put_s)):
            c = at(p, 0)
            smooth, north, south = smoothed(at, p, c, shifted)
            flux = u * c
            advect = (shifted(flux, 1) - shifted(flux, -1)) + (v_north * north - v_south * south)
            put(k, wet * (c - (0.5 * advect_scale) * advect - viscous_scale * smooth))
    return sum_u, sum_v, sum_u - old_u, sum_v - old_v, depth


def mirrored_lanes(side):
    lane = lanes()
    offset = 7 * side
    y = (lane + offset) & (COLS - 1)
    level = y // STRIDE
    col = y % STRIDE
    group = y < STRIDE * LEVELS
    second = lane >= (121 if side == 0 else 112)
    source = jnp.where(group, 2 * STRIDE * level + 3 - lane, jnp.where(second, 241 - lane, 223 - lane)) & (COLS - 1)
    tracer = (col < 2) if side == 0 else (col >= STRIDE - 2)
    with_u = jnp.where(group, jnp.where(tracer, 1.0, -1.0), jnp.where(second, -1.0, 1.0))
    with_v = jnp.where(group, jnp.where(tracer, 1.0, -1.0), jnp.where(second, 1.0, -1.0))
    return source, (with_u, with_v, 1.0, 1.0)


def pick(x, source):
    return jnp.take_along_axis(x, source, axis=1, mode="promise_in_bounds")


def pack_rows(u, v, t, s, w, bottom, eta, ub, vb, cor, a_ref, b_ref,
              u2, v2, t2, s2, w2, flat, deep, lo, hi, downs_ref, ups_ref, folds_ref, sem):
    even, top = lat_place()
    lane = lanes()
    sub = lax.broadcasted_iota(jnp.int32, (8, COLS), 0)
    moves = []
    for src, dst in ((u, u2), (v, v2), (t, t2), (s, s2), (w, w2)):
        moves.append((src.at[:, 0:16, :], dst.at[0]))
        moves.append((src.at[:, ROWS - 16 : ROWS, :], dst.at[1]))
    for n, src in enumerate((eta, ub, vb, cor)):
        moves.append((src, flat.at[n]))
    moves.append((bottom, deep))
    copies = fetch(moves, sem)
    sources = [mirrored_lanes(side) for side in (0, 1)]
    for copy in copies:
        copy.wait()
    for ref in (downs_ref, ups_ref, folds_ref):
        ref[ROW_SLAB - 8 : ROW_SLAB, :] = jnp.zeros((8, COLS), F32)
    d0 = deep[0:16, :]
    d1 = deep[ROWS - 16 : ROWS, :]
    south, north, ninth = Columns(lane), Columns(lane), Columns(lane)

    def lay(r, down, up, fold):
        for ref, val in ((downs_ref, down), (ups_ref, up), (folds_ref, fold)):
            ref[r : r + val.shape[0], :] = val

    def turned(x):
        return flip_rows(flip_lanes(x))

    for k in range(LEVELS):
        wl = jnp.where(k < d0, w2[0, k].astype(F32), 0.0)
        wh = jnp.where(k < d1, w2[1, k].astype(F32), 0.0)
        low = [ref[0, k] * wl for ref in (u2, v2, t2, s2)]
        high = [ref[1, k] * wh for ref in (u2, v2, t2, s2)]
        low_d = haline_scale * low[3] - thermal_scale * low[2]
        high_d = haline_scale * high[3] - thermal_scale * high[2]
        for p, q, sign, x, y in (
            (U, 0, -1.0, low[0], high[0]), (V, 1, -1.0, low[1], high[1]), (D, 2, 1.0, low_d, high_d), (WET, 3, 1.0, wl, wh),
        ):
            lo[p + k, 8:24, :] = x
            hi[p + k, 0:16, :] = y
            south.level(q, k, x[0:8])
            north.level(q, k, y[8:16])
            if q < 2:
                ninth.level(q, k, jnp.where(sub == 0, x[8:9], y[7:8]))
            if q < 2:
                lay(4 * (p + k), x[0:4], y[12:16], sign * turned(y[8:16])[0:4])
            elif q == 2:
                lay(AT_THREE + 3 * k, x[0:3], y[13:16], turned(y[8:16])[0:3])
        south.tracers(k, low[2][0:8], low[3][0:8])
        north.tracers(k, high[2][8:16], high[3][8:16])
        for n, (x, y) in enumerate(((low[2], high[2]), (low[3], high[3]), (wl, wh))):
            lay(AT_PAIR + 20 * n + 2 * k, x[0:2], y[14:16], turned(y[8:16])[0:2])
    for n, (at, count) in enumerate(FLAT_ROWS):
        down, up = flat[n, 0:8, :], flat[n, ROWS - 8 : ROWS, :]
        south.flat(n, down)
        north.flat(n, up)
        mirrored = (-1.0 if n in (1, 2) else 1.0) * turned(up)
        lay(AT_FLAT + at, down[0:count], up[8 - count : 8], mirrored[0:count])
    none = [None] * 4
    down = own_tile(lambda p, d: lo[p, 8 + d : 16 + d, :], rotation_scale * flat[3, 0:8, :], *none)
    up = own_tile(lambda p, d: hi[p, 8 + d : 16 + d, :], rotation_scale * flat[3, ROWS - 8 : ROWS, :], *none)
    for n, sign in enumerate((-1.0, -1.0, 1.0)):
        lay(AT_SUM + 5 * n, down[2 + n][2:7], up[2 + n][1:6], sign * turned(up[2 + n])[2:7])
    for side, (downs, ups, others) in enumerate(((south.east, north.east, north.west), (south.west, north.west, north.east))):
        source, signs = sources[side]
        for q in range(SLABS):
            lay(AT_SLAB + 32 * side + 8 * q, downs[q], ups[q], signs[q] * flip_rows(pick(others[q], source)))
    for side, (mine, other) in enumerate(((ninth.east, ninth.west), (ninth.west, ninth.east))):
        for q in range(2):
            lay(AT_NINE + 2 * side + q, mine[q][0:1], mine[q][1:2], -pick(other[q], sources[side][0])[1:2])
    for r in range(0, ROW_SLAB, 8):
        here = slice(r, r + 8)
        down, up = downs_ref[here, :], ups_ref[here, :]
        a_ref[here, :] = jnp.where(even, up, down)
        b_ref[here, :] = jnp.where(even, down, jnp.where(top, folds_ref[here, :], up))


def level_sums(mats):
    i = lax.broadcasted_iota(jnp.int32, (COLS, COLS), 0)
    j = lax.broadcasted_iota(jnp.int32, (COLS, COLS), 1)
    for side, offset in enumerate((0, 7)):
        def place(x):
            y = (x + offset) & (COLS - 1)
            return jnp.where(y < STRIDE * LEVELS, y % STRIDE, -1), y // STRIDE

        def above(src, dst):
            same = (src[0] == dst[0]) & (src[0] >= 0)
            return jnp.where(same & (src[1] < dst[1]), 1.0, jnp.where(same & (src[1] == dst[1]), 0.5, 0.0))

        src = place(i)
        mats[2 * side] = above(src, place(j))
        mats[2 * side + 1] = above(src, place(j + 1)) - above(src, place(j - 1))
        target = j + 2 if side == 0 else (j + 9) & (COLS - 1)
        low = 2 if side == 0 else 0
        mats[4 + side] = jnp.where((target >= low) & (target < low + 9) & (src[0] == target), 1.0, 0.0)
        if side == 0:
            mats[6] = jnp.where((src[0] == ((j + 2) & (COLS - 1))) & (((j + 2) & (COLS - 1)) < 4), 1.0, 0.0)


def dot(x, mat):
    return jnp.dot(x, mat, precision=lax.Precision.HIGHEST, preferred_element_type=F32)


def centre(u, v, t, s, w, bottom, eta, ub, vb, cor, x_ref, ec, wc, us, vs, tn, sn, sums, mats,
           u2, v2, t2, s2, w2, deep, sem):
    moves = list(zip((u, v, t, s, w, bottom), (u2, v2, t2, s2, w2, deep)))
    for n, src in enumerate((eta, ub, vb, cor)):
        moves.append((src, x_ref.at[FLAT + n]))
    copies = fetch(moves, sem)
    level_sums(mats)
    for copy in copies:
        copy.wait()
    lane = lanes()

    def pack(i, carry):
        rows = pl.ds(pl.multiple_of(8 * i, 8), 8)
        bed = deep[rows, :]
        columns = Columns(lane)
        for k in range(LEVELS):
            wet = jnp.where(k < bed, w2[k, rows, :].astype(F32), 0.0)
            uk = u2[k, rows, :] * wet
            vk = v2[k, rows, :] * wet
            tk = t2[k, rows, :] * wet
            sk = s2[k, rows, :] * wet
            dk = haline_scale * sk - thermal_scale * tk
            for p, val in ((U, uk), (V, vk), (D, dk), (WET, wet), (T, tk), (S, sk)):
                x_ref[p + k, rows, :] = val
            for q, val in enumerate((uk, vk, dk, wet)):
                columns.level(q, k, val)
            columns.tracers(k, tk, sk)
        for n in range(4):
            columns.flat(n, x_ref[FLAT + n, rows, :])
        for q in range(SLABS):
            ec[q, rows, :] = columns.east[q]
            wc[q, rows, :] = columns.west[q]
        return carry

    lax.fori_loop(0, ROWS // 8, pack, 0)

    def inner(i, carry):
        r0 = 8 * i
        rows = pl.ds(pl.multiple_of(r0, 8), 8)

        def store(ref):
            def put(k, val):
                ref[k, rows, :] = val

            return put

        got = own_tile(
            lambda p, d: x_ref[p, pl.ds(r0 + d, 8), :], rotation_scale * x_ref[FLAT + 3, rows, :],
            store(us), store(vs), store(tn), store(sn),
        )
        for n in range(5):
            sums[n, rows, :] = got[n]
        return carry

    lax.fori_loop(1, ROWS // 8 - 1, inner, 0)


def pack_rims(a_ref, b_ref, ec, wc, far_ref, near_ref):
    even, _ = lat_place()
    odd = lon_odd()

    def send(at, east, west):
        here = slice(at, at + east.shape[0])
        far_ref[here, :] = jnp.where(odd, west, east)
        near_ref[here, :] = jnp.where(odd, east, west)

    for q in range(SLABS):
        send(TALL * q + 8, ec[q], wc[q])

    def both(r, n):
        a = a_ref[r : r + n, :]
        b = b_ref[r : r + n, :]
        return jnp.where(even, b, a), jnp.where(even, a, b)

    for q in range(SLABS):
        (e_lo, e_hi), (w_lo, w_hi) = (both(AT_SLAB + 32 * side + 8 * q, 8) for side in (0, 1))
        send(TALL * q, e_lo, w_lo)
        send(TALL * q + 8 + ROWS, e_hi, w_hi)
    for q in range(2):
        pairs = [both(AT_NINE + 2 * side + q, 1) for side in (0, 1)]
        for n in (0, 1):
            send(SLABS * TALL + 2 * q + n, pairs[0][n], pairs[1][n])
    send(SLABS * TALL + 4, *[jnp.zeros((4, COLS), F32)] * 2)


def edges(x_ref, a_ref, b_ref, us, vs, tn, sn, sums, low, high):
    even, _ = lat_place()

    def both(r, n):
        a = a_ref[pl.ds(r, n), :]
        b = b_ref[pl.ds(r, n), :]
        return jnp.where(even, b, a), jnp.where(even, a, b)

    def place(p, carry):
        low[p, 16:32, :] = x_ref[p, 0:16, :]
        high[p, 0:16, :] = x_ref[p, ROWS - 16 : ROWS, :]
        return carry

    lax.fori_loop(0, FLAT, place, 0)

    for p in range(20):
        lo, hi = both(4 * p, 4)
        low[p, 12:16, :] = lo
        high[p, 16:20, :] = hi
    for k in range(LEVELS):
        lo, hi = both(AT_THREE + 3 * k, 3)
        low[D + k, 13:16, :] = lo
        high[D + k, 16:19, :] = hi
    for n, p in enumerate((T, S, WET)):
        for k in range(LEVELS):
            lo, hi = both(AT_PAIR + 20 * n + 2 * k, 2)
            low[p + k, 14:16, :] = lo
            high[p + k, 16:18, :] = hi
    lo, hi = both(AT_FLAT + FLAT_ROWS[3][0], 7)
    low[FLAT, 9:16, :] = lo
    high[FLAT, 16:23, :] = hi
    for n, (ref, r0, spin) in enumerate((
        (low, 16, x_ref[FLAT + 3, 0:8, :]),
        (high, 8, x_ref[FLAT + 3, ROWS - 8 : ROWS, :]),
        (low, 8, low[FLAT, 8:16, :]),
        (high, 16, high[FLAT, 16:24, :]),
    )):
        def store(out):
            def put(k, val):
                out[k, 8 * n : 8 * n + 8, :] = val

            return put

        puts = [store(out) for out in (us, vs, tn, sn)] if n < 2 else [None] * 4
        got = own_tile(lambda p, d: ref[p, r0 + d : r0 + d + 8, :], rotation_scale * spin, *puts)
        for m in range(5):
            at = 8 * n
            sums[m, at : at + 8, :] = got[m]
            if n >= 2 and m >= 2:
                lo, hi = both(AT_SUM + 5 * (m - 2), 5)
                first = at + 1 if n == 2 else at + 2
                sums[m, first : first + 5, :] = lo if n == 2 else hi


class Wide:
    def __init__(self, own, rim):
        self.own, self.rim = own, rim

    def with_other(self, other, op):
        if isinstance(other, Wide):
            return Wide(op(self.own, other.own), op(self.rim, other.rim))
        return Wide(op(self.own, other), op(self.rim, other))

    def __add__(self, other):
        return self.with_other(other, lambda a, b: a + b)

    def __sub__(self, other):
        return self.with_other(other, lambda a, b: a - b)

    def __mul__(self, other):
        return self.with_other(other, lambda a, b: a * b)

    __rmul__ = __mul__

    def __truediv__(self, other):
        return self.with_other(other, lambda a, b: a / b)


def slope(x):
    lane = lanes()
    east_own, east_rim = turn(x.own, -1), turn(x.rim, -1)
    west_own, west_rim = turn(x.own, 1), turn(x.rim, 1)
    last, first = lane == COLS - 1, lane == 0
    return Wide(
        jnp.where(last, east_rim, east_own) - jnp.where(first, west_rim, west_own),
        jnp.where(last, east_own, east_rim) - jnp.where(first, west_own, west_rim),
    )


def step(x_ref, a_ref, b_ref, far_mine, near_mine, far_got, near_got, us, vs, tn, sn, sums, us2, vs2, tn2, sn2, sums2, mats,
         u_out, v_out, t_out, s_out, eta_out, ub_out, vb_out,
         es, ws, own, rim, fix, total, col, fu, fv, mu, mv, tu, tv, spins, t_new, s_new, u_new, v_new, flats, sem):
    even, _ = lat_place()
    lane = lanes()
    rest = lane % STRIDE
    inside = lane < LEVELS * STRIDE
    odd = lon_odd()
    for q, r, count in [(q, r, 8) for r in range(8, 88, 8) for q in range(SLABS)] + [(0, 0, 2), (1, 0, 2)]:
        at = TALL * q + r - 8 if r else SLABS * TALL + 2 * q
        got = slice(at, at + count)
        far_in, near_in = far_got[got, :], near_got[got, :]
        far_out, near_out = far_mine[got, :], near_mine[got, :]
        e_got, w_got = jnp.where(odd, far_in, near_in), jnp.where(odd, near_in, far_in)
        e_mine, w_mine = jnp.where(odd, near_out, far_out), jnp.where(odd, far_out, near_out)
        own_e, own_w = (m[0:count] for m in ((rest < 2) & inside, ((rest == 2) | (rest == 3)) & inside))
        for ref, val in ((es, jnp.where(own_e, w_mine, e_got)), (ws, jnp.where(own_w, e_mine, w_got))):
            if r:
                ref[q, r : r + 8, :] = val
            else:
                ref[q, 7:8, :] = val[0:1]
                ref[q, TOP + ROWS + 8 : TOP + ROWS + 9, :] = val[1:2]
        if q < 2 and r:
            es[SLABS + q, r : r + 8, :] = turn(e_got, 2)
            ws[SLABS + q, r : r + 8, :] = turn(w_got, -2)
    for n in range(4):
        at, count = FLAT_ROWS[n]
        a = a_ref[AT_FLAT + at : AT_FLAT + at + count, :]
        b = b_ref[AT_FLAT + at : AT_FLAT + at + count, :]
        own[n, TOP - count : TOP, :] = jnp.where(even, b, a)
        own[n, TOP : TOP + ROWS, :] = x_ref[FLAT + n]
        own[n, TOP + ROWS : TOP + ROWS + count, :] = jnp.where(even, a, b)
        q, second = divmod(n, 2)
        for r in range(8, 88, 8):
            at = (121, 7) if second else (112, 16)
            rim[n, r : r + 8, :] = turn(jnp.where(lane >= at[0], es[q, r : r + 8, :], ws[q, r : r + 8, :]), at[1])
    for m in range(5):
        total[m, 8:16, :] = sums2[m, 16:24, :]
        total[m, 16:24, :] = sums2[m, 0:8, :]
        total[m, 24:72, :] = sums[m, 8:56, :]
        total[m, 72:80, :] = sums2[m, 8:16, :]
        total[m, 80:88, :] = sums2[m, 24:32, :]

    short = lane
    lane = lanes(BAND)
    rest = lane % STRIDE
    inside = lane < LEVELS * STRIDE
    level_e = jnp.minimum(lane // STRIDE, LEVELS)
    level_w = jnp.minimum(((lane + 7) % COLS) // STRIDE, LEVELS)
    thick_e = jnp.where(level_e < LEVELS, (level_e + 1).astype(F32) * THICK[0], 0.0)
    thick_w = jnp.where(level_w < LEVELS, (level_w + 1).astype(F32) * THICK[0], 0.0)
    edge = (lane < 2) | (lane >= COLS - 2)
    border = (short < 2) | (short >= COLS - 2)

    def slab_tile(i, carry):
        r0 = BAND * i + 8
        here = pl.ds(pl.multiple_of(r0, 8), BAND)
        parts = []
        for ref, side, thick, ahead in ((es, 0, thick_e, 1), (ws, 1, thick_w, -1)):
            def at(q, d):
                return ref[q, pl.ds(r0 + d, BAND), :]

            def around(x, d):
                return turn(x, -d)

            if ahead > 0:
                near, pair = (rest == 2) & inside, ((rest == 2) | (rest == 3)) & inside
            else:
                near, pair = (rest == 1) & inside, (rest < 2) & inside
            wet = at(3, 0)
            u = at(0, 0)
            v = at(1, 0)
            weight = thick * at(2, 0)
            weight_ns = thick * (at(2, 1) - at(2, -1))
            pressure = dot(weight, mats[2 * side])
            pressure_slope = dot(weight, mats[2 * side + 1])
            pressure_ns = dot(weight_ns, mats[2 * side])
            smooth_u, un, us_ = smoothed(at, 0, u, around)
            smooth_v, vn, vs_ = smoothed(at, 1, v, around)
            change = pressure_scale * 0.5 * pressure_slope + viscous_scale * smooth_u
            change_ns = pressure_scale * 0.5 * pressure_ns + viscous_scale * smooth_v
            parts.append((wet * thick, -change, -change_ns, u, v, wet))

            def beyond(c, ns, extra):
                far = viscous_scale * jnp.where(pair, c, 0.0)
                close = jnp.where(near, (2.0 * viscous_scale) * (ns - 4.0 * c) + extra, 0.0)
                return -(turn(far, -2 * ahead) + turn(close, -ahead))

            push = (0.5 * pressure_scale * ahead) * pressure
            fixes = [beyond(u, un + us_, push), beyond(v, vn + vs_, 0.0)]
            carry_u = (0.5 * advect_scale * ahead) * u
            for q in (SLABS, SLABS + 1):
                c = at(q, 0)
                fixes.append(beyond(c, at(q, 1) + at(q, -1), carry_u * c))
            parts.append(fixes)
        (we, due, dve, ue, ve, wet_e), fix_e, (ww, duw, dvw, uw, vw, wet_w), fix_w = parts
        own_wet = jnp.where(rest < 2, wet_e, wet_w)
        own_thick = jnp.where(rest < 2, thick_e, thick_w)
        fixes = [own_wet * (x + y) for x, y in zip(fix_e, fix_w)]
        for n in range(4):
            fix[n, here, :] = fixes[n]

        east = jnp.concatenate([we, we * due, we * dve, we * ue, we * ve], axis=0)
        west = jnp.concatenate([ww, ww * duw, ww * dvw, ww * uw, ww * vw], axis=0)
        rims = dot(east, mats[4]) + dot(west, mats[5])
        rim_depth, rim_du, rim_dv, rim_u, rim_v = (rims[BAND * n : BAND * n + BAND] for n in range(5))
        owns = dot(jnp.concatenate([own_thick * fixes[0], own_thick * fixes[1]], axis=0), mats[6])
        spin = Wide(rotation_scale * own[3, here, :], rotation_scale * rim[3, here, :])
        column = Wide(surface_depth + total[4, here, :], surface_depth + rim_depth)
        diff_u = rim_du + spin.rim * rim_v
        diff_v = rim_dv - spin.rim * rim_u
        fix_u, fix_v = owns[0:BAND], owns[BAND : 2 * BAND]
        part = Wide(1.0 / column.own, 1.0 / column.rim)
        for ref, mean, own_sum, own_diff, rim_diff, x in (
            (fu, mu, total[0, here, :], total[2, here, :], diff_u, fix_u),
            (fv, mv, total[1, here, :], total[3, here, :], diff_v, fix_v),
        ):
            ref[0, here, :] = (own_diff + x) * part.own * (1.0 / SUBSTEPS)
            ref[1, here, :] = rim_diff * part.rim * (1.0 / SUBSTEPS)
            mean[here, :] = (own_sum + x) * part.own
        for ref, x in ((col, column), (spins, spin)):
            ref[0, here, :] = x.own
            ref[1, here, :] = x.rim
        return carry

    lax.fori_loop(0, 80 // BAND, slab_tile, 0)

    def mend(n, k, rows_fix):
        return jnp.where(border, turn(fix[n, rows_fix, :], -(STRIDE * k + 2)), 0.0)

    def tile_of(i):
        return pl.ds(pl.multiple_of(8 * i, 8), 8), pl.ds(pl.multiple_of(8 * i + TOP, 8), 8)

    def tracer_tile(rows, fixed, refs, src):
        for n, (ref, out) in enumerate(zip(refs, (t_new, s_new))):
            for k in range(LEVELS):
                out[k, rows, :] = ref[k, src, :] + mend(2 + n, k, fixed)

    def tracer_loop(i, carry):
        rows, fixed = tile_of(i)
        tracer_tile(rows, fixed, (tn, sn), rows)
        return carry

    lax.fori_loop(1, ROWS // 8 - 1, tracer_loop, 0)
    for n, i in enumerate((0, ROWS // 8 - 1)):
        tracer_tile(slice(8 * i, 8 * i + 8), slice(8 * i + TOP, 8 * i + TOP + 8), (tn2, sn2), slice(8 * n, 8 * n + 8))
    first = [pltpu.make_async_copy(src, dst, sem.at[n]) for n, (src, dst) in enumerate(((t_new, t_out), (s_new, s_out)))]
    for copy in first:
        copy.start()

    def wide(ref, at):
        return Wide(ref[0, at, :], ref[1, at, :])

    def keep(ref, at, x):
        ref[0, at, :] = x.own
        ref[1, at, :] = x.rim

    def flat(p, r):
        return Wide(own[p, r : r + 8, :], rim[p, r : r + 8, :])

    def wet_of(column):
        return Wide(jnp.where(column.own > surface_depth, 1.0, 0.0), jnp.where(column.rim > surface_depth, 1.0, 0.0))

    def substep(n, carry):
        for r in range(8, 88, 8):
            here = slice(r, r + 8)
            column = wide(col, here)
            wet = wet_of(column)
            u = flat(1, r)
            v = flat(2, r)
            spin = wide(spins, here)
            un = wet * (u - (0.5 * gravity_scale) * slope(flat(0, r)) + spin * v + wide(fu, here))
            vn = wet * (v - (0.5 * gravity_scale) * (flat(0, r + 1) - flat(0, r - 1)) - spin * u + wide(fv, here))
            for p, x in ((1, un), (2, vn)):
                own[p, here, :] = x.own
                rim[p, here, :] = x.rim
            keep(tu, here, column * un)
            keep(tv, here, column * vn)
        for r in range(8, 88, 8):
            here = slice(r, r + 8)
            wet = wet_of(wide(col, here))
            flow = slope(wide(tu, here)) + (wide(tv, slice(r + 1, r + 9)) - wide(tv, slice(r - 1, r + 7)))
            eta = wet * (flat(0, r) - (0.5 * divergence_scale) * flow)
            own[0, here, :] = eta.own
            rim[0, here, :] = eta.rim
        return carry

    lax.fori_loop(0, SUBSTEPS, substep, 0)
    second = []
    for n, dst in enumerate((eta_out, ub_out, vb_out)):
        flats[n] = own[n, TOP : TOP + ROWS, :]
        second.append(pltpu.make_async_copy(flats.at[n], dst, sem.at[2 + n]))
        second[-1].start()

    def flow_tile(rows, fixed, refs, src):
        gain = (own[1, fixed, :] - mu[fixed, :], own[2, fixed, :] - mv[fixed, :])
        for k in range(LEVELS):
            wet = x_ref[WET + k, rows, :]
            for n, (ref, out) in enumerate(zip(refs, (u_new, v_new))):
                out[k, rows, :] = ref[k, src, :] + mend(n, k, fixed) + wet * gain[n]

    def flow_loop(i, carry):
        rows, fixed = tile_of(i)
        flow_tile(rows, fixed, (us, vs), rows)
        return carry

    lax.fori_loop(1, ROWS // 8 - 1, flow_loop, 0)
    for n, i in enumerate((0, ROWS // 8 - 1)):
        flow_tile(slice(8 * i, 8 * i + 8), slice(8 * i + TOP, 8 * i + TOP + 8), (us2, vs2), slice(8 * n, 8 * n + 8))
    last = [pltpu.make_async_copy(src, dst, sem.at[5 + n]) for n, (src, dst) in enumerate(((u_new, u_out), (v_new, v_out)))]
    for copy in last:
        copy.start()
    for copy in first + second + last:
        copy.wait()


def colour(parity, lats, lons):
    pairs = []
    for lat in range(lats):
        for lon in range(lons):
            if (lat + parity) % 2 == 0:
                to = (lon, lat + 1) if lat + 1 < lats else (lons - 1 - lon, lat)
            elif lat > 0:
                to = (lon, lat - 1)
            else:
                continue
            pairs.append((lon * lats + lat, to[0] * lats + to[1]))
    return pairs


def partners(first, lons):
    pairs = []
    for west in range(first, lons + first, 2):
        east = (west + 1) % lons
        pairs += [(west % lons, east), (east, west % lons)]
    return pairs


def local(u, v, t, s, w, bottom, eta, ub, vb, cor):
    lats = lax.axis_size("lat")
    lons = lax.axis_size("lon")
    raw = tuple(pltpu.with_memory_space_constraint(z, pltpu.HBM) for z in (u, v, t, s, w, bottom, eta, ub, vb, cor))
    vmem = pltpu.VMEM
    dma = pltpu.SemaphoreType.DMA
    two = (2, LEVELS, 16, COLS)
    a, b = call(
        pack_rows, [(ROW_SLAB, COLS)] * 2,
        [vmem(two, F32)] * 4 + [vmem(two, jnp.int32), vmem((4, ROWS, COLS), F32), vmem(PLANE, jnp.int32)]
        + [vmem((40, 24, COLS), F32)] * 2 + [vmem((ROW_SLAB, COLS), F32)] * 3 + [dma((15,))],
        1_000_000, *raw, ins=[HBM] * 10,
    )
    b = lax.ppermute(b, ("lon", "lat"), colour(1, lats, lons))
    a = lax.ppermute(a, ("lon", "lat"), colour(0, lats, lons))
    x, ec, wc, us, vs, tn, sn, sums, mats = call(
        centre, [(PLANES, ROWS, COLS)] + [(SLABS, ROWS, COLS)] * 2 + [CUBE] * 4 + [(5, ROWS, COLS), (7, COLS, COLS)],
        [vmem(CUBE, F32)] * 4 + [vmem(CUBE, jnp.int32), vmem(PLANE, jnp.int32), dma((10,))],
        20_000_000, *raw, ins=[HBM] * 10,
    )
    far, near = call(pack_rims, [(COLUMN_SLAB, COLS)] * 2, [], 1_000_000, a, b, ec, wc)
    far_got = lax.ppermute(far, "lon", partners(1, lons))
    near_got = lax.ppermute(near, "lon", partners(0, lons))
    window = vmem((FLAT + 1, 32, COLS), F32)
    us2, vs2, tn2, sn2, sums2 = call(
        edges, [(LEVELS, 16, COLS)] * 4 + [(5, 32, COLS)], [window] * 2, 10_000_000, x, a, b,
    )
    wide = vmem((2, HIGH, COLS), F32)
    thin = vmem((HIGH, COLS), F32)
    slab = vmem((SLABS + 2, HIGH, COLS), F32)
    four = vmem((4, HIGH, COLS), F32)
    return tuple(
        call(
            step, [CUBE] * 4 + [PLANE] * 3,
            [slab] * 2 + [four] * 3 + [vmem((5, HIGH, COLS), F32)] + [wide] * 3 + [thin] * 2 + [wide] * 3
            + [vmem(CUBE, F32)] * 4 + [vmem((3, ROWS, COLS), F32), dma((7,))],
            50_000_000, x, a, b, far, near, far_got, near_got, us, vs, tn, sn, sums, us2, vs2, tn2, sn2, sums2, mats,
            outs=[HBM] * 7,
        )
    )


def solution(mesh):
    deep = P(None, "lat", "lon")
    flat = P("lat", "lon")
    return jax.shard_map(
        local,
        mesh=mesh,
        in_specs=(deep,) * 5 + (flat,) * 5,
        out_specs=(deep,) * 4 + (flat,) * 3,
        check_vma=False,
    )
```

```python
import jax
import jax.numpy as jnp
from jax import lax
from jax.experimental import pallas as pl
from jax.experimental.pallas import tpu as pltpu
from jax.sharding import PartitionSpec as P


SUBSTEPS = 4
LEVELS = 10
ROWS = 64
COLS = 128
U, V, D, WET, T, S, FLAT = 0, 10, 20, 30, 40, 50, 60
PLANES = 64
AT_ONE = 40
AT_PAIR = AT_ONE + 10
AT_FLAT = AT_PAIR + 60
AT_SUM = AT_FLAT + 29
AT_SLAB = AT_SUM + 21
AT_NINE = AT_SLAB + 64
ROW_SLAB = AT_NINE + 8
FLAT_ROWS = ((0, 8), (8, 7), (15, 7), (22, 7))
STRIDE = 11
SLABS = 4
TALL = 80
COLUMN_SLAB = SLABS * TALL + 8
TOP = 16
HIGH = 96
BAND = 80

advect_scale = 0.25
viscous_scale = 0.02
pressure_scale = 0.5
rotation_scale = 0.3
thermal_scale = 0.2
haline_scale = 0.8
surface_depth = 0.25
gravity_scale = 0.3
divergence_scale = 0.3

F32 = jnp.float32
THICK = [(k + 1.0) * (2.0 / (LEVELS * (LEVELS + 1))) for k in range(LEVELS)]
HBM = pl.BlockSpec(memory_space=pltpu.HBM)
VMEM = pl.BlockSpec(memory_space=pltpu.VMEM)
CUBE = (LEVELS, ROWS, COLS)
PLANE = (ROWS, COLS)


def call(kernel, out, scratch, flops, *args, ins=None, outs=None):
    return pl.pallas_call(
        kernel,
        out_shape=[jax.ShapeDtypeStruct(s, F32) for s in out],
        in_specs=ins or [VMEM] * len(args),
        out_specs=outs or [VMEM] * len(out),
        scratch_shapes=scratch,
        cost_estimate=pl.CostEstimate(flops=flops, bytes_accessed=2_000_000, transcendentals=0),
        compiler_params=pltpu.CompilerParams(vmem_limit_bytes=LIMIT),
    )(*args)


LIMIT = 40 * 1024 * 1024


def lanes(rows=8):
    return lax.broadcasted_iota(jnp.int32, (rows, COLS), 1)


def flip_lanes(x):
    return jnp.take_along_axis(x, COLS - 1 - lax.broadcasted_iota(jnp.int32, x.shape, 1), axis=1, mode="promise_in_bounds")


def flip_rows(x):
    return jnp.take_along_axis(x, 7 - lax.broadcasted_iota(jnp.int32, x.shape, 0), axis=0, mode="promise_in_bounds")


def turn(x, shift):
    return pltpu.roll(x, shift % COLS, 1)


def lat_place():
    index = lax.axis_index("lat")
    return index % 2 == 0, index == lax.axis_size("lat") - 1


def lon_odd():
    return lax.axis_index("lon") % 2 == 1


def fetch(pairs, sem):
    copies = [pltpu.make_async_copy(src, dst, sem.at[n]) for n, (src, dst) in enumerate(pairs)]
    for copy in copies:
        copy.start()
    return copies


class Columns:
    def __init__(self, lane):
        self.lane = lane
        zero = jnp.zeros((8, COLS), F32)
        self.east = [zero] * SLABS
        self.west = [zero] * SLABS

    def put_east(self, q, moved, at, count):
        lane = self.lane
        self.east[q] = jnp.where((lane >= at) & (lane < at + count), moved, self.east[q])

    def put_west(self, q, moved, end, count):
        lane = self.lane
        low = (end - count) % COLS
        here = (lane >= low) & (lane < end) if low < end else (lane >= low) | (lane < end)
        self.west[q] = jnp.where(here, moved, self.west[q])

    def put(self, q, val, shift, count):
        moved = turn(val, shift)
        self.put_east(q, moved, shift, count)
        self.put_west(q, moved, shift, count)

    def level(self, q, k, val):
        self.put(q, val, STRIDE * k + 2, 9)

    def tracers(self, k, t, s):
        for q, val in enumerate((t, s)):
            self.put_east(q, turn(val, STRIDE * k), STRIDE * k, 2)
            self.put_west(q, turn(val, STRIDE * k + 4), STRIDE * k + 4, 2)

    def flat(self, n, val):
        if n % 2 == 0:
            self.put(n // 2, val, 112, 9)
        else:
            self.put(n // 2, val, 121, 7)


def shifted(x, d):
    lane = lanes()
    keep = lane < COLS - d if d > 0 else lane >= -d
    return jnp.where(keep, turn(x, -d), 0.0)


def smoothed(at, p, c, shift):
    north, south = at(p, 1), at(p, -1)
    q = (north + south) - 4.0 * c
    both = shift(c, 2) + shift(c, -2) + (at(p, 2) + at(p, -2))
    return both + 2.0 * ((shift(q, 1) + shift(q, -1)) - 4.0 * q) - 12.0 * c, north, south


def own_tile(at, spin, put_u, put_v, put_t, put_s):
    zero = jnp.zeros((8, COLS), F32)
    acc = acc_ns = sum_u = sum_v = old_u = old_v = depth = zero
    for k in range(LEVELS):
        wet = at(WET + k, 0)
        u = at(U + k, 0)
        v = at(V + k, 0)
        smooth_u, _, _ = smoothed(at, U + k, u, shifted)
        smooth_v, v_north, v_south = smoothed(at, V + k, v, shifted)
        half = (0.5 * THICK[k]) * at(D + k, 0)
        half_ns = (0.5 * THICK[k]) * (at(D + k, 1) - at(D + k, -1))
        pressure = acc + half
        pressure_ns = acc_ns + half_ns
        acc = pressure + half
        acc_ns = pressure_ns + half_ns
        slope = shifted(pressure, 1) - shifted(pressure, -1)
        u_star = wet * (u + spin * v - (0.5 * pressure_scale) * slope - viscous_scale * smooth_u)
        v_star = wet * (v - spin * u - (0.5 * pressure_scale) * pressure_ns - viscous_scale * smooth_v)
        sum_u = sum_u + THICK[k] * u_star
        sum_v = sum_v + THICK[k] * v_star
        old_u = old_u + THICK[k] * u
        old_v = old_v + THICK[k] * v
        depth = depth + THICK[k] * wet
        if put_u is None:
            continue
        put_u(k, u_star)
        put_v(k, v_star)
        for p, put in ((T + k, put_t), (S + k, put_s)):
            c = at(p, 0)
            smooth, north, south = smoothed(at, p, c, shifted)
            flux = u * c
            advect = (shifted(flux, 1) - shifted(flux, -1)) + (v_north * north - v_south * south)
            put(k, wet * (c - (0.5 * advect_scale) * advect - viscous_scale * smooth))
    return sum_u, sum_v, sum_u - old_u, sum_v - old_v, depth


def mirrored_lanes(side):
    lane = lanes()
    offset = 7 * side
    y = (lane + offset) & (COLS - 1)
    level = y // STRIDE
    col = y % STRIDE
    group = y < STRIDE * LEVELS
    second = lane >= (121 if side == 0 else 112)
    source = jnp.where(group, 2 * STRIDE * level + 3 - lane, jnp.where(second, 241 - lane, 223 - lane)) & (COLS - 1)
    tracer = (col < 2) if side == 0 else (col >= STRIDE - 2)
    with_u = jnp.where(group, jnp.where(tracer, 1.0, -1.0), jnp.where(second, -1.0, 1.0))
    with_v = jnp.where(group, jnp.where(tracer, 1.0, -1.0), jnp.where(second, 1.0, -1.0))
    return source, (with_u, with_v, 1.0, 1.0)


def pick(x, source):
    return jnp.take_along_axis(x, source, axis=1, mode="promise_in_bounds")


def pack_rows(u, v, t, s, w, bottom, eta, ub, vb, cor, a_ref, b_ref,
              u2, v2, t2, s2, w2, flat, deep, lo, hi, downs_ref, ups_ref, folds_ref, sem):
    even, top = lat_place()
    lane = lanes()
    sub = lax.broadcasted_iota(jnp.int32, (8, COLS), 0)
    moves = []
    for src, dst in ((u, u2), (v, v2), (t, t2), (s, s2), (w, w2)):
        moves.append((src.at[:, 0:16, :], dst.at[0]))
        moves.append((src.at[:, ROWS - 16 : ROWS, :], dst.at[1]))
    for n, src in enumerate((eta, ub, vb, cor)):
        moves.append((src, flat.at[n]))
    moves.append((bottom, deep))
    copies = fetch(moves, sem)
    sources = [mirrored_lanes(side) for side in (0, 1)]
    for copy in copies:
        copy.wait()
    for ref in (downs_ref, ups_ref, folds_ref):
        ref[ROW_SLAB - 8 : ROW_SLAB, :] = jnp.zeros((8, COLS), F32)
    d0 = deep[0:16, :]
    d1 = deep[ROWS - 16 : ROWS, :]
    south, north, ninth = Columns(lane), Columns(lane), Columns(lane)

    def lay(r, down, up, fold):
        for ref, val in ((downs_ref, down), (ups_ref, up), (folds_ref, fold)):
            ref[r : r + val.shape[0], :] = val

    def turned(x):
        return flip_rows(flip_lanes(x))

    for k in range(LEVELS):
        wl = jnp.where(k < d0, w2[0, k].astype(F32), 0.0)
        wh = jnp.where(k < d1, w2[1, k].astype(F32), 0.0)
        low = [ref[0, k] * wl for ref in (u2, v2, t2, s2)]
        high = [ref[1, k] * wh for ref in (u2, v2, t2, s2)]
        low_d = haline_scale * low[3] - thermal_scale * low[2]
        high_d = haline_scale * high[3] - thermal_scale * high[2]
        for p, q, sign, x, y in (
            (U, 0, -1.0, low[0], high[0]), (V, 1, -1.0, low[1], high[1]), (D, 2, 1.0, low_d, high_d), (WET, 3, 1.0, wl, wh),
        ):
            lo[p + k, 8:24, :] = x
            hi[p + k, 0:16, :] = y
            if q < 3:
                lo[p + k, 0:8, :] = jnp.zeros((8, COLS), F32)
                hi[p + k, 16:24, :] = jnp.zeros((8, COLS), F32)
            south.level(q, k, x[0:8])
            north.level(q, k, y[8:16])
            if q < 2:
                ninth.level(q, k, jnp.where(sub == 0, x[8:9], y[7:8]))
            if q < 2:
                lay(2 * (p + k), x[0:2], y[14:16], sign * turned(y[8:16])[0:2])
            elif q == 2:
                lay(AT_ONE + k, x[0:1], y[15:16], turned(y[8:16])[0:1])
        south.tracers(k, low[2][0:8], low[3][0:8])
        north.tracers(k, high[2][8:16], high[3][8:16])
        for n, (x, y) in enumerate(((low[2], high[2]), (low[3], high[3]), (wl, wh))):
            lay(AT_PAIR + 20 * n + 2 * k, x[0:2], y[14:16], turned(y[8:16])[0:2])
    for n, (at, count) in enumerate(FLAT_ROWS):
        down, up = flat[n, 0:8, :], flat[n, ROWS - 8 : ROWS, :]
        south.flat(n, down)
        north.flat(n, up)
        mirrored = (-1.0 if n in (1, 2) else 1.0) * turned(up)
        lay(AT_FLAT + at, down[0:count], up[8 - count : 8], mirrored[0:count])
    none = [None] * 4
    down = own_tile(lambda p, d: lo[p, 8 + d : 16 + d, :], rotation_scale * flat[3, 0:8, :], *none)
    up = own_tile(lambda p, d: hi[p, 8 + d : 16 + d, :], rotation_scale * flat[3, ROWS - 8 : ROWS, :], *none)
    for n, sign in enumerate((-1.0, -1.0, 1.0)):
        lay(AT_SUM + 7 * n, down[2 + n][0:7], up[2 + n][1:8], sign * turned(up[2 + n])[0:7])
    for side, (downs, ups, others) in enumerate(((south.east, north.east, north.west), (south.west, north.west, north.east))):
        source, signs = sources[side]
        for q in range(SLABS):
            lay(AT_SLAB + 32 * side + 8 * q, downs[q], ups[q], signs[q] * flip_rows(pick(others[q], source)))
    for side, (mine, other) in enumerate(((ninth.east, ninth.west), (ninth.west, ninth.east))):
        for q in range(2):
            lay(AT_NINE + 2 * side + q, mine[q][0:1], mine[q][1:2], -pick(other[q], sources[side][0])[1:2])
    for r in range(0, ROW_SLAB, 8):
        here = slice(r, r + 8)
        down, up = downs_ref[here, :], ups_ref[here, :]
        a_ref[here, :] = jnp.where(even, up, down)
        b_ref[here, :] = jnp.where(even, down, jnp.where(top, folds_ref[here, :], up))


def level_sums(mats):
    i = lax.broadcasted_iota(jnp.int32, (COLS, COLS), 0)
    j = lax.broadcasted_iota(jnp.int32, (COLS, COLS), 1)
    for side, offset in enumerate((0, 7)):
        def place(x):
            y = (x + offset) & (COLS - 1)
            return jnp.where(y < STRIDE * LEVELS, y % STRIDE, -1), y // STRIDE

        def above(src, dst):
            same = (src[0] == dst[0]) & (src[0] >= 0)
            return jnp.where(same & (src[1] < dst[1]), 1.0, jnp.where(same & (src[1] == dst[1]), 0.5, 0.0))

        src = place(i)
        mats[2 * side] = above(src, place(j))
        mats[2 * side + 1] = above(src, place(j + 1)) - above(src, place(j - 1))
        target = j + 2 if side == 0 else (j + 9) & (COLS - 1)
        low = 2 if side == 0 else 0
        mats[4 + side] = jnp.where((target >= low) & (target < low + 9) & (src[0] == target), 1.0, 0.0)
        if side == 0:
            mats[6] = jnp.where((src[0] == ((j + 2) & (COLS - 1))) & (((j + 2) & (COLS - 1)) < 4), 1.0, 0.0)


def dot(x, mat):
    return jnp.dot(x, mat, precision=lax.Precision.HIGHEST, preferred_element_type=F32)


def centre(u, v, t, s, w, bottom, eta, ub, vb, cor, x_ref, ec, wc, us, vs, tn, sn, sums, mats,
           u2, v2, t2, s2, w2, deep, sem):
    moves = list(zip((u, v, t, s, w, bottom), (u2, v2, t2, s2, w2, deep)))
    for n, src in enumerate((eta, ub, vb, cor)):
        moves.append((src, x_ref.at[FLAT + n]))
    copies = fetch(moves, sem)
    level_sums(mats)
    for copy in copies:
        copy.wait()
    lane = lanes()

    def pack(i, carry):
        rows = pl.ds(pl.multiple_of(8 * i, 8), 8)
        bed = deep[rows, :]
        columns = Columns(lane)
        for k in range(LEVELS):
            wet = jnp.where(k < bed, w2[k, rows, :].astype(F32), 0.0)
            uk = u2[k, rows, :] * wet
            vk = v2[k, rows, :] * wet
            tk = t2[k, rows, :] * wet
            sk = s2[k, rows, :] * wet
            dk = haline_scale * sk - thermal_scale * tk
            for p, val in ((U, uk), (V, vk), (D, dk), (WET, wet), (T, tk), (S, sk)):
                x_ref[p + k, rows, :] = val
            for q, val in enumerate((uk, vk, dk, wet)):
                columns.level(q, k, val)
            columns.tracers(k, tk, sk)
        for n in range(4):
            columns.flat(n, x_ref[FLAT + n, rows, :])
        for q in range(SLABS):
            ec[q, rows, :] = columns.east[q]
            wc[q, rows, :] = columns.west[q]
        return carry

    lax.fori_loop(0, ROWS // 8, pack, 0)

    def inner(i, carry):
        r0 = 8 * i
        rows = pl.ds(pl.multiple_of(r0, 8), 8)

        def store(ref):
            def put(k, val):
                ref[k, rows, :] = val

            return put

        got = own_tile(
            lambda p, d: x_ref[p, pl.ds(r0 + d, 8), :], rotation_scale * x_ref[FLAT + 3, rows, :],
            store(us), store(vs), store(tn), store(sn),
        )
        for n in range(5):
            sums[n, rows, :] = got[n]
        return carry

    lax.fori_loop(1, ROWS // 8 - 1, inner, 0)


def pack_rims(a_ref, b_ref, ec, wc, far_ref, near_ref):
    even, _ = lat_place()
    odd = lon_odd()

    def send(at, east, west):
        here = slice(at, at + east.shape[0])
        far_ref[here, :] = jnp.where(odd, west, east)
        near_ref[here, :] = jnp.where(odd, east, west)

    for q in range(SLABS):
        send(TALL * q + 8, ec[q], wc[q])

    def both(r, n):
        a = a_ref[r : r + n, :]
        b = b_ref[r : r + n, :]
        return jnp.where(even, b, a), jnp.where(even, a, b)

    for q in range(SLABS):
        (e_lo, e_hi), (w_lo, w_hi) = (both(AT_SLAB + 32 * side + 8 * q, 8) for side in (0, 1))
        send(TALL * q, e_lo, w_lo)
        send(TALL * q + 8 + ROWS, e_hi, w_hi)
    for q in range(2):
        pairs = [both(AT_NINE + 2 * side + q, 1) for side in (0, 1)]
        for n in (0, 1):
            send(SLABS * TALL + 2 * q + n, pairs[0][n], pairs[1][n])
    send(SLABS * TALL + 4, *[jnp.zeros((4, COLS), F32)] * 2)


def edges(x_ref, a_ref, b_ref, us, vs, tn, sn, sums, low, high):
    even, _ = lat_place()

    def both(r, n):
        a = a_ref[pl.ds(r, n), :]
        b = b_ref[pl.ds(r, n), :]
        return jnp.where(even, b, a), jnp.where(even, a, b)

    def place(p, carry):
        low[p, 16:32, :] = x_ref[p, 0:16, :]
        high[p, 0:16, :] = x_ref[p, ROWS - 16 : ROWS, :]
        return carry

    lax.fori_loop(0, FLAT, place, 0)

    def clear(p, carry):
        low[p, 8:16, :] = jnp.zeros((8, COLS), F32)
        high[p, 16:24, :] = jnp.zeros((8, COLS), F32)
        return carry

    lax.fori_loop(0, 40, clear, 0)

    def pair(n, p):
        for k in range(LEVELS):
            lo, hi = both(AT_PAIR + 20 * n + 2 * k, 2)
            low[p + k, 14:16, :] = lo
            high[p + k, 16:18, :] = hi

    def tile(n, ref, r0, spin, puts):
        got = own_tile(lambda p, d: ref[p, r0 + d : r0 + d + 8, :], rotation_scale * spin, *puts)
        for m in range(5):
            sums[m, 8 * n : 8 * n + 8, :] = got[m]

    pair(2, WET)
    none = jnp.zeros((8, COLS), F32)
    for n, ref, r0 in ((2, low, 8), (3, high, 16)):
        tile(n, ref, r0, none, [None] * 4)
    for m in (2, 3, 4):
        lo, hi = both(AT_SUM + 7 * (m - 2), 7)
        if m < 4:
            lo = lo + sums[m, 17:24, :]
            hi = hi + sums[m, 24:31, :]
        sums[m, 17:24, :] = lo
        sums[m, 24:31, :] = hi
    for p in range(20):
        lo, hi = both(2 * p, 2)
        low[p, 14:16, :] = lo
        high[p, 16:18, :] = hi
    for k in range(LEVELS):
        lo, hi = both(AT_ONE + k, 1)
        low[D + k, 15:16, :] = lo
        high[D + k, 16:17, :] = hi
    pair(0, T)
    pair(1, S)
    for n, ref, r0, row in ((0, low, 16, 0), (1, high, 8, ROWS - 8)):
        def store(out):
            def put(k, val):
                out[k, 8 * n : 8 * n + 8, :] = val

            return put

        tile(n, ref, r0, x_ref[FLAT + 3, row : row + 8, :], [store(out) for out in (us, vs, tn, sn)])


class Wide:
    def __init__(self, own, rim):
        self.own, self.rim = own, rim

    def with_other(self, other, op):
        if isinstance(other, Wide):
            return Wide(op(self.own, other.own), op(self.rim, other.rim))
        return Wide(op(self.own, other), op(self.rim, other))

    def __add__(self, other):
        return self.with_other(other, lambda a, b: a + b)

    def __sub__(self, other):
        return self.with_other(other, lambda a, b: a - b)

    def __mul__(self, other):
        return self.with_other(other, lambda a, b: a * b)

    __rmul__ = __mul__

    def __truediv__(self, other):
        return self.with_other(other, lambda a, b: a / b)


def slope(x):
    lane = lanes()
    east_own, east_rim = turn(x.own, -1), turn(x.rim, -1)
    west_own, west_rim = turn(x.own, 1), turn(x.rim, 1)
    last, first = lane == COLS - 1, lane == 0
    return Wide(
        jnp.where(last, east_rim, east_own) - jnp.where(first, west_rim, west_own),
        jnp.where(last, east_own, east_rim) - jnp.where(first, west_own, west_rim),
    )


def step(x_ref, a_ref, b_ref, far_mine, near_mine, far_got, near_got, us, vs, tn, sn, sums, us2, vs2, tn2, sn2, sums2, mats,
         u_out, v_out, t_out, s_out, eta_out, ub_out, vb_out,
         es, ws, own, rim, fix, total, col, fu, fv, mu, mv, tu, tv, spins, t_new, s_new, u_new, v_new, flats, sem):
    even, _ = lat_place()
    lane = lanes()
    rest = lane % STRIDE
    inside = lane < LEVELS * STRIDE
    odd = lon_odd()
    for q, r, count in [(q, r, 8) for r in range(8, 88, 8) for q in range(SLABS)] + [(0, 0, 2), (1, 0, 2)]:
        at = TALL * q + r - 8 if r else SLABS * TALL + 2 * q
        got = slice(at, at + count)
        far_in, near_in = far_got[got, :], near_got[got, :]
        far_out, near_out = far_mine[got, :], near_mine[got, :]
        e_got, w_got = jnp.where(odd, far_in, near_in), jnp.where(odd, near_in, far_in)
        e_mine, w_mine = jnp.where(odd, near_out, far_out), jnp.where(odd, far_out, near_out)
        own_e, own_w = (m[0:count] for m in ((rest < 2) & inside, ((rest == 2) | (rest == 3)) & inside))
        for ref, val in ((es, jnp.where(own_e, w_mine, e_got)), (ws, jnp.where(own_w, e_mine, w_got))):
            if r:
                ref[q, r : r + 8, :] = val
            else:
                ref[q, 7:8, :] = val[0:1]
                ref[q, TOP + ROWS + 8 : TOP + ROWS + 9, :] = val[1:2]
        if q < 2 and r:
            es[SLABS + q, r : r + 8, :] = turn(e_got, 2)
            ws[SLABS + q, r : r + 8, :] = turn(w_got, -2)
    for n in range(4):
        at, count = FLAT_ROWS[n]
        a = a_ref[AT_FLAT + at : AT_FLAT + at + count, :]
        b = b_ref[AT_FLAT + at : AT_FLAT + at + count, :]
        own[n, TOP - count : TOP, :] = jnp.where(even, b, a)
        own[n, TOP : TOP + ROWS, :] = x_ref[FLAT + n]
        own[n, TOP + ROWS : TOP + ROWS + count, :] = jnp.where(even, a, b)
        q, second = divmod(n, 2)
        for r in range(8, 88, 8):
            at = (121, 7) if second else (112, 16)
            rim[n, r : r + 8, :] = turn(jnp.where(lane >= at[0], es[q, r : r + 8, :], ws[q, r : r + 8, :]), at[1])
    for m in range(5):
        total[m, 8:16, :] = sums2[m, 16:24, :]
        total[m, 16:24, :] = sums2[m, 0:8, :]
        total[m, 24:72, :] = sums[m, 8:56, :]
        total[m, 72:80, :] = sums2[m, 8:16, :]
        total[m, 80:88, :] = sums2[m, 24:32, :]

    short = lane
    lane = lanes(BAND)
    rest = lane % STRIDE
    inside = lane < LEVELS * STRIDE
    level_e = jnp.minimum(lane // STRIDE, LEVELS)
    level_w = jnp.minimum(((lane + 7) % COLS) // STRIDE, LEVELS)
    thick_e = jnp.where(level_e < LEVELS, (level_e + 1).astype(F32) * THICK[0], 0.0)
    thick_w = jnp.where(level_w < LEVELS, (level_w + 1).astype(F32) * THICK[0], 0.0)
    edge = (lane < 2) | (lane >= COLS - 2)
    border = (short < 2) | (short >= COLS - 2)

    def slab_tile(i, carry):
        r0 = BAND * i + 8
        here = pl.ds(pl.multiple_of(r0, 8), BAND)
        parts = []
        for ref, side, thick, ahead in ((es, 0, thick_e, 1), (ws, 1, thick_w, -1)):
            def at(q, d):
                return ref[q, pl.ds(r0 + d, BAND), :]

            def around(x, d):
                return turn(x, -d)

            if ahead > 0:
                near, pair = (rest == 2) & inside, ((rest == 2) | (rest == 3)) & inside
            else:
                near, pair = (rest == 1) & inside, (rest < 2) & inside
            wet = at(3, 0)
            u = at(0, 0)
            v = at(1, 0)
            weight = thick * at(2, 0)
            weight_ns = thick * (at(2, 1) - at(2, -1))
            pressure = dot(weight, mats[2 * side])
            pressure_slope = dot(weight, mats[2 * side + 1])
            pressure_ns = dot(weight_ns, mats[2 * side])
            smooth_u, un, us_ = smoothed(at, 0, u, around)
            smooth_v, vn, vs_ = smoothed(at, 1, v, around)
            change = pressure_scale * 0.5 * pressure_slope + viscous_scale * smooth_u
            change_ns = pressure_scale * 0.5 * pressure_ns + viscous_scale * smooth_v
            parts.append((wet * thick, -change, -change_ns, u, v, wet))

            def beyond(c, ns, extra):
                far = viscous_scale * jnp.where(pair, c, 0.0)
                close = jnp.where(near, (2.0 * viscous_scale) * (ns - 4.0 * c) + extra, 0.0)
                return -(turn(far, -2 * ahead) + turn(close, -ahead))

            push = (0.5 * pressure_scale * ahead) * pressure
            fixes = [beyond(u, un + us_, push), beyond(v, vn + vs_, 0.0)]
            carry_u = (0.5 * advect_scale * ahead) * u
            for q in (SLABS, SLABS + 1):
                c = at(q, 0)
                fixes.append(beyond(c, at(q, 1) + at(q, -1), carry_u * c))
            parts.append(fixes)
        (we, due, dve, ue, ve, wet_e), fix_e, (ww, duw, dvw, uw, vw, wet_w), fix_w = parts
        own_wet = jnp.where(rest < 2, wet_e, wet_w)
        own_thick = jnp.where(rest < 2, thick_e, thick_w)
        fixes = [own_wet * (x + y) for x, y in zip(fix_e, fix_w)]
        for n in range(4):
            fix[n, here, :] = fixes[n]

        east = jnp.concatenate([we, we * due, we * dve, we * ue, we * ve], axis=0)
        west = jnp.concatenate([ww, ww * duw, ww * dvw, ww * uw, ww * vw], axis=0)
        rims = dot(east, mats[4]) + dot(west, mats[5])
        rim_depth, rim_du, rim_dv, rim_u, rim_v = (rims[BAND * n : BAND * n + BAND] for n in range(5))
        owns = dot(jnp.concatenate([own_thick * fixes[0], own_thick * fixes[1]], axis=0), mats[6])
        spin = Wide(rotation_scale * own[3, here, :], rotation_scale * rim[3, here, :])
        column = Wide(surface_depth + total[4, here, :], surface_depth + rim_depth)
        diff_u = rim_du + spin.rim * rim_v
        diff_v = rim_dv - spin.rim * rim_u
        fix_u, fix_v = owns[0:BAND], owns[BAND : 2 * BAND]
        part = Wide(1.0 / column.own, 1.0 / column.rim)
        for ref, mean, own_sum, own_diff, rim_diff, x in (
            (fu, mu, total[0, here, :], total[2, here, :], diff_u, fix_u),
            (fv, mv, total[1, here, :], total[3, here, :], diff_v, fix_v),
        ):
            ref[0, here, :] = (own_diff + x) * part.own * (1.0 / SUBSTEPS)
            ref[1, here, :] = rim_diff * part.rim * (1.0 / SUBSTEPS)
            mean[here, :] = (own_sum + x) * part.own
        for ref, x in ((col, column), (spins, spin)):
            ref[0, here, :] = x.own
            ref[1, here, :] = x.rim
        return carry

    lax.fori_loop(0, 80 // BAND, slab_tile, 0)

    def mend(n, k, rows_fix):
        return jnp.where(border, turn(fix[n, rows_fix, :], -(STRIDE * k + 2)), 0.0)

    def tile_of(i):
        return pl.ds(pl.multiple_of(8 * i, 8), 8), pl.ds(pl.multiple_of(8 * i + TOP, 8), 8)

    def tracer_tile(rows, fixed, refs, src):
        for n, (ref, out) in enumerate(zip(refs, (t_new, s_new))):
            for k in range(LEVELS):
                out[k, rows, :] = ref[k, src, :] + mend(2 + n, k, fixed)

    def tracer_loop(i, carry):
        rows, fixed = tile_of(i)
        tracer_tile(rows, fixed, (tn, sn), rows)
        return carry

    lax.fori_loop(1, ROWS // 8 - 1, tracer_loop, 0)
    for n, i in enumerate((0, ROWS // 8 - 1)):
        tracer_tile(slice(8 * i, 8 * i + 8), slice(8 * i + TOP, 8 * i + TOP + 8), (tn2, sn2), slice(8 * n, 8 * n + 8))
    first = [pltpu.make_async_copy(src, dst, sem.at[n]) for n, (src, dst) in enumerate(((t_new, t_out), (s_new, s_out)))]
    for copy in first:
        copy.start()

    def wide(ref, at):
        return Wide(ref[0, at, :], ref[1, at, :])

    def keep(ref, at, x):
        ref[0, at, :] = x.own
        ref[1, at, :] = x.rim

    def flat(p, r):
        return Wide(own[p, r : r + 8, :], rim[p, r : r + 8, :])

    def wet_of(column):
        return Wide(jnp.where(column.own > surface_depth, 1.0, 0.0), jnp.where(column.rim > surface_depth, 1.0, 0.0))

    def substep(n, carry):
        for r in range(8, 88, 8):
            here = slice(r, r + 8)
            column = wide(col, here)
            wet = wet_of(column)
            u = flat(1, r)
            v = flat(2, r)
            spin = wide(spins, here)
            un = wet * (u - (0.5 * gravity_scale) * slope(flat(0, r)) + spin * v + wide(fu, here))
            vn = wet * (v - (0.5 * gravity_scale) * (flat(0, r + 1) - flat(0, r - 1)) - spin * u + wide(fv, here))
            for p, x in ((1, un), (2, vn)):
                own[p, here, :] = x.own
                rim[p, here, :] = x.rim
            keep(tu, here, column * un)
            keep(tv, here, column * vn)
        for r in range(8, 88, 8):
            here = slice(r, r + 8)
            wet = wet_of(wide(col, here))
            flow = slope(wide(tu, here)) + (wide(tv, slice(r + 1, r + 9)) - wide(tv, slice(r - 1, r + 7)))
            eta = wet * (flat(0, r) - (0.5 * divergence_scale) * flow)
            own[0, here, :] = eta.own
            rim[0, here, :] = eta.rim
        return carry

    lax.fori_loop(0, SUBSTEPS, substep, 0)
    second = []
    for n, dst in enumerate((eta_out, ub_out, vb_out)):
        flats[n] = own[n, TOP : TOP + ROWS, :]
        second.append(pltpu.make_async_copy(flats.at[n], dst, sem.at[2 + n]))
        second[-1].start()

    def flow_tile(rows, fixed, refs, src):
        gain = (own[1, fixed, :] - mu[fixed, :], own[2, fixed, :] - mv[fixed, :])
        for k in range(LEVELS):
            wet = x_ref[WET + k, rows, :]
            for n, (ref, out) in enumerate(zip(refs, (u_new, v_new))):
                out[k, rows, :] = ref[k, src, :] + mend(n, k, fixed) + wet * gain[n]

    def flow_loop(i, carry):
        rows, fixed = tile_of(i)
        flow_tile(rows, fixed, (us, vs), rows)
        return carry

    lax.fori_loop(1, ROWS // 8 - 1, flow_loop, 0)
    for n, i in enumerate((0, ROWS // 8 - 1)):
        flow_tile(slice(8 * i, 8 * i + 8), slice(8 * i + TOP, 8 * i + TOP + 8), (us2, vs2), slice(8 * n, 8 * n + 8))
    last = [pltpu.make_async_copy(src, dst, sem.at[5 + n]) for n, (src, dst) in enumerate(((u_new, u_out), (v_new, v_out)))]
    for copy in last:
        copy.start()
    for copy in first + second + last:
        copy.wait()


def colour(parity, lats, lons):
    pairs = []
    for lat in range(lats):
        for lon in range(lons):
            if (lat + parity) % 2 == 0:
                to = (lon, lat + 1) if lat + 1 < lats else (lons - 1 - lon, lat)
            elif lat > 0:
                to = (lon, lat - 1)
            else:
                continue
            pairs.append((lon * lats + lat, to[0] * lats + to[1]))
    return pairs


def partners(first, lons):
    pairs = []
    for west in range(first, lons + first, 2):
        east = (west + 1) % lons
        pairs += [(west % lons, east), (east, west % lons)]
    return pairs


def local(u, v, t, s, w, bottom, eta, ub, vb, cor):
    lats = lax.axis_size("lat")
    lons = lax.axis_size("lon")
    raw = tuple(pltpu.with_memory_space_constraint(z, pltpu.HBM) for z in (u, v, t, s, w, bottom, eta, ub, vb, cor))
    vmem = pltpu.VMEM
    dma = pltpu.SemaphoreType.DMA
    two = (2, LEVELS, 16, COLS)
    a, b = call(
        pack_rows, [(ROW_SLAB, COLS)] * 2,
        [vmem(two, F32)] * 4 + [vmem(two, jnp.int32), vmem((4, ROWS, COLS), F32), vmem(PLANE, jnp.int32)]
        + [vmem((40, 24, COLS), F32)] * 2 + [vmem((ROW_SLAB, COLS), F32)] * 3 + [dma((15,))],
        1_000_000, *raw, ins=[HBM] * 10,
    )
    b = lax.ppermute(b, ("lon", "lat"), colour(1, lats, lons))
    a = lax.ppermute(a, ("lon", "lat"), colour(0, lats, lons))
    x, ec, wc, us, vs, tn, sn, sums, mats = call(
        centre, [(PLANES, ROWS, COLS)] + [(SLABS, ROWS, COLS)] * 2 + [CUBE] * 4 + [(5, ROWS, COLS), (7, COLS, COLS)],
        [vmem(CUBE, F32)] * 4 + [vmem(CUBE, jnp.int32), vmem(PLANE, jnp.int32), dma((10,))],
        20_000_000, *raw, ins=[HBM] * 10,
    )
    far, near = call(pack_rims, [(COLUMN_SLAB, COLS)] * 2, [], 1_000_000, a, b, ec, wc)
    far_got = lax.ppermute(far, "lon", partners(1, lons))
    near_got = lax.ppermute(near, "lon", partners(0, lons))
    window = vmem((FLAT, 32, COLS), F32)
    us2, vs2, tn2, sn2, sums2 = call(
        edges, [(LEVELS, 16, COLS)] * 4 + [(5, 32, COLS)], [window] * 2, 10_000_000, x, a, b,
    )
    wide = vmem((2, HIGH, COLS), F32)
    thin = vmem((HIGH, COLS), F32)
    slab = vmem((SLABS + 2, HIGH, COLS), F32)
    four = vmem((4, HIGH, COLS), F32)
    return tuple(
        call(
            step, [CUBE] * 4 + [PLANE] * 3,
            [slab] * 2 + [four] * 3 + [vmem((5, HIGH, COLS), F32)] + [wide] * 3 + [thin] * 2 + [wide] * 3
            + [vmem(CUBE, F32)] * 4 + [vmem((3, ROWS, COLS), F32), dma((7,))],
            50_000_000, x, a, b, far, near, far_got, near_got, us, vs, tn, sn, sums, us2, vs2, tn2, sn2, sums2, mats,
            outs=[HBM] * 7,
        )
    )


def solution(mesh):
    deep = P(None, "lat", "lon")
    flat = P("lat", "lon")
    return jax.shard_map(
        local,
        mesh=mesh,
        in_specs=(deep,) * 5 + (flat,) * 5,
        out_specs=(deep,) * 4 + (flat,) * 3,
        check_vma=False,
    )
```

```python
import jax
import jax.numpy as jnp
from jax import lax
from jax.experimental import pallas as pl
from jax.experimental.pallas import tpu as pltpu
from jax.sharding import PartitionSpec as P


SUBSTEPS = 4
LEVELS = 10
ROWS = 64
COLS = 128
U, V, D, WET, T, S, FLAT = 0, 10, 20, 30, 40, 50, 60
PLANES = 64
AT_ONE = 40
AT_PAIR = AT_ONE + 10
AT_FLAT = AT_PAIR + 60
AT_SUM = AT_FLAT + 29
AT_SLAB = AT_SUM + 21
AT_NINE = AT_SLAB + 64
ROW_SLAB = AT_NINE + 8
FLAT_ROWS = ((0, 8), (8, 7), (15, 7), (22, 7))
STRIDE = 11
SLABS = 4
TALL = 80
COLUMN_SLAB = SLABS * TALL + 8
TOP = 16
HIGH = 96
BAND = 80

advect_scale = 0.25
viscous_scale = 0.02
pressure_scale = 0.5
rotation_scale = 0.3
thermal_scale = 0.2
haline_scale = 0.8
surface_depth = 0.25
gravity_scale = 0.3
divergence_scale = 0.3

F32 = jnp.float32
THICK = [(k + 1.0) * (2.0 / (LEVELS * (LEVELS + 1))) for k in range(LEVELS)]
HBM = pl.BlockSpec(memory_space=pltpu.HBM)
VMEM = pl.BlockSpec(memory_space=pltpu.VMEM)
CUBE = (LEVELS, ROWS, COLS)
PLANE = (ROWS, COLS)


def call(kernel, out, scratch, flops, *args, ins=None, outs=None):
    return pl.pallas_call(
        kernel,
        out_shape=[jax.ShapeDtypeStruct(s, F32) for s in out],
        in_specs=ins or [VMEM] * len(args),
        out_specs=outs or [VMEM] * len(out),
        scratch_shapes=scratch,
        cost_estimate=pl.CostEstimate(flops=flops, bytes_accessed=2_000_000, transcendentals=0),
        compiler_params=pltpu.CompilerParams(vmem_limit_bytes=LIMIT),
    )(*args)


LIMIT = 40 * 1024 * 1024


def lanes(rows=8):
    return lax.broadcasted_iota(jnp.int32, (rows, COLS), 1)


def flip_lanes(x):
    return jnp.take_along_axis(x, COLS - 1 - lax.broadcasted_iota(jnp.int32, x.shape, 1), axis=1, mode="promise_in_bounds")


def flip_rows(x):
    return jnp.take_along_axis(x, 7 - lax.broadcasted_iota(jnp.int32, x.shape, 0), axis=0, mode="promise_in_bounds")


def turn(x, shift):
    return pltpu.roll(x, shift % COLS, 1)


def lat_place():
    index = lax.axis_index("lat")
    return index % 2 == 0, index == lax.axis_size("lat") - 1


def lon_odd():
    return lax.axis_index("lon") % 2 == 1


def fetch(pairs, sem):
    copies = [pltpu.make_async_copy(src, dst, sem.at[n]) for n, (src, dst) in enumerate(pairs)]
    for copy in copies:
        copy.start()
    return copies


class Columns:
    def __init__(self, lane):
        self.lane = lane
        zero = jnp.zeros((8, COLS), F32)
        self.east = [zero] * SLABS
        self.west = [zero] * SLABS

    def put_east(self, q, moved, at, count):
        lane = self.lane
        self.east[q] = jnp.where((lane >= at) & (lane < at + count), moved, self.east[q])

    def put_west(self, q, moved, end, count):
        lane = self.lane
        low = (end - count) % COLS
        here = (lane >= low) & (lane < end) if low < end else (lane >= low) | (lane < end)
        self.west[q] = jnp.where(here, moved, self.west[q])

    def put(self, q, val, shift, count):
        moved = turn(val, shift)
        self.put_east(q, moved, shift, count)
        self.put_west(q, moved, shift, count)

    def level(self, q, k, val):
        self.put(q, val, STRIDE * k + 2, 9)

    def tracers(self, k, t, s):
        for q, val in enumerate((t, s)):
            self.put_east(q, turn(val, STRIDE * k), STRIDE * k, 2)
            self.put_west(q, turn(val, STRIDE * k + 4), STRIDE * k + 4, 2)

    def flat(self, n, val):
        if n % 2 == 0:
            self.put(n // 2, val, 112, 9)
        else:
            self.put(n // 2, val, 121, 7)


def shifted(x, d):
    lane = lanes()
    keep = lane < COLS - d if d > 0 else lane >= -d
    return jnp.where(keep, turn(x, -d), 0.0)


def smoothed(at, p, c, shift):
    north, south = at(p, 1), at(p, -1)
    q = (north + south) - 4.0 * c
    both = shift(c, 2) + shift(c, -2) + (at(p, 2) + at(p, -2))
    return both + 2.0 * ((shift(q, 1) + shift(q, -1)) - 4.0 * q) - 12.0 * c, north, south


def own_tile(at, spin, put_u, put_v, put_t, put_s):
    zero = jnp.zeros((8, COLS), F32)
    acc = acc_ns = sum_u = sum_v = old_u = old_v = depth = zero
    for k in range(LEVELS):
        wet = at(WET + k, 0)
        u = at(U + k, 0)
        v = at(V + k, 0)
        smooth_u, _, _ = smoothed(at, U + k, u, shifted)
        smooth_v, v_north, v_south = smoothed(at, V + k, v, shifted)
        half = (0.5 * THICK[k]) * at(D + k, 0)
        half_ns = (0.5 * THICK[k]) * (at(D + k, 1) - at(D + k, -1))
        pressure = acc + half
        pressure_ns = acc_ns + half_ns
        acc = pressure + half
        acc_ns = pressure_ns + half_ns
        slope = shifted(pressure, 1) - shifted(pressure, -1)
        u_star = wet * (u + spin * v - (0.5 * pressure_scale) * slope - viscous_scale * smooth_u)
        v_star = wet * (v - spin * u - (0.5 * pressure_scale) * pressure_ns - viscous_scale * smooth_v)
        sum_u = sum_u + THICK[k] * u_star
        sum_v = sum_v + THICK[k] * v_star
        old_u = old_u + THICK[k] * u
        old_v = old_v + THICK[k] * v
        depth = depth + THICK[k] * wet
        if put_u is None:
            continue
        put_u(k, u_star)
        put_v(k, v_star)
        for p, put in ((T + k, put_t), (S + k, put_s)):
            c = at(p, 0)
            smooth, north, south = smoothed(at, p, c, shifted)
            flux = u * c
            advect = (shifted(flux, 1) - shifted(flux, -1)) + (v_north * north - v_south * south)
            put(k, wet * (c - (0.5 * advect_scale) * advect - viscous_scale * smooth))
    return sum_u, sum_v, sum_u - old_u, sum_v - old_v, depth


def mirrored_lanes(side):
    lane = lanes()
    offset = 7 * side
    y = (lane + offset) & (COLS - 1)
    level = y // STRIDE
    col = y % STRIDE
    group = y < STRIDE * LEVELS
    second = lane >= (121 if side == 0 else 112)
    source = jnp.where(group, 2 * STRIDE * level + 3 - lane, jnp.where(second, 241 - lane, 223 - lane)) & (COLS - 1)
    tracer = (col < 2) if side == 0 else (col >= STRIDE - 2)
    with_u = jnp.where(group, jnp.where(tracer, 1.0, -1.0), jnp.where(second, -1.0, 1.0))
    with_v = jnp.where(group, jnp.where(tracer, 1.0, -1.0), jnp.where(second, 1.0, -1.0))
    return source, (with_u, with_v, 1.0, 1.0)


def pick(x, source):
    return jnp.take_along_axis(x, source, axis=1, mode="promise_in_bounds")


def pack_rows(u, v, t, s, w, bottom, eta, ub, vb, cor, a_ref, b_ref,
              u2, v2, t2, s2, w2, flat, deep, lo, hi, downs_ref, ups_ref, folds_ref, sem):
    even, top = lat_place()
    lane = lanes()
    sub = lax.broadcasted_iota(jnp.int32, (8, COLS), 0)
    moves = []
    for src, dst in ((u, u2), (v, v2), (t, t2), (s, s2), (w, w2)):
        moves.append((src.at[:, 0:16, :], dst.at[0]))
        moves.append((src.at[:, ROWS - 16 : ROWS, :], dst.at[1]))
    for n, src in enumerate((eta, ub, vb, cor)):
        moves.append((src, flat.at[n]))
    moves.append((bottom, deep))
    copies = fetch(moves, sem)
    sources = [mirrored_lanes(side) for side in (0, 1)]
    for copy in copies:
        copy.wait()
    for ref in (downs_ref, ups_ref, folds_ref):
        ref[ROW_SLAB - 8 : ROW_SLAB, :] = jnp.zeros((8, COLS), F32)
    d0 = deep[0:16, :]
    d1 = deep[ROWS - 16 : ROWS, :]
    south, north, ninth = Columns(lane), Columns(lane), Columns(lane)

    def lay(r, down, up, fold):
        for ref, val in ((downs_ref, down), (ups_ref, up), (folds_ref, fold)):
            ref[r : r + val.shape[0], :] = val

    def turned(x):
        return flip_rows(flip_lanes(x))

    for k in range(LEVELS):
        wl = jnp.where(k < d0, w2[0, k].astype(F32), 0.0)
        wh = jnp.where(k < d1, w2[1, k].astype(F32), 0.0)
        low = [ref[0, k] * wl for ref in (u2, v2, t2, s2)]
        high = [ref[1, k] * wh for ref in (u2, v2, t2, s2)]
        low_d = haline_scale * low[3] - thermal_scale * low[2]
        high_d = haline_scale * high[3] - thermal_scale * high[2]
        for p, q, sign, x, y in (
            (U, 0, -1.0, low[0], high[0]), (V, 1, -1.0, low[1], high[1]), (D, 2, 1.0, low_d, high_d), (WET, 3, 1.0, wl, wh),
        ):
            lo[p + k, 8:24, :] = x
            hi[p + k, 0:16, :] = y
            if q < 3:
                lo[p + k, 0:8, :] = jnp.zeros((8, COLS), F32)
                hi[p + k, 16:24, :] = jnp.zeros((8, COLS), F32)
            south.level(q, k, x[0:8])
            north.level(q, k, y[8:16])
            if q < 2:
                ninth.level(q, k, jnp.where(sub == 0, x[8:9], y[7:8]))
            if q < 2:
                lay(2 * (p + k), x[0:2], y[14:16], sign * turned(y[8:16])[0:2])
            elif q == 2:
                lay(AT_ONE + k, x[0:1], y[15:16], turned(y[8:16])[0:1])
        south.tracers(k, low[2][0:8], low[3][0:8])
        north.tracers(k, high[2][8:16], high[3][8:16])
        for n, (x, y) in enumerate(((low[2], high[2]), (low[3], high[3]), (wl, wh))):
            lay(AT_PAIR + 20 * n + 2 * k, x[0:2], y[14:16], turned(y[8:16])[0:2])
    for n, (at, count) in enumerate(FLAT_ROWS):
        down, up = flat[n, 0:8, :], flat[n, ROWS - 8 : ROWS, :]
        south.flat(n, down)
        north.flat(n, up)
        mirrored = (-1.0 if n in (1, 2) else 1.0) * turned(up)
        lay(AT_FLAT + at, down[0:count], up[8 - count : 8], mirrored[0:count])
    none = [None] * 4
    down = own_tile(lambda p, d: lo[p, 8 + d : 16 + d, :], rotation_scale * flat[3, 0:8, :], *none)
    up = own_tile(lambda p, d: hi[p, 8 + d : 16 + d, :], rotation_scale * flat[3, ROWS - 8 : ROWS, :], *none)
    for n, sign in enumerate((-1.0, -1.0, 1.0)):
        lay(AT_SUM + 7 * n, down[2 + n][0:7], up[2 + n][1:8], sign * turned(up[2 + n])[0:7])
    for side, (downs, ups, others) in enumerate(((south.east, north.east, north.west), (south.west, north.west, north.east))):
        source, signs = sources[side]
        for q in range(SLABS):
            lay(AT_SLAB + 32 * side + 8 * q, downs[q], ups[q], signs[q] * flip_rows(pick(others[q], source)))
    for side, (mine, other) in enumerate(((ninth.east, ninth.west), (ninth.west, ninth.east))):
        for q in range(2):
            lay(AT_NINE + 2 * side + q, mine[q][0:1], mine[q][1:2], -pick(other[q], sources[side][0])[1:2])
    for r in range(0, ROW_SLAB, 8):
        here = slice(r, r + 8)
        down, up = downs_ref[here, :], ups_ref[here, :]
        a_ref[here, :] = jnp.where(even, up, down)
        b_ref[here, :] = jnp.where(even, down, jnp.where(top, folds_ref[here, :], up))


def level_sums(mats):
    i = lax.broadcasted_iota(jnp.int32, (COLS, COLS), 0)
    j = lax.broadcasted_iota(jnp.int32, (COLS, COLS), 1)
    for side, offset in enumerate((0, 7)):
        def place(x):
            y = (x + offset) & (COLS - 1)
            return jnp.where(y < STRIDE * LEVELS, y % STRIDE, -1), y // STRIDE

        def above(src, dst):
            same = (src[0] == dst[0]) & (src[0] >= 0)
            return jnp.where(same & (src[1] < dst[1]), 1.0, jnp.where(same & (src[1] == dst[1]), 0.5, 0.0))

        src = place(i)
        mats[2 * side] = above(src, place(j))
        mats[2 * side + 1] = above(src, place(j + 1)) - above(src, place(j - 1))
        target = j + 2 if side == 0 else (j + 9) & (COLS - 1)
        low = 2 if side == 0 else 0
        mats[4 + side] = jnp.where((target >= low) & (target < low + 9) & (src[0] == target), 1.0, 0.0)
        if side == 0:
            mats[6] = jnp.where((src[0] == ((j + 2) & (COLS - 1))) & (((j + 2) & (COLS - 1)) < 4), 1.0, 0.0)


def dot(x, mat):
    return jnp.dot(x, mat, precision=lax.Precision.HIGHEST, preferred_element_type=F32)


def centre(u, v, t, s, w, bottom, eta, ub, vb, cor, x_ref, ec, wc, us, vs, tn, sn, sums, mats,
           u2, v2, t2, s2, w2, deep, sem):
    moves = list(zip((u, v, t, s, w, bottom), (u2, v2, t2, s2, w2, deep)))
    for n, src in enumerate((eta, ub, vb, cor)):
        moves.append((src, x_ref.at[FLAT + n]))
    copies = fetch(moves, sem)
    level_sums(mats)
    for copy in copies:
        copy.wait()
    lane = lanes()

    def pack(i, carry):
        rows = pl.ds(pl.multiple_of(8 * i, 8), 8)
        bed = deep[rows, :]
        columns = Columns(lane)
        for k in range(LEVELS):
            wet = jnp.where(k < bed, w2[k, rows, :].astype(F32), 0.0)
            uk = u2[k, rows, :] * wet
            vk = v2[k, rows, :] * wet
            tk = t2[k, rows, :] * wet
            sk = s2[k, rows, :] * wet
            dk = haline_scale * sk - thermal_scale * tk
            for p, val in ((U, uk), (V, vk), (D, dk), (WET, wet), (T, tk), (S, sk)):
                x_ref[p + k, rows, :] = val
            for q, val in enumerate((uk, vk, dk, wet)):
                columns.level(q, k, val)
            columns.tracers(k, tk, sk)
        for n in range(4):
            columns.flat(n, x_ref[FLAT + n, rows, :])
        for q in range(SLABS):
            ec[q, rows, :] = columns.east[q]
            wc[q, rows, :] = columns.west[q]
        return carry

    lax.fori_loop(0, ROWS // 8, pack, 0)

    def inner(i, carry):
        r0 = 8 * i
        rows = pl.ds(pl.multiple_of(r0, 8), 8)

        def store(ref):
            def put(k, val):
                ref[k, rows, :] = val

            return put

        got = own_tile(
            lambda p, d: x_ref[p, pl.ds(r0 + d, 8), :], rotation_scale * x_ref[FLAT + 3, rows, :],
            store(us), store(vs), store(tn), store(sn),
        )
        for n in range(5):
            sums[n, rows, :] = got[n]
        return carry

    lax.fori_loop(1, ROWS // 8 - 1, inner, 0)


def pack_rims(a_ref, b_ref, ec, wc, far_ref, near_ref):
    even, _ = lat_place()
    odd = lon_odd()

    def send(at, east, west):
        here = slice(at, at + east.shape[0])
        far_ref[here, :] = jnp.where(odd, west, east)
        near_ref[here, :] = jnp.where(odd, east, west)

    for q in range(SLABS):
        send(TALL * q + 8, ec[q], wc[q])

    def both(r, n):
        a = a_ref[r : r + n, :]
        b = b_ref[r : r + n, :]
        return jnp.where(even, b, a), jnp.where(even, a, b)

    for q in range(SLABS):
        (e_lo, e_hi), (w_lo, w_hi) = (both(AT_SLAB + 32 * side + 8 * q, 8) for side in (0, 1))
        send(TALL * q, e_lo, w_lo)
        send(TALL * q + 8 + ROWS, e_hi, w_hi)
    for q in range(2):
        pairs = [both(AT_NINE + 2 * side + q, 1) for side in (0, 1)]
        for n in (0, 1):
            send(SLABS * TALL + 2 * q + n, pairs[0][n], pairs[1][n])
    send(SLABS * TALL + 4, *[jnp.zeros((4, COLS), F32)] * 2)


def edges(x_ref, a_ref, b_ref, us, vs, tn, sn, sums, low, high):
    even, _ = lat_place()

    def both(r, n):
        a = a_ref[pl.ds(r, n), :]
        b = b_ref[pl.ds(r, n), :]
        return jnp.where(even, b, a), jnp.where(even, a, b)

    def place(p, carry):
        low[p, 16:32, :] = x_ref[p, 0:16, :]
        high[p, 0:16, :] = x_ref[p, ROWS - 16 : ROWS, :]
        return carry

    lax.fori_loop(0, FLAT, place, 0)

    def clear(p, carry):
        low[p, 8:16, :] = jnp.zeros((8, COLS), F32)
        high[p, 16:24, :] = jnp.zeros((8, COLS), F32)
        return carry

    lax.fori_loop(0, 40, clear, 0)

    def pair(n, p):
        for k in range(LEVELS):
            lo, hi = both(AT_PAIR + 20 * n + 2 * k, 2)
            low[p + k, 14:16, :] = lo
            high[p + k, 16:18, :] = hi

    def tile(n, ref, r0, spin, puts):
        got = own_tile(lambda p, d: ref[p, r0 + d : r0 + d + 8, :], rotation_scale * spin, *puts)
        for m in range(5):
            sums[m, 8 * n : 8 * n + 8, :] = got[m]

    pair(2, WET)
    none = jnp.zeros((8, COLS), F32)
    for n, ref, r0 in ((2, low, 8), (3, high, 16)):
        tile(n, ref, r0, none, [None] * 4)
    for m in (2, 3, 4):
        lo, hi = both(AT_SUM + 7 * (m - 2), 7)
        if m < 4:
            lo = lo + sums[m, 17:24, :]
            hi = hi + sums[m, 24:31, :]
        sums[m, 17:24, :] = lo
        sums[m, 24:31, :] = hi
    for p in range(20):
        lo, hi = both(2 * p, 2)
        low[p, 14:16, :] = lo
        high[p, 16:18, :] = hi
    for k in range(LEVELS):
        lo, hi = both(AT_ONE + k, 1)
        low[D + k, 15:16, :] = lo
        high[D + k, 16:17, :] = hi
    pair(0, T)
    pair(1, S)
    for n, ref, r0, row in ((0, low, 16, 0), (1, high, 8, ROWS - 8)):
        def store(out):
            def put(k, val):
                out[k, 8 * n : 8 * n + 8, :] = val

            return put

        tile(n, ref, r0, x_ref[FLAT + 3, row : row + 8, :], [store(out) for out in (us, vs, tn, sn)])


class Wide:
    def __init__(self, own, rim):
        self.own, self.rim = own, rim

    def with_other(self, other, op):
        if isinstance(other, Wide):
            return Wide(op(self.own, other.own), op(self.rim, other.rim))
        return Wide(op(self.own, other), op(self.rim, other))

    def __add__(self, other):
        return self.with_other(other, lambda a, b: a + b)

    def __sub__(self, other):
        return self.with_other(other, lambda a, b: a - b)

    def __mul__(self, other):
        return self.with_other(other, lambda a, b: a * b)

    __rmul__ = __mul__

    def __truediv__(self, other):
        return self.with_other(other, lambda a, b: a / b)


def slope(x):
    lane = lanes()
    east_own, east_rim = turn(x.own, -1), turn(x.rim, -1)
    west_own, west_rim = turn(x.own, 1), turn(x.rim, 1)
    last, first = lane == COLS - 1, lane == 0
    return Wide(
        jnp.where(last, east_rim, east_own) - jnp.where(first, west_rim, west_own),
        jnp.where(last, east_own, east_rim) - jnp.where(first, west_own, west_rim),
    )


def step(x_ref, a_ref, b_ref, far_mine, near_mine, far_got, near_got, us, vs, tn, sn, sums, us2, vs2, tn2, sn2, sums2, mats,
         u_out, v_out, t_out, s_out, eta_out, ub_out, vb_out,
         es, ws, own, rim, fix, total, col, fu, fv, mu, mv, tu, tv, spins, t_new, s_new, u_new, v_new, flats, sem):
    even, _ = lat_place()
    lane = lanes()
    rest = lane % STRIDE
    inside = lane < LEVELS * STRIDE
    odd = lon_odd()
    for q, r, count in [(q, r, 8) for r in range(8, 88, 8) for q in range(SLABS)] + [(0, 0, 2), (1, 0, 2)]:
        at = TALL * q + r - 8 if r else SLABS * TALL + 2 * q
        got = slice(at, at + count)
        far_in, near_in = far_got[got, :], near_got[got, :]
        far_out, near_out = far_mine[got, :], near_mine[got, :]
        e_got, w_got = jnp.where(odd, far_in, near_in), jnp.where(odd, near_in, far_in)
        e_mine, w_mine = jnp.where(odd, near_out, far_out), jnp.where(odd, far_out, near_out)
        own_e, own_w = (m[0:count] for m in ((rest < 2) & inside, ((rest == 2) | (rest == 3)) & inside))
        for ref, val in ((es, jnp.where(own_e, w_mine, e_got)), (ws, jnp.where(own_w, e_mine, w_got))):
            if r:
                ref[q, r : r + 8, :] = val
            else:
                ref[q, 7:8, :] = val[0:1]
                ref[q, TOP + ROWS + 8 : TOP + ROWS + 9, :] = val[1:2]
        if q < 2 and r:
            es[SLABS + q, r : r + 8, :] = turn(e_got, 2)
            ws[SLABS + q, r : r + 8, :] = turn(w_got, -2)
    for n in range(4):
        at, count = FLAT_ROWS[n]
        a = a_ref[AT_FLAT + at : AT_FLAT + at + count, :]
        b = b_ref[AT_FLAT + at : AT_FLAT + at + count, :]
        own[n, TOP - count : TOP, :] = jnp.where(even, b, a)
        own[n, TOP : TOP + ROWS, :] = x_ref[FLAT + n]
        own[n, TOP + ROWS : TOP + ROWS + count, :] = jnp.where(even, a, b)
        q, second = divmod(n, 2)
        for r in range(8, 88, 8):
            at = (121, 7) if second else (112, 16)
            rim[n, r : r + 8, :] = turn(jnp.where(lane >= at[0], es[q, r : r + 8, :], ws[q, r : r + 8, :]), at[1])
    for m in range(5):
        total[m, 8:16, :] = sums2[m, 16:24, :]
        total[m, 16:24, :] = sums2[m, 0:8, :]
        total[m, 24:72, :] = sums[m, 8:56, :]
        total[m, 72:80, :] = sums2[m, 8:16, :]
        total[m, 80:88, :] = sums2[m, 24:32, :]

    short = lane
    lane = lanes(BAND)
    rest = lane % STRIDE
    inside = lane < LEVELS * STRIDE
    level_e = jnp.minimum(lane // STRIDE, LEVELS)
    level_w = jnp.minimum(((lane + 7) % COLS) // STRIDE, LEVELS)
    thick_e = jnp.where(level_e < LEVELS, (level_e + 1).astype(F32) * THICK[0], 0.0)
    thick_w = jnp.where(level_w < LEVELS, (level_w + 1).astype(F32) * THICK[0], 0.0)
    edge = (lane < 2) | (lane >= COLS - 2)
    border = (short < 2) | (short >= COLS - 2)

    def slab_tile(i, carry):
        r0 = BAND * i + 8
        here = pl.ds(pl.multiple_of(r0, 8), BAND)
        parts = []
        for ref, side, thick, ahead in ((es, 0, thick_e, 1), (ws, 1, thick_w, -1)):
            def at(q, d):
                return ref[q, pl.ds(r0 + d, BAND), :]

            def around(x, d):
                return turn(x, -d)

            if ahead > 0:
                near, pair = (rest == 2) & inside, ((rest == 2) | (rest == 3)) & inside
            else:
                near, pair = (rest == 1) & inside, (rest < 2) & inside
            wet = at(3, 0)
            u = at(0, 0)
            v = at(1, 0)
            weight = thick * at(2, 0)
            weight_ns = thick * (at(2, 1) - at(2, -1))
            pressure = dot(weight, mats[2 * side])
            pressure_slope = dot(weight, mats[2 * side + 1])
            pressure_ns = dot(weight_ns, mats[2 * side])
            smooth_u, un, us_ = smoothed(at, 0, u, around)
            smooth_v, vn, vs_ = smoothed(at, 1, v, around)
            change = pressure_scale * 0.5 * pressure_slope + viscous_scale * smooth_u
            change_ns = pressure_scale * 0.5 * pressure_ns + viscous_scale * smooth_v
            parts.append((wet * thick, -change, -change_ns, u, v, wet))

            def beyond(c, ns, extra):
                far = viscous_scale * jnp.where(pair, c, 0.0)
                close = jnp.where(near, (2.0 * viscous_scale) * (ns - 4.0 * c) + extra, 0.0)
                return -(turn(far, -2 * ahead) + turn(close, -ahead))

            push = (0.5 * pressure_scale * ahead) * pressure
            fixes = [beyond(u, un + us_, push), beyond(v, vn + vs_, 0.0)]
            carry_u = (0.5 * advect_scale * ahead) * u
            for q in (SLABS, SLABS + 1):
                c = at(q, 0)
                fixes.append(beyond(c, at(q, 1) + at(q, -1), carry_u * c))
            parts.append(fixes)
        (we, due, dve, ue, ve, wet_e), fix_e, (ww, duw, dvw, uw, vw, wet_w), fix_w = parts
        own_wet = jnp.where(rest < 2, wet_e, wet_w)
        own_thick = jnp.where(rest < 2, thick_e, thick_w)
        fixes = [own_wet * (x + y) for x, y in zip(fix_e, fix_w)]
        for n in range(4):
            fix[n, here, :] = fixes[n]

        east = jnp.concatenate([we, we * due, we * dve, we * ue, we * ve], axis=0)
        west = jnp.concatenate([ww, ww * duw, ww * dvw, ww * uw, ww * vw], axis=0)
        rims = dot(east, mats[4]) + dot(west, mats[5])
        rim_depth, rim_du, rim_dv, rim_u, rim_v = (rims[BAND * n : BAND * n + BAND] for n in range(5))
        owns = dot(jnp.concatenate([own_thick * fixes[0], own_thick * fixes[1]], axis=0), mats[6])
        spin = Wide(rotation_scale * own[3, here, :], rotation_scale * rim[3, here, :])
        column = Wide(surface_depth + total[4, here, :], surface_depth + rim_depth)
        diff_u = rim_du + spin.rim * rim_v
        diff_v = rim_dv - spin.rim * rim_u
        fix_u, fix_v = owns[0:BAND], owns[BAND : 2 * BAND]
        part = Wide(1.0 / column.own, 1.0 / column.rim)
        for ref, mean, own_sum, own_diff, rim_diff, x in (
            (fu, mu, total[0, here, :], total[2, here, :], diff_u, fix_u),
            (fv, mv, total[1, here, :], total[3, here, :], diff_v, fix_v),
        ):
            ref[0, here, :] = (own_diff + x) * part.own * (1.0 / SUBSTEPS)
            ref[1, here, :] = rim_diff * part.rim * (1.0 / SUBSTEPS)
            mean[here, :] = (own_sum + x) * part.own
        for ref, x in ((col, column), (spins, spin)):
            ref[0, here, :] = x.own
            ref[1, here, :] = x.rim
        return carry

    lax.fori_loop(0, 80 // BAND, slab_tile, 0)

    def mend(n, k, rows_fix):
        return jnp.where(border, turn(fix[n, rows_fix, :], -(STRIDE * k + 2)), 0.0)

    def tile_of(i):
        return pl.ds(pl.multiple_of(8 * i, 8), 8), pl.ds(pl.multiple_of(8 * i + TOP, 8), 8)

    def tracer_tile(rows, fixed, refs, src):
        for n, (ref, out) in enumerate(zip(refs, (t_new, s_new))):
            for k in range(LEVELS):
                out[k, rows, :] = ref[k, src, :] + mend(2 + n, k, fixed)

    def tracer_loop(i, carry):
        rows, fixed = tile_of(i)
        tracer_tile(rows, fixed, (tn, sn), rows)
        return carry

    lax.fori_loop(1, ROWS // 8 - 1, tracer_loop, 0)
    for n, i in enumerate((0, ROWS // 8 - 1)):
        tracer_tile(slice(8 * i, 8 * i + 8), slice(8 * i + TOP, 8 * i + TOP + 8), (tn2, sn2), slice(8 * n, 8 * n + 8))
    first = [pltpu.make_async_copy(src, dst, sem.at[n]) for n, (src, dst) in enumerate(((t_new, t_out), (s_new, s_out)))]
    for copy in first:
        copy.start()

    def wide(ref, at):
        return Wide(ref[0, at, :], ref[1, at, :])

    def keep(ref, at, x):
        ref[0, at, :] = x.own
        ref[1, at, :] = x.rim

    def flat(p, r):
        return Wide(own[p, r : r + 8, :], rim[p, r : r + 8, :])

    def wet_of(column):
        return Wide(jnp.where(column.own > surface_depth, 1.0, 0.0), jnp.where(column.rim > surface_depth, 1.0, 0.0))

    def substep(n, carry):
        for r in range(8, 88, 8):
            here = slice(r, r + 8)
            column = wide(col, here)
            wet = wet_of(column)
            u = flat(1, r)
            v = flat(2, r)
            spin = wide(spins, here)
            un = wet * (u - (0.5 * gravity_scale) * slope(flat(0, r)) + spin * v + wide(fu, here))
            vn = wet * (v - (0.5 * gravity_scale) * (flat(0, r + 1) - flat(0, r - 1)) - spin * u + wide(fv, here))
            for p, x in ((1, un), (2, vn)):
                own[p, here, :] = x.own
                rim[p, here, :] = x.rim
            keep(tu, here, column * un)
            keep(tv, here, column * vn)
        for r in range(8, 88, 8):
            here = slice(r, r + 8)
            wet = wet_of(wide(col, here))
            flow = slope(wide(tu, here)) + (wide(tv, slice(r + 1, r + 9)) - wide(tv, slice(r - 1, r + 7)))
            eta = wet * (flat(0, r) - (0.5 * divergence_scale) * flow)
            own[0, here, :] = eta.own
            rim[0, here, :] = eta.rim
        return carry

    lax.fori_loop(0, SUBSTEPS, substep, 0)
    second = []
    for n, dst in enumerate((eta_out, ub_out, vb_out)):
        flats[n] = own[n, TOP : TOP + ROWS, :]
        second.append(pltpu.make_async_copy(flats.at[n], dst, sem.at[2 + n]))
        second[-1].start()

    last = []
    for n, (base, edge_base, mean, out, dst) in enumerate(((us, us2, mu, u_new, u_out), (vs, vs2, mv, v_new, v_out))):
        def flow_tile(rows, fixed, ref, src):
            gain = own[1 + n, fixed, :] - mean[fixed, :]
            for k in range(LEVELS):
                out[k, rows, :] = ref[k, src, :] + mend(n, k, fixed) + x_ref[WET + k, rows, :] * gain

        def flow_loop(i, carry):
            rows, fixed = tile_of(i)
            flow_tile(rows, fixed, base, rows)
            return carry

        lax.fori_loop(1, ROWS // 8 - 1, flow_loop, 0)
        for m, i in enumerate((0, ROWS // 8 - 1)):
            flow_tile(slice(8 * i, 8 * i + 8), slice(8 * i + TOP, 8 * i + TOP + 8), edge_base, slice(8 * m, 8 * m + 8))
        last.append(pltpu.make_async_copy(out, dst, sem.at[5 + n]))
        last[-1].start()
    for copy in first + second + last:
        copy.wait()


def colour(parity, lats, lons):
    pairs = []
    for lat in range(lats):
        for lon in range(lons):
            if (lat + parity) % 2 == 0:
                to = (lon, lat + 1) if lat + 1 < lats else (lons - 1 - lon, lat)
            elif lat > 0:
                to = (lon, lat - 1)
            else:
                continue
            pairs.append((lon * lats + lat, to[0] * lats + to[1]))
    return pairs


def partners(first, lons):
    pairs = []
    for west in range(first, lons + first, 2):
        east = (west + 1) % lons
        pairs += [(west % lons, east), (east, west % lons)]
    return pairs


def local(u, v, t, s, w, bottom, eta, ub, vb, cor):
    lats = lax.axis_size("lat")
    lons = lax.axis_size("lon")
    raw = tuple(pltpu.with_memory_space_constraint(z, pltpu.HBM) for z in (u, v, t, s, w, bottom, eta, ub, vb, cor))
    vmem = pltpu.VMEM
    dma = pltpu.SemaphoreType.DMA
    two = (2, LEVELS, 16, COLS)
    a, b = call(
        pack_rows, [(ROW_SLAB, COLS)] * 2,
        [vmem(two, F32)] * 4 + [vmem(two, jnp.int32), vmem((4, ROWS, COLS), F32), vmem(PLANE, jnp.int32)]
        + [vmem((40, 24, COLS), F32)] * 2 + [vmem((ROW_SLAB, COLS), F32)] * 3 + [dma((15,))],
        1_000_000, *raw, ins=[HBM] * 10,
    )
    b = lax.ppermute(b, ("lon", "lat"), colour(1, lats, lons))
    a = lax.ppermute(a, ("lon", "lat"), colour(0, lats, lons))
    x, ec, wc, us, vs, tn, sn, sums, mats = call(
        centre, [(PLANES, ROWS, COLS)] + [(SLABS, ROWS, COLS)] * 2 + [CUBE] * 4 + [(5, ROWS, COLS), (7, COLS, COLS)],
        [vmem(CUBE, F32)] * 4 + [vmem(CUBE, jnp.int32), vmem(PLANE, jnp.int32), dma((10,))],
        20_000_000, *raw, ins=[HBM] * 10,
    )
    far, near = call(pack_rims, [(COLUMN_SLAB, COLS)] * 2, [], 1_000_000, a, b, ec, wc)
    far_got = lax.ppermute(far, "lon", partners(1, lons))
    near_got = lax.ppermute(near, "lon", partners(0, lons))
    window = vmem((FLAT, 32, COLS), F32)
    us2, vs2, tn2, sn2, sums2 = call(
        edges, [(LEVELS, 16, COLS)] * 4 + [(5, 32, COLS)], [window] * 2, 10_000_000, x, a, b,
    )
    wide = vmem((2, HIGH, COLS), F32)
    thin = vmem((HIGH, COLS), F32)
    slab = vmem((SLABS + 2, HIGH, COLS), F32)
    four = vmem((4, HIGH, COLS), F32)
    return tuple(
        call(
            step, [CUBE] * 4 + [PLANE] * 3,
            [slab] * 2 + [four] * 3 + [vmem((5, HIGH, COLS), F32)] + [wide] * 3 + [thin] * 2 + [wide] * 3
            + [vmem(CUBE, F32)] * 4 + [vmem((3, ROWS, COLS), F32), dma((7,))],
            50_000_000, x, a, b, far, near, far_got, near_got, us, vs, tn, sn, sums, us2, vs2, tn2, sn2, sums2, mats,
            outs=[HBM] * 7,
        )
    )


def solution(mesh):
    deep = P(None, "lat", "lon")
    flat = P("lat", "lon")
    return jax.shard_map(
        local,
        mesh=mesh,
        in_specs=(deep,) * 5 + (flat,) * 5,
        out_specs=(deep,) * 4 + (flat,) * 3,
        check_vma=False,
    )
```
